256 devices in a mesh: row: 32 (over z, y), col: 8 (over x, core).
Axes of the slice: x: 4, y: 4, z: 8, core: 2. Of those that a mesh axis runs over, the one named last changes fastest.
Arguments:
- object_field: float32 [2, 3, 8192, 2048], P(None, None, 'row', 'col'), may hold values from -1 to 1
- probe: float32 [2, 128, 128], replicated, may hold values from -4 to 4
- propagator: float32 [128, 128], replicated, may hold values from -3.140625 to 3.140625
- measured: float32 [32, 8, 6, 128, 128], P('row', 'col'), may hold values from 0 to 1
- offsets: int32 [32, 8, 6, 2], P('row', 'col'), may hold values from 0 to 255
Outputs:
- updated: float32 [2, 3, 8192, 2048], P(None, None, 'row', 'col')
The draws below stay inside these ranges and needn't reach their ends.
Inputs may be any that keep to these rules, and one draw needn't show every extreme that they name: `offsets`: entry 0 is the row offset and entry 1 the column offset of a window inside its tile.
All inputs are finite; a program needn't handle non-finite values.
Results may differ from the reference program's by a relative error of at most 0.0003.
Values sent between devices are 32-bit elements; how exact they have to be, the bound alone decides.
No kernel may reach another device: no remote copies, remote signals or barrier semaphores. Data moves between devices by JAX's collectives and lax.ppermute only.
A program may use at most 64 MiB of HBM per device.

```python
import jax
import jax.numpy as jnp
from jax import lax

PROBE = 128
SLICES = 3
POS = 6
ITERS = 2
TILE = 256
ROWS_ALL = 8192
COLS_ALL = 2048
N_ROW = 32
N_COL = 8


def with_ends(drawn, own_key, least, largest):
    extent = drawn.shape
    index_at = [jax.random.randint(jax.random.fold_in(own_key, axis), (), 0, extent[axis]) for axis in range(len(extent))]
    drawn = drawn.at[tuple(index_at)].set(least)
    longest = extent.index(max(extent))
    index_at[longest] = (index_at[longest] + 1) % extent[longest]
    return drawn.at[tuple(index_at)].set(largest)


def levels(stream_key, dims, shards, least, high):
    gain, own = 1.0, jax.random.fold_in(stream_key, 6)
    for position, parts in shards:
        draws = jnp.exp(jax.random.uniform(jax.random.fold_in(own, position), (parts,), jnp.float32, least / len(shards), high / len(shards)))
        gain = gain * jnp.repeat(draws, dims[position] // parts).reshape([-1 if axis == position else 1 for axis in range(len(dims))])
    return gain


def noise(key, extent, deviation, limit, held_as=jnp.bfloat16):
    array = deviation * jax.random.normal(key, extent, jnp.float32)
    return jnp.clip(array, min=-limit, max=limit).astype(held_as)


def setup_inputs(seed: int = 0) -> dict:
    key_of = jax.random.split(jax.random.key(seed), 6)
    object_field = jnp.clip(jax.random.uniform(key_of[0], (2, SLICES, ROWS_ALL, COLS_ALL), jnp.float32, -1.0, 1.0) * levels(key_of[0], (2, SLICES, ROWS_ALL, COLS_ALL), ((2, 32), (3, 8)), -0.4, 0.0), -1.0, 1.0)
    probe = noise(key_of[1], (2, PROBE, PROBE), 1.0, 4.0, jnp.float32)
    propagator = jnp.clip(jax.random.uniform(key_of[2], (PROBE, PROBE), jnp.float32, -3.140625, 3.140625), -3.140625, 3.140625)
    measured = jnp.clip(1.0 * jax.random.uniform(key_of[3], (N_ROW, N_COL, POS, PROBE, PROBE), jnp.float32) ** levels(key_of[3], (N_ROW, N_COL, POS, PROBE, PROBE), ((0, 32), (1, 8)), -0.2, 0.2), 0.0, 1.0)
    offsets = with_ends(jax.random.randint(key_of[4], (N_ROW, N_COL, POS, 2), 0, TILE), jax.random.fold_in(key_of[4], 1), 0, TILE - 1).astype(jnp.int32)
    return {"object_field": object_field, "probe": probe, "propagator": propagator, "measured": measured, "offsets": offsets}


step_size = 0.05

def total_loss(field, probe, propagator, measured, offsets):
    wrapped = jnp.concatenate([field, field[:, :, :PROBE, :]], axis=2)
    wrapped = jnp.concatenate([wrapped, wrapped[:, :, :, :PROBE]], axis=3)
    row_base = (jnp.arange(N_ROW, dtype=jnp.int32) * TILE)[:, None, None] + offsets[:, :, :, 0].astype(jnp.int32)
    col_base = (jnp.arange(N_COL, dtype=jnp.int32) * TILE)[None, :, None] + offsets[:, :, :, 1].astype(jnp.int32)
    initial = probe[0] + 1j * probe[1]
    transfer = jnp.exp(1j * propagator)

    def one_position(start_row, start_col, target):
        anchor = jnp.zeros((), jnp.int32)
        patch = lax.dynamic_slice(wrapped, (anchor, anchor, start_row, start_col), (2, SLICES, PROBE, PROBE))
        wave = initial
        for layer in range(SLICES):
            wave = wave * (patch[0, layer] + 1j * patch[1, layer])
            if layer + 1 < SLICES:
                wave = jnp.fft.ifft2(jnp.fft.fft2(wave, norm='ortho') * transfer, norm='ortho')
        far = jnp.fft.fft2(wave, norm='ortho')
        power = jnp.real(far) ** 2 + jnp.imag(far) ** 2
        return jnp.sum((power - target) ** 2)

    def one_row(inputs):
        rows_here, cols_here, targets = inputs
        values = jax.vmap(one_position)(rows_here.reshape(-1), cols_here.reshape(-1), targets.reshape(-1, PROBE, PROBE))
        return jnp.sum(values)
    return jnp.sum(lax.map(one_row, (row_base, col_base, measured)))

def reference(object_field, probe, propagator, measured, offsets):
    field = object_field
    for step in range(ITERS):
        field = field - step_size * jax.grad(total_loss)(field, probe, propagator, measured, offsets)
    return field
```

```python
import functools
import math

import jax
import jax.numpy as jnp
import numpy as np
from jax import lax
from jax.experimental import pallas as pl
from jax.experimental.pallas import tpu as pltpu
from jax.sharding import PartitionSpec as P

PROBE = 128
SLICES = 3
POS = 6
TILE = 256
EXT = TILE + PROBE
SUB = 8
STEP = 0.05
F32 = jnp.float32
BF16 = jnp.bfloat16


def dft_tables():
    index = np.arange(PROBE)
    angle = (index[:, None] * index[None, :] % PROBE) * (-2.0 * math.pi / PROBE)
    cosines, sines = np.cos(angle) / math.sqrt(PROBE), np.sin(angle) / math.sqrt(PROBE)
    right = np.block([[cosines, sines], [-sines, cosines]]).astype(np.float32)
    left = np.block([[cosines, -sines], [sines, cosines]]).astype(np.float32)
    parts = []
    for matrix in (right, left):
        high = matrix.astype(BF16)
        parts += [high, (matrix - high.astype(np.float32)).astype(BF16)]
    return np.stack(parts)


def split(value):
    high = value.astype(BF16)
    return high, (value - high.astype(F32)).astype(BF16)


def dot(a, b):
    return jnp.dot(a, b, preferred_element_type=F32)


def times_right(block, table):
    high, low = split(block)
    wide, fine = table
    return dot(high, wide) + dot(low, wide) + dot(high, fine)


def times_left(block, table):
    high, low = split(block)
    wide, fine = table
    return dot(wide, high) + dot(wide, low) + dot(fine, high)


def side_to_stack(block):
    h = PROBE
    top = jnp.concatenate([block[:h, :h], block[h:, :h]], axis=1)
    low = jnp.concatenate([block[:h, h:], block[h:, h:]], axis=1)
    return jnp.concatenate([top, low], axis=0)


def times_phase(block, phase_real, phase_imag):
    h = PROBE
    re, im = block[:h], block[h:]
    pr = jnp.concatenate([phase_real, phase_real], axis=1)
    pi = jnp.concatenate([phase_imag, phase_imag], axis=1)
    return jnp.concatenate([re * pr - im * pi, re * pi + im * pr], axis=0)


def tables_of(table_ref):
    right = (table_ref[0], table_ref[1])
    left = (table_ref[2], table_ref[3])
    return right, left


def propagate(block, right, left, phase_real, phase_imag):
    block = side_to_stack(times_right(block, right))
    block = times_left(block, left)
    block = times_phase(block, phase_real, phase_imag)
    block = times_left(block, right)
    return times_right(side_to_stack(block), left)


def pair_of(ref, p):
    top = jnp.concatenate([ref[0, p], ref[1, p]], axis=1)
    low = jnp.concatenate([ref[0, p + 1], ref[1, p + 1]], axis=1)
    return jnp.concatenate([top, low], axis=0)


def put_pair(ref, p, block):
    h = PROBE
    ref[0, p] = block[:h, :h]
    ref[1, p] = block[:h, h:]
    ref[0, p + 1] = block[h:, :h]
    ref[1, p + 1] = block[h:, h:]


def place(offset_ref, p):
    row, col = offset_ref[p, 0], offset_ref[p, 1]
    over = lax.rem(row, SUB)
    base = jnp.where(col >= PROBE, PROBE, 0)
    return pl.multiple_of(row - over, SUB), over, pl.multiple_of(base, PROBE), col - base


def take_window(ext, offset_ref, p, part):
    row, over, base, shift = place(offset_ref, p)
    tall, wide = PROBE + SUB, 2 * PROBE
    block = ext[part, pl.ds(row, tall), pl.ds(base, wide)]
    block = pltpu.roll(block, jnp.where(over == 0, 0, tall - over), 0)[:PROBE]
    return pltpu.roll(block, jnp.where(shift == 0, 0, wide - shift), 1)[:, :PROBE]


def add_window(grad, offset_ref, p, part, value):
    row, over, base, shift = place(offset_ref, p)
    tall, wide = PROBE + SUB, 2 * PROBE
    block = jnp.concatenate([value, jnp.zeros_like(value)], axis=1)
    block = pltpu.roll(block, shift, 1)
    block = jnp.concatenate([block, jnp.zeros((SUB, wide), F32)], axis=0)
    where = (part, pl.ds(row, tall), pl.ds(base, wide))
    grad[where] = grad[where] + pltpu.roll(block, over, 0)


def times(ar, ai, br, bi):
    return ar * br - ai * bi, ar * bi + ai * br


def times_conj(ar, ai, br, bi):
    return ar * br + ai * bi, ar * bi - ai * br


def fill_first(ext, refs):
    tile, low_left, low_right, right, corner = refs
    t, h = TILE, PROBE
    ext[:, :t, :t] = tile[:, 0]
    ext[:, t:, :h] = low_left[...]
    ext[:, t:, h:t] = low_right[...]
    ext[:, :t, t:] = right[...]
    ext[:, t:, t:] = corner[...]


def fill_next(ext, refs):
    left, middle, right = refs
    t, h = TILE, PROBE
    ext[:, :, :h] = left[...]
    ext[:, :, h:t] = middle[...]
    ext[:, :, t:] = right[...]


def forward_kernel(fill, n_field, first, *refs):
    offset_ref, table_ref, phase_ref, wave = refs[:4]
    field = refs[4 : 4 + n_field]
    windows, out, ext = refs[4 + n_field :]
    fill(ext, field)
    right, left = tables_of(table_ref)
    for p in range(0, POS, 2):
        rows = []
        for q in (p, p + 1):
            tr = take_window(ext, offset_ref, q, 0)
            ti = take_window(ext, offset_ref, q, 1)
            windows[0, q] = tr
            windows[1, q] = ti
            if first:
                wr, wi = wave[0], wave[1]
            else:
                wr, wi = wave[0, q], wave[1, q]
            rows.append(jnp.concatenate(times(wr, wi, tr, ti), axis=1))
        block = jnp.concatenate(rows, axis=0)
        put_pair(out, p, propagate(block, right, left, phase_ref[0], phase_ref[1]))


def write_gradient(grad, outs):
    left, top, middle, low, right = outs
    t, h = TILE, PROBE
    left[...] = grad[:, :, :h]
    top[...] = grad[:, :h, h:t]
    middle[...] = grad[:, h:t, h:t]
    low[...] = grad[:, t:, h:t]
    right[...] = grad[:, :, t:]


def turn_kernel(fill, n_field, *refs):
    offset_ref, table_ref, intensity, wave = refs[:4]
    field = refs[4 : 4 + n_field]
    outs = refs[4 + n_field : 9 + n_field]
    back, ext, grad = refs[9 + n_field :]
    fill(ext, field)
    grad[...] = jnp.zeros_like(grad)
    right, left = tables_of(table_ref)
    h = PROBE
    for p in range(0, POS, 2):
        rows, windows = [], []
        for q in (p, p + 1):
            tr = take_window(ext, offset_ref, q, 0)
            ti = take_window(ext, offset_ref, q, 1)
            windows.append((tr, ti))
            rows.append(jnp.concatenate(times(wave[0, q], wave[1, q], tr, ti), axis=1))
        block = jnp.concatenate(rows, axis=0)
        block = times_left(side_to_stack(times_right(block, right)), left)
        re, im = block[:h], block[h:]
        target = jnp.concatenate([intensity[p], intensity[p + 1]], axis=1)
        weight = 4.0 * (re * re + im * im - target)
        block = jnp.concatenate([re * weight, im * weight], axis=0)
        block = times_right(side_to_stack(times_left(block, right)), left)
        for i, q in enumerate((p, p + 1)):
            gr, gi = block[i * h : (i + 1) * h, :h], block[i * h : (i + 1) * h, h:]
            br, bi = times_conj(*windows[i], gr, gi)
            back[0, q] = br
            back[1, q] = bi
            dr, di = times_conj(wave[0, q], wave[1, q], gr, gi)
            add_window(grad, offset_ref, q, 0, dr)
            add_window(grad, offset_ref, q, 1, di)
    write_gradient(grad, outs)


def backward_kernel(first, *refs):
    if first:
        offset_ref, table_ref, phase_ref, back_in, wave = refs[:5]
        outs, grad = refs[5:10], refs[10]
    else:
        offset_ref, table_ref, phase_ref, back_in, wave, windows = refs[:6]
        outs, back, grad = refs[6:11], refs[11], refs[12]
    grad[...] = jnp.zeros_like(grad)
    right, left = tables_of(table_ref)
    h = PROBE
    for p in range(0, POS, 2):
        block = propagate(pair_of(back_in, p), right, left, phase_ref[0], -phase_ref[1])
        for i, q in enumerate((p, p + 1)):
            gr, gi = block[i * h : (i + 1) * h, :h], block[i * h : (i + 1) * h, h:]
            if first:
                dr, di = times_conj(wave[0], wave[1], gr, gi)
            else:
                br, bi = times_conj(windows[0, q], windows[1, q], gr, gi)
                back[0, q] = br
                back[1, q] = bi
                dr, di = times_conj(wave[0, q], wave[1, q], gr, gi)
            add_window(grad, offset_ref, q, 0, dr)
            add_window(grad, offset_ref, q, 1, di)
    write_gradient(grad, outs)


def whole(array):
    rank = len(array.shape)
    return pl.BlockSpec(array.shape, lambda i: (0,) * rank)


def tile_of(layer):
    return pl.BlockSpec((2, 1, TILE, TILE), lambda i: (0, layer, 0, 0))


def shape(*dims):
    return jax.ShapeDtypeStruct(dims, F32)


STACK = (2, POS, PROBE, PROBE)
GRADIENT = [
    shape(2, EXT, PROBE),
    shape(2, PROBE, PROBE),
    shape(2, PROBE, PROBE),
    shape(2, PROBE, PROBE),
    shape(2, EXT, PROBE),
]
SCRATCH = pltpu.VMEM((2, EXT, EXT), F32)


def run(body, operands, outs, scratch, name, stages, specs=None):
    specs = specs or {}
    flops = stages * POS * PROBE * 256 * 256 * 2 * 3
    moved = sum(math.prod(o.shape) * 4 for o in operands) + sum(math.prod(o.shape) * 4 for o in outs)
    in_specs = [pl.BlockSpec(memory_space=pltpu.SMEM)]
    in_specs += [specs.get(n, None) or whole(o) for n, o in enumerate(operands) if n > 0]
    return pl.pallas_call(
        body,
        grid=(1,),
        in_specs=in_specs,
        out_specs=[whole(o) for o in outs],
        out_shape=outs,
        scratch_shapes=scratch,
        name=name,
        cost_estimate=pl.CostEstimate(flops=flops, bytes_accessed=moved, transcendentals=0),
        compiler_params=pltpu.CompilerParams(vmem_limit_bytes=40 * 2**20),
    )(*operands)


def forward(offsets, tables, phase, wave, field, layer, fill, first):
    operands = [offsets, tables, phase, wave, *field]
    specs = {4: tile_of(layer)} if fill is fill_first else {}
    body = functools.partial(forward_kernel, fill, len(field), first)
    return run(body, operands, [shape(*STACK)] * 2, [SCRATCH], "forward", 4, specs)


def turn(offsets, tables, intensity, wave, field, layer, fill):
    operands = [offsets, tables, intensity, wave, *field]
    specs = {4: tile_of(layer)} if fill is fill_first else {}
    body = functools.partial(turn_kernel, fill, len(field))
    return run(body, operands, [*GRADIENT, shape(*STACK)], [SCRATCH] * 2, "turn", 4, specs)


def backward(offsets, tables, phase, back, wave, windows):
    first = windows is None
    operands = [offsets, tables, phase, back, wave] + ([] if first else [windows])
    outs = [*GRADIENT] if first else [*GRADIENT, shape(*STACK)]
    return run(functools.partial(backward_kernel, first), operands, outs, [SCRATCH], "backward", 4)


def shifted(block, axis, distance):
    size = lax.axis_size(axis)
    return lax.ppermute(block, axis, [((i - distance) % size, i) for i in range(size)])


def gradients(offsets, tables, phase, probe, intensity, fields, fill, launch):
    win0, wave1 = forward(offsets, tables, phase, probe, fields[0], 0, fill, True)
    win1, wave2 = forward(offsets, tables, phase, wave1, fields[1], 1, fill, False)
    *grad2, back2 = turn(offsets, tables, intensity, wave2, fields[2], 2, fill)
    *grad1, back1 = backward(offsets, tables, phase, back2, wave1, win1)
    grad0 = backward(offsets, tables, phase, back1, probe, None)
    return [grad0, grad1, grad2]


def middle_step(grad, old):
    h, t = PROBE, TILE
    left, top, middle, low, right = grad
    from_left = shifted(right, "col", 1)
    above_r = shifted(low, "row", 1)
    below_r = shifted(top, "row", -1)
    left = left + from_left
    above_l = shifted(left[:, t:], "row", 1)
    below_l = shifted(left[:, :h], "row", -1)
    old_l, old_m = old
    new_l = jnp.concatenate(
        [
            old_l[:, :h] - STEP * (left[:, :h] + above_l),
            old_l[:, h:t] - STEP * left[:, h:t],
            old_l[:, t:] - STEP * (left[:, t:] + below_l),
        ],
        axis=1,
    )
    from_right = shifted(new_l, "col", -1)
    new_m = jnp.concatenate(
        [
            old_m[:, :h] - STEP * (top + above_r),
            old_m[:, h:t] - STEP * middle,
            old_m[:, t:] - STEP * (low + below_r),
        ],
        axis=1,
    )
    return new_l, new_m, from_right


def last_step(grad, old):
    h, t = PROBE, TILE
    left, top, middle, low, right = grad
    from_left = shifted(right, "col", 1)
    above_r = shifted(low, "row", 1)
    left = left + from_left
    above_l = shifted(left[:, t:], "row", 1)
    old_l, old_m, _ = old
    new_l = jnp.concatenate(
        [old_l[:, :h] - STEP * (left[:, :h] + above_l), old_l[:, h:t] - STEP * left[:, h:t]], axis=1
    )
    new_m = jnp.concatenate(
        [old_m[:, :h] - STEP * (top + above_r), old_m[:, h:t] - STEP * middle], axis=1
    )
    return jnp.concatenate([new_l, new_m], axis=2)


def on_device(object_field, probe, propagator, measured, offsets):
    h, t = PROBE, TILE
    tables = jnp.asarray(dft_tables())
    offsets = offsets.reshape(POS, 2)
    intensity = measured.reshape(POS, h, h)
    phase = jnp.stack([jnp.cos(propagator), jnp.sin(propagator)])
    fields, olds = [], []
    for layer in range(SLICES):
        own = object_field[:, layer]
        low_left = shifted(own[:, :h, :h], "row", -1)
        low_right = shifted(own[:, :h, h:], "row", -1)
        right = shifted(own[:, :, :h], "col", -1)
        corner = shifted(low_left, "col", -1)
        fields.append([object_field, low_left, low_right, right, corner])
        olds.append(
            (
                jnp.concatenate([own[:, :, :h], low_left], axis=1),
                jnp.concatenate([own[:, :, h:], low_right], axis=1),
            )
        )
    grads = gradients(offsets, tables, phase, probe, intensity, fields, fill_first, None)
    fields = [None] * SLICES
    for layer in (2, 0, 1):
        fields[layer] = middle_step(grads[layer], olds[layer])
    grads = gradients(offsets, tables, phase, probe, intensity, fields, fill_next, None)
    return jnp.stack([last_step(grads[n], fields[n]) for n in range(SLICES)], axis=1)


def solution(mesh):
    placed = (
        P(None, None, "row", "col"),
        P(),
        P(),
        P("row", "col", None, None, None),
        P("row", "col", None, None),
    )
    return jax.shard_map(
        on_device,
        mesh=mesh,
        in_specs=placed,
        out_specs=P(None, None, "row", "col"),
        check_vma=False,
    )
```

```python
import functools
import math

import jax
import jax.numpy as jnp
import numpy as np
from jax import lax
from jax.experimental import pallas as pl
from jax.experimental.pallas import tpu as pltpu
from jax.sharding import PartitionSpec as P


PROBE = 128
SLICES = 3
POS = 6
TILE = 256
EXT = TILE + PROBE
SUB = 8
STEP = 0.05
F32 = jnp.float32
BF16 = jnp.bfloat16


def dft_tables():
    index = np.arange(PROBE)
    angle = (index[:, None] * index[None, :] % PROBE) * (-2.0 * math.pi / PROBE)
    cosines, sines = np.cos(angle) / math.sqrt(PROBE), np.sin(angle) / math.sqrt(PROBE)
    right = np.block([[cosines, sines], [-sines, cosines]]).astype(np.float32)
    left = np.block([[cosines, -sines], [sines, cosines]]).astype(np.float32)
    parts = []
    for matrix in (right, left):
        high = matrix.astype(BF16)
        parts += [high, (matrix - high.astype(np.float32)).astype(BF16)]
    return np.stack(parts)


def split(value):
    high = value.astype(BF16)
    return high, (value - high.astype(F32)).astype(BF16)


def dot(a, b):
    return jnp.dot(a, b, preferred_element_type=F32)


def times_right(block, table):
    high, low = block
    wide, fine = table
    return dot(jnp.concatenate([high, low, high], axis=1), jnp.concatenate([wide, wide, fine], axis=0))


def times_left(block, table):
    high, low = block
    wide, fine = table
    return dot(jnp.concatenate([wide, wide, fine], axis=1), jnp.concatenate([high, low, high], axis=0))


def side_to_stack(block):
    h = PROBE
    top = jnp.concatenate([block[:h, :h], block[h:, :h]], axis=1)
    low = jnp.concatenate([block[:h, h:], block[h:, h:]], axis=1)
    return jnp.concatenate([top, low], axis=0)


def times_phase(block, phase_real, phase_imag):
    h = PROBE
    re, im = block[:h], block[h:]
    pr = jnp.concatenate([phase_real, phase_real], axis=1)
    pi = jnp.concatenate([phase_imag, phase_imag], axis=1)
    return jnp.concatenate([re * pr - im * pi, re * pi + im * pr], axis=0)


def keep(work, n, slot, block):
    work[slot, n, 0], work[slot, n, 1] = split(block)


def kept(work, n, slot):
    return work[slot, n, 0], work[slot, n, 1]


PAIRS = POS // 2


def propagate(work, right, left, phase_real, phase_imag, finish):
    for n in range(PAIRS):
        keep(work, n, 1, side_to_stack(times_right(kept(work, n, 0), right)))
    for n in range(PAIRS):
        keep(work, n, 0, times_phase(times_left(kept(work, n, 1), left), phase_real, phase_imag))
    for n in range(PAIRS):
        keep(work, n, 1, side_to_stack(times_left(kept(work, n, 0), right)))
    for n in range(PAIRS):
        finish(n, times_right(kept(work, n, 1), left))


def tables_of(table_ref):
    right = (table_ref[0], table_ref[1])
    left = (table_ref[2], table_ref[3])
    return right, left


def pair_of(ref, p):
    top = jnp.concatenate([ref[0, p], ref[1, p]], axis=1)
    low = jnp.concatenate([ref[0, p + 1], ref[1, p + 1]], axis=1)
    return jnp.concatenate([top, low], axis=0)


def put_pair(ref, p, block):
    h = PROBE
    ref[0, p] = block[:h, :h]
    ref[1, p] = block[:h, h:]
    ref[0, p + 1] = block[h:, :h]
    ref[1, p + 1] = block[h:, h:]


def place(offset_ref, p):
    row, col = offset_ref[p, 0], offset_ref[p, 1]
    over = lax.rem(row, SUB)
    base = jnp.where(col >= PROBE, PROBE, 0)
    return pl.multiple_of(row - over, SUB), over, pl.multiple_of(base, PROBE), col - base


TALL = PROBE + SUB


def lanes(rows):
    return lax.broadcasted_iota(jnp.int32, (rows, PROBE), 1)


def take_window(ext, offset_ref, p, part):
    row, over, base, shift = place(offset_ref, p)
    after = pl.multiple_of(base + PROBE, PROBE)
    first = ext[part, pl.ds(row, TALL), pl.ds(base, PROBE)]
    second = ext[part, pl.ds(row, TALL), pl.ds(after, PROBE)]
    block = jnp.where(lanes(TALL) >= shift, first, second)
    block = pltpu.roll(block, jnp.where(shift == 0, 0, PROBE - shift), 1)
    return pltpu.roll(block, jnp.where(over == 0, 0, TALL - over), 0)[:PROBE]


def turn_window(offset_ref, p, value):
    _, over, _, shift = place(offset_ref, p)
    block = jnp.concatenate([value, jnp.zeros((SUB, PROBE), F32)], axis=0)
    return pltpu.roll(pltpu.roll(block, over, 0), shift, 1)


def add_windows(grads, offset_ref, turned):
    for p in range(POS):
        row, _, base, shift = place(offset_ref, p)
        after = pl.multiple_of(base + PROBE, PROBE)
        here = lanes(TALL) >= shift
        for part in range(2):
            block = turned[part, p]
            where = (pl.ds(row, TALL), pl.ds(base, PROBE))
            grads[part][where] = grads[part][where] + jnp.where(here, block, 0.0)
            where = (pl.ds(row, TALL), pl.ds(after, PROBE))
            grads[part][where] = grads[part][where] + jnp.where(here, 0.0, block)


def times(ar, ai, br, bi):
    return ar * br - ai * bi, ar * bi + ai * br


def times_conj(ar, ai, br, bi):
    return ar * br + ai * bi, ar * bi - ai * br


def fill_first(ext, refs):
    tile, low, right, corner = refs
    t = TILE
    ext[:, :t, :t] = tile[:, 0]
    ext[:, t:, :t] = low[...]
    ext[:, :t, t:] = right[...]
    ext[:, t:, t:] = corner[...]


def fill_next(ext, refs):
    left, middle, right = refs
    t, h = TILE, PROBE
    ext[:, :, :h] = left[...]
    ext[:, :, h:t] = middle[...]
    ext[:, :, t:] = right[...]


def forward_kernel(fill, n_field, first, *refs):
    offset_ref, table_ref, phase_ref, wave = refs[:4]
    field = refs[4 : 4 + n_field]
    windows, out, ext, work = refs[4 + n_field :]
    fill(ext, field)
    right, left = tables_of(table_ref)
    for n in range(PAIRS):
        rows = []
        for q in (2 * n, 2 * n + 1):
            tr = take_window(ext, offset_ref, q, 0)
            ti = take_window(ext, offset_ref, q, 1)
            windows[0, q] = tr
            windows[1, q] = ti
            if first:
                wr, wi = wave[0], wave[1]
            else:
                wr, wi = wave[0, q], wave[1, q]
            rows.append(jnp.concatenate(times(wr, wi, tr, ti), axis=1))
        keep(work, n, 0, jnp.concatenate(rows, axis=0))

    def finish(n, block):
        put_pair(out, 2 * n, block)

    propagate(work, right, left, phase_ref[0], phase_ref[1], finish)


def write_gradient(grads, outs):
    for n, out in enumerate(outs):
        for part in range(2):
            out[part] = grads[part][:, n * PROBE : (n + 1) * PROBE]


def turn_kernel(fill, n_field, *refs):
    offset_ref, table_ref, intensity, wave = refs[:4]
    field = refs[4 : 4 + n_field]
    outs = refs[4 + n_field : 7 + n_field]
    back, ext, windows, work, turned, *grads = refs[7 + n_field :]
    fill(ext, field)
    for part in grads:
        part[...] = jnp.zeros_like(part)
    right, left = tables_of(table_ref)
    h = PROBE
    for n in range(PAIRS):
        rows = []
        for q in (2 * n, 2 * n + 1):
            tr = take_window(ext, offset_ref, q, 0)
            ti = take_window(ext, offset_ref, q, 1)
            windows[0, q] = tr
            windows[1, q] = ti
            rows.append(jnp.concatenate(times(wave[0, q], wave[1, q], tr, ti), axis=1))
        keep(work, n, 0, jnp.concatenate(rows, axis=0))
    for n in range(PAIRS):
        keep(work, n, 1, side_to_stack(times_right(kept(work, n, 0), right)))
    for n in range(PAIRS):
        block = times_left(kept(work, n, 1), left)
        re, im = block[:h], block[h:]
        target = jnp.concatenate([intensity[2 * n], intensity[2 * n + 1]], axis=1)
        weight = 4.0 * (re * re + im * im - target)
        keep(work, n, 0, jnp.concatenate([re * weight, im * weight], axis=0))
    for n in range(PAIRS):
        keep(work, n, 1, side_to_stack(times_left(kept(work, n, 0), right)))
    for n in range(PAIRS):
        block = times_right(kept(work, n, 1), left)
        for i in range(2):
            q = 2 * n + i
            gr, gi = block[i * h : (i + 1) * h, :h], block[i * h : (i + 1) * h, h:]
            br, bi = times_conj(windows[0, q], windows[1, q], gr, gi)
            back[0, q] = br
            back[1, q] = bi
            dr, di = times_conj(wave[0, q], wave[1, q], gr, gi)
            turned[0, q] = turn_window(offset_ref, q, dr)
            turned[1, q] = turn_window(offset_ref, q, di)
    add_windows(grads, offset_ref, turned)
    write_gradient(grads, outs)


def backward_kernel(first, *refs):
    if first:
        offset_ref, table_ref, phase_ref, back_in, wave = refs[:5]
        outs = refs[5:8]
    else:
        offset_ref, table_ref, phase_ref, back_in, wave, windows = refs[:6]
        outs, back = refs[6:9], refs[9]
    work, turned, *grads = refs[-4:]
    for part in grads:
        part[...] = jnp.zeros_like(part)
    right, left = tables_of(table_ref)
    h = PROBE
    for n in range(PAIRS):
        keep(work, n, 0, pair_of(back_in, 2 * n))

    def finish(n, block):
        for i in range(2):
            q = 2 * n + i
            gr, gi = block[i * h : (i + 1) * h, :h], block[i * h : (i + 1) * h, h:]
            if first:
                dr, di = times_conj(wave[0], wave[1], gr, gi)
            else:
                br, bi = times_conj(windows[0, q], windows[1, q], gr, gi)
                back[0, q] = br
                back[1, q] = bi
                dr, di = times_conj(wave[0, q], wave[1, q], gr, gi)
            turned[0, q] = turn_window(offset_ref, q, dr)
            turned[1, q] = turn_window(offset_ref, q, di)

    propagate(work, right, left, phase_ref[0], -phase_ref[1], finish)
    add_windows(grads, offset_ref, turned)
    write_gradient(grads, outs)


def whole(array):
    rank = len(array.shape)
    return pl.BlockSpec(array.shape, lambda i: (0,) * rank)


def tile_of(layer):
    return pl.BlockSpec((2, 1, TILE, TILE), lambda i: (0, layer, 0, 0))


def shape(*dims):
    return jax.ShapeDtypeStruct(dims, F32)


STACK = (2, POS, PROBE, PROBE)
GRADIENT = [shape(2, EXT, PROBE)] * 3
WORK = pltpu.VMEM((2, PAIRS, 2, 256, 256), BF16)
SCRATCH = pltpu.VMEM((2, EXT, EXT), F32)
GRADS = [pltpu.VMEM((2, POS, TALL, PROBE), F32)] + [pltpu.VMEM((EXT, EXT), F32)] * 2


def run(body, operands, outs, scratch, stages, specs=None):
    specs = specs or {}
    flops = stages * POS * PROBE * 256 * 256 * 2 * 3
    moved = sum(math.prod(o.shape) * 4 for o in operands) + sum(math.prod(o.shape) * 4 for o in outs)
    in_specs = [pl.BlockSpec(memory_space=pltpu.SMEM)]
    in_specs += [specs.get(n, None) or whole(o) for n, o in enumerate(operands) if n > 0]
    return pl.pallas_call(
        body,
        grid=(1,),
        in_specs=in_specs,
        out_specs=[whole(o) for o in outs],
        out_shape=outs,
        scratch_shapes=scratch,
        cost_estimate=pl.CostEstimate(flops=flops, bytes_accessed=moved, transcendentals=0),
        compiler_params=pltpu.CompilerParams(vmem_limit_bytes=40 * 2**20),
    )(*operands)


def forward(offsets, tables, phase, wave, field, layer, fill, first):
    operands = [offsets, tables, phase, wave, *field]
    specs = {4: tile_of(layer)} if fill is fill_first else {}
    body = functools.partial(forward_kernel, fill, len(field), first)
    return run(body, operands, [shape(*STACK)] * 2, [SCRATCH, WORK], 4, specs)


def turn(offsets, tables, intensity, wave, field, layer, fill):
    operands = [offsets, tables, intensity, wave, *field]
    specs = {4: tile_of(layer)} if fill is fill_first else {}
    body = functools.partial(turn_kernel, fill, len(field))
    return run(body, operands, [*GRADIENT, shape(*STACK)], [SCRATCH, pltpu.VMEM(STACK, F32), WORK, *GRADS], 4, specs)


def backward(offsets, tables, phase, back, wave, windows):
    first = windows is None
    operands = [offsets, tables, phase, back, wave] + ([] if first else [windows])
    outs = [*GRADIENT] if first else [*GRADIENT, shape(*STACK)]
    return run(functools.partial(backward_kernel, first), operands, outs, [WORK, *GRADS], 4)


def shifted(block, axis, distance):
    size = lax.axis_size(axis)
    return lax.ppermute(block, axis, [((i - distance) % size, i) for i in range(size)])


def plain(body, outs, operands, specs=None, aliases=None, out_specs=None):
    specs = specs or {}
    moved = sum(math.prod(o.shape) * 4 for o in outs)
    return pl.pallas_call(
        body,
        grid=(1,),
        in_specs=[specs.get(n, None) or whole(o) for n, o in enumerate(operands)],
        out_specs=out_specs or [whole(o) for o in outs],
        out_shape=outs,
        input_output_aliases=aliases or {},
        cost_estimate=pl.CostEstimate(flops=0, bytes_accessed=2 * moved, transcendentals=0),
        compiler_params=pltpu.CompilerParams(vmem_limit_bytes=24 * 2**20),
    )(*operands)


ROWS = shape(2, PROBE, TILE)
SIDE = shape(2, EXT, PROBE)


def pack_kernel(layer, tile, rows, cols, sems):
    first = pltpu.make_async_copy(tile.at[:, layer, pl.ds(0, PROBE)], rows, sems.at[0])
    second = pltpu.make_async_copy(tile.at[:, layer, :, pl.ds(0, PROBE)], cols, sems.at[1])
    first.start()
    second.start()
    first.wait()
    second.wait()


def pack(object_field, layer):
    cols = shape(2, TILE, PROBE)
    return pl.pallas_call(
        functools.partial(pack_kernel, layer),
        in_specs=[pl.BlockSpec(memory_space=pltpu.HBM)],
        out_specs=[pl.BlockSpec(memory_space=pltpu.VMEM)] * 2,
        out_shape=[ROWS, cols],
        scratch_shapes=[pltpu.SemaphoreType.DMA((2,))],
        name="pack",
        cost_estimate=pl.CostEstimate(flops=0, bytes_accessed=4 * 2**18, transcendentals=0),
    )(object_field)


def sums_kernel(both, left, middle, from_left, *outs):
    h, t = PROBE, TILE
    down = outs[0]
    down[:, :, :h] = left[:, t:] + from_left[:, t:]
    down[:, :, h:] = middle[:, t:]
    if both:
        up = outs[1]
        up[:, :, :h] = left[:, :h] + from_left[:, :h]
        up[:, :, h:] = middle[:, :h]


def sums(left, middle, from_left, both):
    body = functools.partial(sums_kernel, both)
    return plain(body, [ROWS] * (1 + both), [left, middle, from_left])


def update_kernel(tile, low, left, middle, from_left, above, below, new_l, new_m):
    h, t = PROBE, TILE
    top, mid, end = slice(0, h), slice(h, t), slice(t, t + h)
    for new, grad, cols in ((new_l, left, slice(0, h)), (new_m, middle, slice(h, t))):
        extra = (lambda rows: grad[:, rows] + from_left[:, rows]) if new is new_l else (lambda rows: grad[:, rows])
        new[:, top] = tile[:, 0, top, cols] - STEP * (extra(top) + above[:, :, cols])
        new[:, mid] = tile[:, 0, mid, cols] - STEP * extra(mid)
        new[:, end] = low[:, :, cols] - STEP * (extra(end) + below[:, :, cols])


def update(object_field, layer, low, grad, from_left, above, below):
    operands = [object_field, low, grad[0], grad[1], from_left, above, below]
    return plain(update_kernel, [SIDE] * 2, operands, {0: tile_of(layer)})


def last_kernel(n_alias, *refs):
    old_l, old_m, left, middle, from_left, above = refs[:6]
    out = refs[6 + n_alias]
    h, t = PROBE, TILE
    out[:, 0, :h, :h] = old_l[:, :h] - STEP * (left[:, :h] + from_left[:, :h] + above[:, :, :h])
    out[:, 0, h:, :h] = old_l[:, h:t] - STEP * (left[:, h:t] + from_left[:, h:t])
    out[:, 0, :h, h:] = old_m[:, :h] - STEP * (middle[:, :h] + above[:, :, h:])
    out[:, 0, h:, h:] = old_m[:, h:t] - STEP * middle[:, h:t]


def last(result, layer, field, grad, from_left, above):
    operands = [field[0], field[1], grad[0], grad[1], from_left, above]
    specs, aliases = {}, {}
    if result is not None:
        operands.append(result)
        specs, aliases = {6: pl.BlockSpec(memory_space=pl.ANY)}, {6: 0}
    return plain(
        functools.partial(last_kernel, len(operands) - 6),
        [shape(2, SLICES, TILE, TILE)],
        operands,
        specs,
        aliases,
        [tile_of(layer)],
    )[0]


def on_device(object_field, probe, propagator, measured, offsets):
    h = PROBE
    tables = jnp.asarray(dft_tables())
    offsets = offsets.reshape(POS, 2)
    intensity = measured.reshape(POS, h, h)
    phase = jnp.stack([jnp.cos(propagator), jnp.sin(propagator)])

    packed = [pack(object_field, layer) for layer in range(SLICES)]
    lows, fields = [], []
    for rows, cols in packed:
        low = shifted(rows, "row", -1)
        right = shifted(cols, "col", -1)
        corner = shifted(low[:, :, :h], "col", -1)
        lows.append(low)
        fields.append([object_field, low, right, corner])

    def gradients(fields, fill):
        _, wave1 = forward(offsets, tables, phase, probe, fields[0], 0, fill, True)
        win1, wave2 = forward(offsets, tables, phase, wave1, fields[1], 1, fill, False)
        *grad2, back = turn(offsets, tables, intensity, wave2, fields[2], 2, fill)
        *grad1, back = backward(offsets, tables, phase, back, wave1, win1)
        grad0 = backward(offsets, tables, phase, back, probe, None)
        return [grad0, grad1, grad2]

    grads = gradients(fields, fill_first)
    fields = [None] * SLICES
    for layer in (2, 1, 0):
        grad = grads[layer]
        from_left = shifted(grad[2], "col", 1)
        down, up = sums(grad[0], grad[1], from_left, True)
        above = shifted(down, "row", 1)
        below = shifted(up, "row", -1)
        new_l, new_m = update(object_field, layer, lows[layer], grad, from_left, above, below)
        fields[layer] = [new_l, new_m, shifted(new_l, "col", -1)]
    grads = gradients(fields, fill_next)
    result = None
    for layer in (2, 1, 0):
        grad = grads[layer]
        from_left = shifted(grad[2], "col", 1)
        down = sums(grad[0], grad[1], from_left, False)[0]
        above = shifted(down, "row", 1)
        result = last(result, layer, fields[layer], grad, from_left, above)
    return result


def solution(mesh):
    placed = (
        P(None, None, "row", "col"),
        P(),
        P(),
        P("row", "col", None, None, None),
        P("row", "col", None, None),
    )
    return jax.shard_map(
        on_device,
        mesh=mesh,
        in_specs=placed,
        out_specs=P(None, None, "row", "col"),
        check_vma=False,
    )
```

```python
import functools
import math

import jax
import jax.numpy as jnp
import numpy as np
from jax import lax
from jax.experimental import pallas as pl
from jax.experimental.pallas import tpu as pltpu
from jax.sharding import PartitionSpec as P


PROBE = 128
SLICES = 3
POS = 6
TILE = 256
EXT = TILE + PROBE
SUB = 8
STEP = 0.05
F32 = jnp.float32
BF16 = jnp.bfloat16


def dft_tables():
    index = np.arange(PROBE)
    angle = (index[:, None] * index[None, :] % PROBE) * (-2.0 * math.pi / PROBE)
    cosines, sines = np.cos(angle) / math.sqrt(PROBE), np.sin(angle) / math.sqrt(PROBE)
    right = np.block([[cosines, sines], [-sines, cosines]]).astype(np.float32)
    left = np.block([[cosines, -sines], [sines, cosines]]).astype(np.float32)
    parts = []
    for matrix in (right, left):
        high = matrix.astype(BF16)
        parts += [high, (matrix - high.astype(np.float32)).astype(BF16)]
    return np.stack(parts)


def split(value):
    high = value.astype(BF16)
    return high, (value - high.astype(F32)).astype(BF16)


def dot(a, b):
    return jnp.dot(a, b, preferred_element_type=F32)


def times_right(block, table):
    high, low = block
    wide, fine = table
    return dot(jnp.concatenate([high, low, high], axis=1), jnp.concatenate([wide, wide, fine], axis=0))


def times_left(block, table):
    high, low = block
    wide, fine = table
    return dot(jnp.concatenate([wide, wide, fine], axis=1), jnp.concatenate([high, low, high], axis=0))


def side_to_stack(block):
    h = PROBE
    top = jnp.concatenate([block[:h, :h], block[h:, :h]], axis=1)
    low = jnp.concatenate([block[:h, h:], block[h:, h:]], axis=1)
    return jnp.concatenate([top, low], axis=0)


def times_phase(block, phase_real, phase_imag):
    h = PROBE
    re, im = block[:h], block[h:]
    pr = jnp.concatenate([phase_real, phase_real], axis=1)
    pi = jnp.concatenate([phase_imag, phase_imag], axis=1)
    return jnp.concatenate([re * pr - im * pi, re * pi + im * pr], axis=0)


def keep(work, n, slot, block):
    work[slot, n, 0], work[slot, n, 1] = split(block)


def kept(work, n, slot):
    return work[slot, n, 0], work[slot, n, 1]


PAIRS = POS // 2


def propagate(work, right, left, phase_real, phase_imag, finish):
    for n in range(PAIRS):
        keep(work, n, 1, side_to_stack(times_right(kept(work, n, 0), right)))
    for n in range(PAIRS):
        keep(work, n, 0, times_phase(times_left(kept(work, n, 1), left), phase_real, phase_imag))
    for n in range(PAIRS):
        keep(work, n, 1, side_to_stack(times_left(kept(work, n, 0), right)))
    for n in range(PAIRS):
        finish(n, times_right(kept(work, n, 1), left))


def tables_of(table_ref):
    right = (table_ref[0], table_ref[1])
    left = (table_ref[2], table_ref[3])
    return right, left


def pair_of(ref, p):
    top = jnp.concatenate([ref[0, p], ref[1, p]], axis=1)
    low = jnp.concatenate([ref[0, p + 1], ref[1, p + 1]], axis=1)
    return jnp.concatenate([top, low], axis=0)


def put_pair(ref, p, block):
    h = PROBE
    ref[0, p] = block[:h, :h]
    ref[1, p] = block[:h, h:]
    ref[0, p + 1] = block[h:, :h]
    ref[1, p + 1] = block[h:, h:]


def place(offset_ref, p):
    row, col = offset_ref[p, 0], offset_ref[p, 1]
    over = lax.rem(row, SUB)
    base = jnp.where(col >= PROBE, PROBE, 0)
    return pl.multiple_of(row - over, SUB), over, pl.multiple_of(base, PROBE), col - base


TALL = PROBE + SUB


def lanes(rows):
    return lax.broadcasted_iota(jnp.int32, (rows, PROBE), 1)


def take_window(ext, offset_ref, p, part):
    row, over, base, shift = place(offset_ref, p)
    after = pl.multiple_of(base + PROBE, PROBE)
    first = ext[part, pl.ds(row, TALL), pl.ds(base, PROBE)]
    second = ext[part, pl.ds(row, TALL), pl.ds(after, PROBE)]
    block = jnp.where(lanes(TALL) >= shift, first, second)
    block = pltpu.roll(block, jnp.where(shift == 0, 0, PROBE - shift), 1)
    return pltpu.roll(block, jnp.where(over == 0, 0, TALL - over), 0)[:PROBE]


def turn_window(offset_ref, p, value):
    _, over, _, shift = place(offset_ref, p)
    block = jnp.concatenate([value, jnp.zeros((SUB, PROBE), F32)], axis=0)
    return pltpu.roll(pltpu.roll(block, over, 0), shift, 1)


def add_windows(grads, offset_ref, turned):
    for p in range(POS):
        row, _, base, shift = place(offset_ref, p)
        after = pl.multiple_of(base + PROBE, PROBE)
        here = lanes(TALL) >= shift
        for part in range(2):
            block = turned[part, p]
            where = (pl.ds(row, TALL), pl.ds(base, PROBE))
            grads[part][where] = grads[part][where] + jnp.where(here, block, 0.0)
            where = (pl.ds(row, TALL), pl.ds(after, PROBE))
            grads[part][where] = grads[part][where] + jnp.where(here, 0.0, block)


def times(ar, ai, br, bi):
    return ar * br - ai * bi, ar * bi + ai * br


def times_conj(ar, ai, br, bi):
    return ar * br + ai * bi, ar * bi - ai * br


def fill_first(ext, refs):
    tile, low, right, corner = refs
    t = TILE
    ext[:, :t, :t] = tile[:, 0]
    ext[:, t:, :t] = low[...]
    ext[:, :t, t:] = right[...]
    ext[:, t:, t:] = corner[...]


def fill_next(ext, refs):
    left, middle, right = refs
    t, h = TILE, PROBE
    ext[:, :, :h] = left[...]
    ext[:, :, h:t] = middle[...]
    ext[:, :, t:] = right[...]


def forward_kernel(fill, n_field, first, *refs):
    offset_ref, table_ref, phase_ref = refs[:3]
    wave = None if first else refs[3]
    field = refs[4 - first : 4 - first + n_field]
    windows, out, ext, work = refs[4 - first + n_field :]
    fill(ext, field)
    right, left = tables_of(table_ref)
    for n in range(PAIRS):
        rows = []
        for q in (2 * n, 2 * n + 1):
            tr = take_window(ext, offset_ref, q, 0)
            ti = take_window(ext, offset_ref, q, 1)
            windows[0, q] = tr
            windows[1, q] = ti
            if first:
                wr, wi = phase_ref[0], phase_ref[1]
            else:
                wr, wi = wave[0, q], wave[1, q]
            rows.append(jnp.concatenate(times(wr, wi, tr, ti), axis=1))
        keep(work, n, 0, jnp.concatenate(rows, axis=0))

    def finish(n, block):
        put_pair(out, 2 * n, block)

    propagate(work, right, left, phase_ref[2], phase_ref[3], finish)


def write_gradient(grads, outs):
    left, middle, low, right = outs
    h, t = PROBE, TILE
    for part in range(2):
        left[part] = grads[part][:, :h]
        middle[part] = grads[part][:t, h:t]
        low[part] = grads[part][t:, h:t]
        right[part] = grads[part][:, t:]


def turn_kernel(fill, n_field, *refs):
    offset_ref, table_ref, intensity, wave = refs[:4]
    field = refs[4 : 4 + n_field]
    outs = refs[4 + n_field : 8 + n_field]
    back, ext, windows, work, turned, *grads = refs[8 + n_field :]
    fill(ext, field)
    for part in grads:
        part[...] = jnp.zeros_like(part)
    right, left = tables_of(table_ref)
    h = PROBE
    for n in range(PAIRS):
        rows = []
        for q in (2 * n, 2 * n + 1):
            tr = take_window(ext, offset_ref, q, 0)
            ti = take_window(ext, offset_ref, q, 1)
            windows[0, q] = tr
            windows[1, q] = ti
            rows.append(jnp.concatenate(times(wave[0, q], wave[1, q], tr, ti), axis=1))
        keep(work, n, 0, jnp.concatenate(rows, axis=0))
    for n in range(PAIRS):
        keep(work, n, 1, side_to_stack(times_right(kept(work, n, 0), right)))
    for n in range(PAIRS):
        block = times_left(kept(work, n, 1), left)
        re, im = block[:h], block[h:]
        target = jnp.concatenate([intensity[2 * n], intensity[2 * n + 1]], axis=1)
        weight = 4.0 * (re * re + im * im - target)
        keep(work, n, 0, jnp.concatenate([re * weight, im * weight], axis=0))
    for n in range(PAIRS):
        keep(work, n, 1, side_to_stack(times_left(kept(work, n, 0), right)))
    for n in range(PAIRS):
        block = times_right(kept(work, n, 1), left)
        for i in range(2):
            q = 2 * n + i
            gr, gi = block[i * h : (i + 1) * h, :h], block[i * h : (i + 1) * h, h:]
            br, bi = times_conj(windows[0, q], windows[1, q], gr, gi)
            back[0, q] = br
            back[1, q] = bi
            dr, di = times_conj(wave[0, q], wave[1, q], gr, gi)
            turned[0, q] = turn_window(offset_ref, q, dr)
            turned[1, q] = turn_window(offset_ref, q, di)
    add_windows(grads, offset_ref, turned)
    write_gradient(grads, outs)


def backward_kernel(first, *refs):
    if first:
        offset_ref, table_ref, phase_ref, back_in = refs[:4]
        outs = refs[4:8]
    else:
        offset_ref, table_ref, phase_ref, back_in, wave, windows = refs[:6]
        outs, back = refs[6:10], refs[10]
    work, turned, *grads = refs[-4:]
    for part in grads:
        part[...] = jnp.zeros_like(part)
    right, left = tables_of(table_ref)
    h = PROBE
    for n in range(PAIRS):
        keep(work, n, 0, pair_of(back_in, 2 * n))

    def finish(n, block):
        for i in range(2):
            q = 2 * n + i
            gr, gi = block[i * h : (i + 1) * h, :h], block[i * h : (i + 1) * h, h:]
            if first:
                dr, di = times_conj(phase_ref[0], phase_ref[1], gr, gi)
            else:
                br, bi = times_conj(windows[0, q], windows[1, q], gr, gi)
                back[0, q] = br
                back[1, q] = bi
                dr, di = times_conj(wave[0, q], wave[1, q], gr, gi)
            turned[0, q] = turn_window(offset_ref, q, dr)
            turned[1, q] = turn_window(offset_ref, q, di)

    propagate(work, right, left, phase_ref[2], -phase_ref[3], finish)
    add_windows(grads, offset_ref, turned)
    write_gradient(grads, outs)


def whole(array):
    rank = len(array.shape)
    return pl.BlockSpec(array.shape, lambda i: (0,) * rank)


def tile_of(layer):
    return pl.BlockSpec((2, 1, TILE, TILE), lambda i: (0, layer, 0, 0))


def shape(*dims):
    return jax.ShapeDtypeStruct(dims, F32)


STACK = (2, POS, PROBE, PROBE)
GRADIENT = [
    shape(2, EXT, PROBE),
    shape(2, TILE, PROBE),
    shape(2, PROBE, PROBE),
    shape(2, EXT, PROBE),
]
WORK = pltpu.VMEM((2, PAIRS, 2, 256, 256), BF16)
SCRATCH = pltpu.VMEM((2, EXT, EXT), F32)
GRADS = [pltpu.VMEM((2, POS, TALL, PROBE), F32)] + [pltpu.VMEM((EXT, EXT), F32)] * 2


def run(body, operands, outs, scratch, stages, specs=None):
    specs = specs or {}
    flops = stages * POS * PROBE * 256 * 256 * 2 * 3
    moved = sum(math.prod(o.shape) * 4 for o in operands) + sum(math.prod(o.shape) * 4 for o in outs)
    in_specs = [pl.BlockSpec(memory_space=pltpu.SMEM)]
    in_specs += [specs.get(n, None) or whole(o) for n, o in enumerate(operands) if n > 0]
    return pl.pallas_call(
        body,
        grid=(1,),
        in_specs=in_specs,
        out_specs=[whole(o) for o in outs],
        out_shape=outs,
        scratch_shapes=scratch,
        cost_estimate=pl.CostEstimate(flops=flops, bytes_accessed=moved, transcendentals=0),
        compiler_params=pltpu.CompilerParams(vmem_limit_bytes=40 * 2**20),
    )(*operands)


def field_specs(start, layer, fill):
    if fill is not fill_first:
        return {}
    specs = {start: tile_of(layer)}
    if layer > 0:
        specs[start + 2] = pl.BlockSpec((2, None, TILE, PROBE), lambda i: (0, layer - 1, 0, 0))
    return specs


def forward(offsets, tables, phase, wave, field, layer, fill):
    first = wave is None
    operands = [offsets, tables, phase] + ([] if first else [wave])
    specs = field_specs(len(operands), layer, fill)
    body = functools.partial(forward_kernel, fill, len(field), first)
    return run(body, operands + field, [shape(*STACK)] * 2, [SCRATCH, WORK], 4, specs)


def turn(offsets, tables, intensity, wave, field, layer, fill):
    operands = [offsets, tables, intensity, wave]
    specs = field_specs(len(operands), layer, fill)
    body = functools.partial(turn_kernel, fill, len(field))
    scratch = [SCRATCH, pltpu.VMEM(STACK, F32), WORK, *GRADS]
    return run(body, operands + field, [*GRADIENT, shape(*STACK)], scratch, 4, specs)


def backward(offsets, tables, phase, back, wave, windows):
    first = wave is None
    operands = [offsets, tables, phase, back] + ([] if first else [wave, windows])
    outs = [*GRADIENT] if first else [*GRADIENT, shape(*STACK)]
    return run(functools.partial(backward_kernel, first), operands, outs, [WORK, *GRADS], 4)


def shifted(block, axis, distance):
    size = lax.axis_size(axis)
    return lax.ppermute(block, axis, [((i - distance) % size, i) for i in range(size)])


def swapped(block, odd):
    size = lax.axis_size("row")
    route = []
    for i in range(odd, size + odd, 2):
        route += [(i % size, (i + 1) % size), ((i + 1) % size, i % size)]
    return lax.ppermute(block, "row", sorted(route))


def plain(body, outs, operands, specs=None, aliases=None, out_specs=None):
    specs = specs or {}
    moved = sum(math.prod(o.shape) * 4 for o in outs)
    return pl.pallas_call(
        body,
        grid=(1,),
        in_specs=[specs.get(n, None) or whole(o) for n, o in enumerate(operands)],
        out_specs=out_specs or [whole(o) for o in outs],
        out_shape=outs,
        input_output_aliases=aliases or {},
        cost_estimate=pl.CostEstimate(flops=0, bytes_accessed=2 * moved, transcendentals=0),
        compiler_params=pltpu.CompilerParams(vmem_limit_bytes=24 * 2**20),
    )(*operands)


IN_SMEM = pl.BlockSpec(memory_space=pltpu.SMEM)
SIDE = shape(2, EXT, PROBE)


def pack_kernel(jobs, tile, *refs):
    outs, sems = refs[:-1], refs[-1]
    copies = [
        pltpu.make_async_copy(tile.at[:, layer, rows, cols], out, sems.at[n])
        for n, ((layer, rows, cols), out) in enumerate(zip(jobs, outs))
    ]
    for copy in copies:
        copy.start()
    for copy in copies:
        copy.wait()


def pack(object_field, jobs, outs):
    return pl.pallas_call(
        functools.partial(pack_kernel, jobs),
        in_specs=[pl.BlockSpec(memory_space=pltpu.HBM)],
        out_specs=[pl.BlockSpec(memory_space=pltpu.VMEM)] * len(outs),
        out_shape=outs,
        scratch_shapes=[pltpu.SemaphoreType.DMA((len(outs),))],
        name="pack",
        cost_estimate=pl.CostEstimate(flops=0, bytes_accessed=4 * 2**18, transcendentals=0),
    )(object_field)


def sums_kernel(wide, parity, left, middle, low, right, from_left, *refs):
    h, t = PROBE, TILE
    from_right = refs[0] if wide else None
    even_out, odd_out = refs[-2:]

    def fill(down, up):
        down[:, :, :h] = left[:, t:] + from_left[:, t:]
        up[:, :, :h] = left[:, :h] + from_left[:, :h]
        down[:, :, h:t] = low[...]
        up[:, :, h:t] = middle[:, :h]
        if wide:
            down[:, :, t:] = right[:, t:] + from_right[:, t:]
            up[:, :, t:] = right[:, :h] + from_right[:, :h]

    @pl.when(parity[0] == 0)
    def _():
        fill(even_out, odd_out)

    @pl.when(parity[0] == 1)
    def _():
        fill(odd_out, even_out)


def sums(parity, grad, from_left, from_right):
    wide = from_right is not None
    operands = [parity, *grad, from_left] + ([from_right] if wide else [])
    outs = [shape(2, PROBE, EXT if wide else TILE)] * 2
    return plain(functools.partial(sums_kernel, wide), outs, operands, {0: IN_SMEM})


def update_kernel(wide, parity, *refs):
    h, t = PROBE, TILE
    if wide:
        tile, low, side, corner, left, middle, bottom, right, from_left, from_right, even, odd = refs[:12]
        new_l, new_m, new_r = refs[12:]
    else:
        tile, low, left, middle, bottom, from_left, even, odd, new_l, new_m = refs
    top, mid, end = slice(0, h), slice(h, t), slice(t, t + h)
    first, second, third = slice(0, h), slice(h, t), slice(t, t + h)

    swap = parity[0] == 1

    class Chosen:
        def __init__(self, first, second):
            self.first, self.second = first, second

        def __getitem__(self, where):
            return jnp.where(swap, self.second[where], self.first[where])

    def fill(above, below):
        new_l[:, top] = tile[:, 0, top, first] - STEP * (left[:, top] + from_left[:, top] + above[:, :, first])
        new_l[:, mid] = tile[:, 0, mid, first] - STEP * (left[:, mid] + from_left[:, mid])
        new_l[:, end] = low[:, :, first] - STEP * (left[:, end] + from_left[:, end] + below[:, :, first])
        new_m[:, top] = tile[:, 0, top, second] - STEP * (middle[:, top] + above[:, :, second])
        new_m[:, mid] = tile[:, 0, mid, second] - STEP * middle[:, mid]
        new_m[:, end] = low[:, :, second] - STEP * (bottom[...] + below[:, :, second])
        if wide:
            new_r[:, top] = side[:, top] - STEP * (right[:, top] + from_right[:, top] + above[:, :, third])
            new_r[:, mid] = side[:, mid] - STEP * (right[:, mid] + from_right[:, mid])
            new_r[:, end] = corner[...] - STEP * (right[:, end] + from_right[:, end] + below[:, :, third])

    fill(Chosen(odd, even), Chosen(even, odd))


def update(parity, layer, field, grad, from_left, from_right, even, odd):
    tile, low, side, corner = field
    if from_right is None:
        operands = [parity, tile, low, *grad[:3], from_left, even, odd]
        specs = {0: IN_SMEM, 1: tile_of(layer)}
        return plain(functools.partial(update_kernel, False), [SIDE] * 2, operands, specs)
    operands = [parity, tile, low, side, corner, *grad, from_left, from_right, even, odd]
    specs = {0: IN_SMEM, **field_specs(1, layer, fill_first)}
    return plain(functools.partial(update_kernel, True), [SIDE] * 3, operands, specs)


def spill_kernel(left, from_left, down):
    down[...] = left[:, TILE:] + from_left[:, TILE:]


def last_kernel(n_alias, *refs):
    old_l, old_m, left, middle, from_left, above_l, above_m = refs[:7]
    out = refs[7 + n_alias]
    h, t = PROBE, TILE
    out[:, 0, :h, :h] = old_l[:, :h] - STEP * (left[:, :h] + from_left[:, :h] + above_l[...])
    out[:, 0, h:, :h] = old_l[:, h:t] - STEP * (left[:, h:t] + from_left[:, h:t])
    out[:, 0, :h, h:] = old_m[:, :h] - STEP * (middle[:, :h] + above_m[...])
    out[:, 0, h:, h:] = old_m[:, h:t] - STEP * middle[:, h:t]


def last(result, layer, field, grad, from_left, above_l, above_m):
    operands = [field[0], field[1], grad[0], grad[1], from_left, above_l, above_m]
    specs, aliases = {}, {}
    if result is not None:
        operands.append(result)
        specs, aliases = {7: pl.BlockSpec(memory_space=pl.ANY)}, {7: 0}
    return plain(
        functools.partial(last_kernel, len(operands) - 7),
        [shape(2, SLICES, TILE, TILE)],
        operands,
        specs,
        aliases,
        [tile_of(layer)],
    )[0]


def on_device(object_field, probe, propagator, measured, offsets):
    h, t = PROBE, TILE
    tables = jnp.asarray(dft_tables())
    offsets = offsets.reshape(POS, 2)
    intensity = measured.reshape(POS, h, h)
    phase = jnp.stack([probe[0], probe[1], jnp.cos(propagator), jnp.sin(propagator)])
    parity = (lax.axis_index("row") & 1).astype(jnp.int32).reshape(1)

    top, all_rows, left, all_cols = pl.ds(0, h), pl.ds(0, t), pl.ds(0, h), pl.ds(0, t)
    rows_shape = shape(2, h, t)
    rows0, cols0 = pack(
        object_field, [(0, top, all_cols), (0, all_rows, left)], [rows_shape, shape(2, t, h)]
    )
    rows1, rows2, cols12 = pack(
        object_field,
        [(1, top, all_cols), (2, top, all_cols), (pl.ds(1, 2), all_rows, left)],
        [rows_shape, rows_shape, shape(2, 2, t, h)],
    )
    right0 = shifted(cols0, "col", -1)
    right12 = shifted(cols12, "col", -1)
    fields = []
    for layer, rows in enumerate((rows0, rows1, rows2)):
        low = shifted(rows, "row", -1)
        corner = shifted(low[:, :, :h], "col", -1)
        fields.append([object_field, low, right0 if layer == 0 else right12, corner])

    def gradients(fields, fill):
        _, wave1 = forward(offsets, tables, phase, None, fields[0], 0, fill)
        win1, wave2 = forward(offsets, tables, phase, wave1, fields[1], 1, fill)
        *grad2, back = turn(offsets, tables, intensity, wave2, fields[2], 2, fill)
        *grad1, back = backward(offsets, tables, phase, back, wave1, win1)
        grad0 = backward(offsets, tables, phase, back, None, None)
        return [grad0, grad1, grad2]

    grads = gradients(fields, fill_first)
    renewed = [None] * SLICES
    for layer in (2, 0, 1):
        grad, from_right = grads[layer], None
        from_left = shifted(grad[3], "col", 1)
        if layer == 1:
            from_right = shifted(grad[0], "col", -1)
        for_even, for_odd = sums(parity, grad, from_left, from_right)
        even = swapped(for_even, 0)
        odd = swapped(for_odd, 1)
        new = update(parity, layer, fields[layer], grad, from_left, from_right, even, odd)
        if layer != 1:
            new = [*new, shifted(new[0], "col", -1)]
        renewed[layer] = list(new)
    grads = gradients(renewed, fill_next)
    result = None
    for layer in (2, 1, 0):
        grad = grads[layer]
        from_left = shifted(grad[3], "col", 1)
        above_m = shifted(grad[2], "row", 1)
        down = plain(spill_kernel, [shape(2, h, h)], [grad[0], from_left])[0]
        above_l = shifted(down, "row", 1)
        result = last(result, layer, renewed[layer], grad, from_left, above_l, above_m)
    return result


def solution(mesh):
    placed = (
        P(None, None, "row", "col"),
        P(),
        P(),
        P("row", "col", None, None, None),
        P("row", "col", None, None),
    )
    return jax.shard_map(
        on_device,
        mesh=mesh,
        in_specs=placed,
        out_specs=P(None, None, "row", "col"),
        check_vma=False,
    )
```

```python
import functools
import math

import jax
import jax.numpy as jnp
import numpy as np
from jax import lax
from jax.experimental import pallas as pl
from jax.experimental.pallas import tpu as pltpu
from jax.sharding import PartitionSpec as P


PROBE = 128
SLICES = 3
POS = 6
TILE = 256
EXT = TILE + PROBE
SUB = 8
STEP = 0.05
F32 = jnp.float32
BF16 = jnp.bfloat16


def dft_tables():
    index = np.arange(PROBE)
    angle = (index[:, None] * index[None, :] % PROBE) * (-2.0 * math.pi / PROBE)
    cosines, sines = np.cos(angle) / math.sqrt(PROBE), np.sin(angle) / math.sqrt(PROBE)
    right = np.block([[cosines, sines], [-sines, cosines]]).astype(np.float32)
    left = np.block([[cosines, -sines], [sines, cosines]]).astype(np.float32)
    parts = []
    for matrix in (right, left):
        high = matrix.astype(BF16)
        parts += [high, (matrix - high.astype(np.float32)).astype(BF16)]
    return np.stack(parts)


def split(value):
    high = value.astype(BF16)
    return high, (value - high.astype(F32)).astype(BF16)


def dot(a, b):
    return jnp.dot(a, b, preferred_element_type=F32)


def times_right(block, table):
    high, low = block
    wide, fine = table
    return dot(jnp.concatenate([high, low, high], axis=1), jnp.concatenate([wide, wide, fine], axis=0))


def times_left(block, table):
    high, low = block
    wide, fine = table
    return dot(jnp.concatenate([wide, wide, fine], axis=1), jnp.concatenate([high, low, high], axis=0))


def side_to_stack(block):
    h = PROBE
    top = jnp.concatenate([block[:h, :h], block[h:, :h]], axis=1)
    low = jnp.concatenate([block[:h, h:], block[h:, h:]], axis=1)
    return jnp.concatenate([top, low], axis=0)


def times_phase(block, phase_real, phase_imag):
    h = PROBE
    re, im = block[:h], block[h:]
    pr = jnp.concatenate([phase_real, phase_real], axis=1)
    pi = jnp.concatenate([phase_imag, phase_imag], axis=1)
    return jnp.concatenate([re * pr - im * pi, re * pi + im * pr], axis=0)


def keep(work, n, slot, block):
    work[slot, n, 0], work[slot, n, 1] = split(block)


def kept(work, n, slot):
    return work[slot, n, 0], work[slot, n, 1]


PAIRS = POS // 2


def propagate(work, right, left, phase_real, phase_imag, finish):
    for n in range(PAIRS):
        keep(work, n, 1, side_to_stack(times_right(kept(work, n, 0), right)))
    for n in range(PAIRS):
        keep(work, n, 0, times_phase(times_left(kept(work, n, 1), left), phase_real, phase_imag))
    for n in range(PAIRS):
        keep(work, n, 1, side_to_stack(times_left(kept(work, n, 0), right)))
    for n in range(PAIRS):
        finish(n, times_right(kept(work, n, 1), left))


def tables_of(table_ref):
    right = (table_ref[0], table_ref[1])
    left = (table_ref[2], table_ref[3])
    return right, left


def pair_of(ref, p):
    top = jnp.concatenate([ref[0, p], ref[1, p]], axis=1)
    low = jnp.concatenate([ref[0, p + 1], ref[1, p + 1]], axis=1)
    return jnp.concatenate([top, low], axis=0)


def put_pair(ref, p, block):
    h = PROBE
    ref[0, p] = block[:h, :h]
    ref[1, p] = block[:h, h:]
    ref[0, p + 1] = block[h:, :h]
    ref[1, p + 1] = block[h:, h:]


def place(offset_ref, p):
    row, col = offset_ref[0, p], offset_ref[1, p]
    over = lax.rem(row, SUB)
    base = jnp.where(col >= PROBE, PROBE, 0)
    return pl.multiple_of(row - over, SUB), over, pl.multiple_of(base, PROBE), col - base


TALL = PROBE + SUB


def lanes(rows):
    return lax.broadcasted_iota(jnp.int32, (rows, PROBE), 1)


def take_window(ext, offset_ref, p, part):
    row, over, base, shift = place(offset_ref, p)
    after = pl.multiple_of(base + PROBE, PROBE)
    first = ext[part, pl.ds(row, TALL), pl.ds(base, PROBE)]
    second = ext[part, pl.ds(row, TALL), pl.ds(after, PROBE)]
    block = jnp.where(lanes(TALL) >= shift, first, second)
    block = pltpu.roll(block, jnp.where(shift == 0, 0, PROBE - shift), 1)
    return pltpu.roll(block, jnp.where(over == 0, 0, TALL - over), 0)[:PROBE]


def turn_window(offset_ref, p, value):
    _, over, _, shift = place(offset_ref, p)
    block = jnp.concatenate([value, jnp.zeros((SUB, PROBE), F32)], axis=0)
    return pltpu.roll(pltpu.roll(block, over, 0), shift, 1)


def add_windows(grads, offset_ref, turned):
    for p in range(POS):
        row, _, base, shift = place(offset_ref, p)
        after = pl.multiple_of(base + PROBE, PROBE)
        here = lanes(TALL) >= shift
        for part in range(2):
            block = turned[part, p]
            where = (pl.ds(row, TALL), pl.ds(base, PROBE))
            grads[part][where] = grads[part][where] + jnp.where(here, block, 0.0)
            where = (pl.ds(row, TALL), pl.ds(after, PROBE))
            grads[part][where] = grads[part][where] + jnp.where(here, 0.0, block)


def times(ar, ai, br, bi):
    return ar * br - ai * bi, ar * bi + ai * br


def times_conj(ar, ai, br, bi):
    return ar * br + ai * bi, ar * bi - ai * br


def fill_first(ext, refs):
    tile, low, right, corner = refs
    t = TILE
    ext[:, :t, :t] = tile[:, 0]
    ext[:, t:, :t] = low[...]
    ext[:, :t, t:] = right[...]
    ext[:, t:, t:] = corner[...]


def fill_next(ext, refs):
    left, middle, right = refs
    t, h = TILE, PROBE
    ext[:, :, :h] = left[...]
    ext[:, :, h:t] = middle[...]
    ext[:, :, t:] = right[...]


def forward_kernel(fill, n_field, first, *refs):
    offset_ref, table_ref, phase_ref = refs[:3]
    wave = None if first else refs[3]
    field = refs[4 - first : 4 - first + n_field]
    windows, out, ext, work = refs[4 - first + n_field :]
    fill(ext, field)
    right, left = tables_of(table_ref)
    for n in range(PAIRS):
        rows = []
        for q in (2 * n, 2 * n + 1):
            tr = take_window(ext, offset_ref, q, 0)
            ti = take_window(ext, offset_ref, q, 1)
            windows[0, q] = tr
            windows[1, q] = ti
            if first:
                wr, wi = phase_ref[0], phase_ref[1]
            else:
                wr, wi = wave[0, q], wave[1, q]
            rows.append(jnp.concatenate(times(wr, wi, tr, ti), axis=1))
        keep(work, n, 0, jnp.concatenate(rows, axis=0))

    def finish(n, block):
        put_pair(out, 2 * n, block)

    propagate(work, right, left, phase_ref[2], phase_ref[3], finish)


def write_gradient(grads, outs):
    left, middle, low, right = outs
    h, t = PROBE, TILE
    for part in range(2):
        left[part] = grads[part][:, :h]
        middle[part] = grads[part][:t, h:t]
        low[part] = grads[part][t:, h:t]
        right[part] = grads[part][:, t:]


def turn_kernel(fill, n_field, *refs):
    offset_ref, table_ref, intensity, wave = refs[:4]
    field = refs[4 : 4 + n_field]
    outs = refs[4 + n_field : 8 + n_field]
    back, ext, windows, work, turned, *grads = refs[8 + n_field :]
    fill(ext, field)
    for part in grads:
        part[...] = jnp.zeros_like(part)
    right, left = tables_of(table_ref)
    h = PROBE
    for n in range(PAIRS):
        rows = []
        for q in (2 * n, 2 * n + 1):
            tr = take_window(ext, offset_ref, q, 0)
            ti = take_window(ext, offset_ref, q, 1)
            windows[0, q] = tr
            windows[1, q] = ti
            rows.append(jnp.concatenate(times(wave[0, q], wave[1, q], tr, ti), axis=1))
        keep(work, n, 0, jnp.concatenate(rows, axis=0))
    for n in range(PAIRS):
        keep(work, n, 1, side_to_stack(times_right(kept(work, n, 0), right)))
    for n in range(PAIRS):
        block = times_left(kept(work, n, 1), left)
        re, im = block[:h], block[h:]
        target = jnp.concatenate([intensity[2 * n], intensity[2 * n + 1]], axis=1)
        weight = 4.0 * (re * re + im * im - target)
        keep(work, n, 0, jnp.concatenate([re * weight, im * weight], axis=0))
    for n in range(PAIRS):
        keep(work, n, 1, side_to_stack(times_left(kept(work, n, 0), right)))
    for n in range(PAIRS):
        block = times_right(kept(work, n, 1), left)
        for i in range(2):
            q = 2 * n + i
            gr, gi = block[i * h : (i + 1) * h, :h], block[i * h : (i + 1) * h, h:]
            br, bi = times_conj(windows[0, q], windows[1, q], gr, gi)
            back[0, q] = br
            back[1, q] = bi
            dr, di = times_conj(wave[0, q], wave[1, q], gr, gi)
            turned[0, q] = turn_window(offset_ref, q, dr)
            turned[1, q] = turn_window(offset_ref, q, di)
    add_windows(grads, offset_ref, turned)
    write_gradient(grads, outs)


def backward_kernel(first, *refs):
    if first:
        offset_ref, table_ref, phase_ref, back_in = refs[:4]
        outs = refs[4:8]
    else:
        offset_ref, table_ref, phase_ref, back_in, wave, windows = refs[:6]
        outs, back = refs[6:10], refs[10]
    work, turned, *grads = refs[-4:]
    for part in grads:
        part[...] = jnp.zeros_like(part)
    right, left = tables_of(table_ref)
    h = PROBE
    for n in range(PAIRS):
        keep(work, n, 0, pair_of(back_in, 2 * n))

    def finish(n, block):
        for i in range(2):
            q = 2 * n + i
            gr, gi = block[i * h : (i + 1) * h, :h], block[i * h : (i + 1) * h, h:]
            if first:
                dr, di = times_conj(phase_ref[0], phase_ref[1], gr, gi)
            else:
                br, bi = times_conj(windows[0, q], windows[1, q], gr, gi)
                back[0, q] = br
                back[1, q] = bi
                dr, di = times_conj(wave[0, q], wave[1, q], gr, gi)
            turned[0, q] = turn_window(offset_ref, q, dr)
            turned[1, q] = turn_window(offset_ref, q, di)

    propagate(work, right, left, phase_ref[2], -phase_ref[3], finish)
    add_windows(grads, offset_ref, turned)
    write_gradient(grads, outs)


def whole(array):
    rank = len(array.shape)
    return pl.BlockSpec(array.shape, lambda i: (0,) * rank)


def tile_of(layer):
    return pl.BlockSpec((2, 1, TILE, TILE), lambda i: (0, layer, 0, 0))


def shape(*dims):
    return jax.ShapeDtypeStruct(dims, F32)


STACK = (2, POS, PROBE, PROBE)
GRADIENT = [
    shape(2, EXT, PROBE),
    shape(2, TILE, PROBE),
    shape(2, PROBE, PROBE),
    shape(2, EXT, PROBE),
]
WORK = pltpu.VMEM((2, PAIRS, 2, 256, 256), BF16)
SCRATCH = pltpu.VMEM((2, EXT, EXT), F32)
GRADS = [pltpu.VMEM((2, POS, TALL, PROBE), F32)] + [pltpu.VMEM((EXT, EXT), F32)] * 2


def run(body, operands, outs, scratch, stages, specs=None):
    specs = specs or {}
    flops = stages * POS * PROBE * 256 * 256 * 2 * 3
    moved = sum(math.prod(o.shape) * 4 for o in operands) + sum(math.prod(o.shape) * 4 for o in outs)
    in_specs = [pl.BlockSpec(memory_space=pltpu.SMEM)]
    in_specs += [specs.get(n, None) or whole(o) for n, o in enumerate(operands) if n > 0]
    return pl.pallas_call(
        body,
        grid=(1,),
        in_specs=in_specs,
        out_specs=[whole(o) for o in outs],
        out_shape=outs,
        scratch_shapes=scratch,
        cost_estimate=pl.CostEstimate(flops=flops, bytes_accessed=moved, transcendentals=0),
        compiler_params=pltpu.CompilerParams(vmem_limit_bytes=14 * 2**20),
    )(*operands)


def field_specs(start, layer, fill):
    if fill is not fill_first:
        return {}
    specs = {start: tile_of(layer)}
    if layer > 0:
        specs[start + 2] = pl.BlockSpec((2, None, TILE, PROBE), lambda i: (0, layer - 1, 0, 0))
    return specs


def forward(offsets, tables, phase, wave, field, layer, fill):
    first = wave is None
    operands = [offsets, tables, phase] + ([] if first else [wave])
    specs = field_specs(len(operands), layer, fill)
    body = functools.partial(forward_kernel, fill, len(field), first)
    return run(body, operands + field, [shape(*STACK)] * 2, [SCRATCH, WORK], 4, specs)


def turn(offsets, tables, intensity, wave, field, layer, fill):
    operands = [offsets, tables, intensity, wave]
    specs = field_specs(len(operands), layer, fill)
    body = functools.partial(turn_kernel, fill, len(field))
    scratch = [SCRATCH, pltpu.VMEM(STACK, F32), WORK, *GRADS]
    return run(body, operands + field, [*GRADIENT, shape(*STACK)], scratch, 4, specs)


def backward(offsets, tables, phase, back, wave, windows):
    first = wave is None
    operands = [offsets, tables, phase, back] + ([] if first else [wave, windows])
    outs = [*GRADIENT] if first else [*GRADIENT, shape(*STACK)]
    return run(functools.partial(backward_kernel, first), operands, outs, [WORK, *GRADS], 4)


def shifted(block, axis, distance):
    size = lax.axis_size(axis)
    return lax.ppermute(block, axis, [((i - distance) % size, i) for i in range(size)])


def swapped(block, odd):
    size = lax.axis_size("row")
    route = []
    for i in range(odd, size + odd, 2):
        route += [(i % size, (i + 1) % size), ((i + 1) % size, i % size)]
    return lax.ppermute(block, "row", sorted(route))


def plain(body, outs, operands, specs=None, aliases=None, out_specs=None):
    specs = specs or {}
    moved = sum(math.prod(o.shape) * 4 for o in outs)
    return pl.pallas_call(
        body,
        grid=(1,),
        in_specs=[specs.get(n, None) or whole(o) for n, o in enumerate(operands)],
        out_specs=out_specs or [whole(o) for o in outs],
        out_shape=outs,
        input_output_aliases=aliases or {},
        cost_estimate=pl.CostEstimate(flops=0, bytes_accessed=2 * moved, transcendentals=0),
        compiler_params=pltpu.CompilerParams(vmem_limit_bytes=8 * 2**20),
    )(*operands)


SIDE = shape(2, EXT, PROBE)


def pack_kernel(jobs, tile, *refs):
    outs, sems = refs[:-1], refs[-1]
    copies = [
        pltpu.make_async_copy(tile.at[:, layer, rows, cols], out, sems.at[n])
        for n, ((layer, rows, cols), out) in enumerate(zip(jobs, outs))
    ]
    for copy in copies:
        copy.start()
    for copy in copies:
        copy.wait()


def pack(object_field, jobs, outs):
    return pl.pallas_call(
        functools.partial(pack_kernel, jobs),
        in_specs=[pl.BlockSpec(memory_space=pltpu.HBM)],
        out_specs=[pl.BlockSpec(memory_space=pltpu.VMEM)] * len(outs),
        out_shape=outs,
        scratch_shapes=[pltpu.SemaphoreType.DMA((len(outs),))],
        name="pack",
        cost_estimate=pl.CostEstimate(flops=0, bytes_accessed=4 * 2**18, transcendentals=0),
        compiler_params=pltpu.CompilerParams(vmem_limit_bytes=4 * 2**20),
    )(object_field)


def prepare_kernel(probe, propagator, tables, phase, copied):
    phase[:2] = probe[...]
    phase[2] = jnp.cos(propagator[...])
    phase[3] = jnp.sin(propagator[...])
    copied[...] = tables[...]


def prepare(probe, propagator):
    tables = jnp.asarray(dft_tables())
    outs = [shape(4, PROBE, PROBE), jax.ShapeDtypeStruct(tables.shape, BF16)]
    return plain(prepare_kernel, outs, [probe, propagator, tables])


def sums_kernel(wide, left, middle, low, right, from_left, *refs):
    h, t = PROBE, TILE
    from_right = refs[0] if wide else None
    even_out, odd_out = refs[-2:]

    def fill(down, up):
        down[:, :, :h] = left[:, t:] + from_left[:, t:]
        up[:, :, :h] = left[:, :h] + from_left[:, :h]
        down[:, :, h:t] = low[...]
        up[:, :, h:t] = middle[:, :h]
        if wide:
            down[:, :, t:] = right[:, t:] + from_right[:, t:]
            up[:, :, t:] = right[:, :h] + from_right[:, :h]

    parity = lax.axis_index("row") & 1

    @pl.when(parity == 0)
    def _():
        fill(even_out, odd_out)

    @pl.when(parity == 1)
    def _():
        fill(odd_out, even_out)


def sums(grad, from_left, from_right):
    wide = from_right is not None
    operands = [*grad, from_left] + ([from_right] if wide else [])
    outs = [shape(2, PROBE, EXT if wide else TILE)] * 2
    return plain(functools.partial(sums_kernel, wide), outs, operands)


def update_kernel(wide, *refs):
    h, t = PROBE, TILE
    if wide:
        tile, low, side, corner, left, middle, bottom, right, from_left, from_right, even, odd = refs[:12]
        new_l, new_m, new_r = refs[12:]
    else:
        tile, low, left, middle, bottom, from_left, even, odd, new_l, new_m = refs
    top, mid, end = slice(0, h), slice(h, t), slice(t, t + h)
    first, second, third = slice(0, h), slice(h, t), slice(t, t + h)

    swap = (lax.axis_index("row") & 1) == 1

    class Chosen:
        def __init__(self, first, second):
            self.first, self.second = first, second

        def __getitem__(self, where):
            return jnp.where(swap, self.second[where], self.first[where])

    def fill(above, below):
        new_l[:, top] = tile[:, 0, top, first] - STEP * (left[:, top] + from_left[:, top] + above[:, :, first])
        new_l[:, mid] = tile[:, 0, mid, first] - STEP * (left[:, mid] + from_left[:, mid])
        new_l[:, end] = low[:, :, first] - STEP * (left[:, end] + from_left[:, end] + below[:, :, first])
        new_m[:, top] = tile[:, 0, top, second] - STEP * (middle[:, top] + above[:, :, second])
        new_m[:, mid] = tile[:, 0, mid, second] - STEP * middle[:, mid]
        new_m[:, end] = low[:, :, second] - STEP * (bottom[...] + below[:, :, second])
        if wide:
            new_r[:, top] = side[:, top] - STEP * (right[:, top] + from_right[:, top] + above[:, :, third])
            new_r[:, mid] = side[:, mid] - STEP * (right[:, mid] + from_right[:, mid])
            new_r[:, end] = corner[...] - STEP * (right[:, end] + from_right[:, end] + below[:, :, third])

    fill(Chosen(odd, even), Chosen(even, odd))


def update(layer, field, grad, from_left, from_right, even, odd):
    tile, low, side, corner = field
    if from_right is None:
        operands = [tile, low, *grad[:3], from_left, even, odd]
        specs = {0: tile_of(layer)}
        return plain(functools.partial(update_kernel, False), [SIDE] * 2, operands, specs)
    operands = [tile, low, side, corner, *grad, from_left, from_right, even, odd]
    specs = field_specs(0, layer, fill_first)
    return plain(functools.partial(update_kernel, True), [SIDE] * 3, operands, specs)


def spill_kernel(left, from_left, down):
    down[...] = left[:, TILE:] + from_left[:, TILE:]


def last_kernel(n_alias, *refs):
    old_l, old_m, left, middle, from_left, above_l, above_m = refs[:7]
    out = refs[7 + n_alias]
    h, t = PROBE, TILE
    out[:, 0, :h, :h] = old_l[:, :h] - STEP * (left[:, :h] + from_left[:, :h] + above_l[...])
    out[:, 0, h:, :h] = old_l[:, h:t] - STEP * (left[:, h:t] + from_left[:, h:t])
    out[:, 0, :h, h:] = old_m[:, :h] - STEP * (middle[:, :h] + above_m[...])
    out[:, 0, h:, h:] = old_m[:, h:t] - STEP * middle[:, h:t]


def last(result, layer, field, grad, from_left, above_l, above_m):
    operands = [field[0], field[1], grad[0], grad[1], from_left, above_l, above_m]
    specs, aliases = {}, {}
    if result is not None:
        operands.append(result)
        specs, aliases = {7: pl.BlockSpec(memory_space=pl.ANY)}, {7: 0}
    return plain(
        functools.partial(last_kernel, len(operands) - 7),
        [shape(2, SLICES, TILE, TILE)],
        operands,
        specs,
        aliases,
        [tile_of(layer)],
    )[0]


def on_device(object_field, probe, propagator, measured, offsets):
    h, t = PROBE, TILE
    phase, tables = prepare(probe, propagator)
    offsets = jnp.swapaxes(offsets, 2, 3).reshape(2, POS)
    intensity = measured.reshape(POS, h, h)

    top, all_rows, left, all_cols = pl.ds(0, h), pl.ds(0, t), pl.ds(0, h), pl.ds(0, t)
    rows_shape = shape(2, h, t)
    rows0, cols0 = pack(
        object_field, [(0, top, all_cols), (0, all_rows, left)], [rows_shape, shape(2, t, h)]
    )
    rows1, rows2, cols12 = pack(
        object_field,
        [(1, top, all_cols), (2, top, all_cols), (pl.ds(1, 2), all_rows, left)],
        [rows_shape, rows_shape, shape(2, 2, t, h)],
    )
    right0 = shifted(cols0, "col", -1)
    right12 = shifted(cols12, "col", -1)
    fields = []
    for layer, rows in enumerate((rows0, rows1, rows2)):
        low = shifted(rows, "row", -1)
        corner = shifted(low[:, :, :h], "col", -1)
        fields.append([object_field, low, right0 if layer == 0 else right12, corner])

    def gradients(fields, fill):
        _, wave1 = forward(offsets, tables, phase, None, fields[0], 0, fill)
        win1, wave2 = forward(offsets, tables, phase, wave1, fields[1], 1, fill)
        *grad2, back = turn(offsets, tables, intensity, wave2, fields[2], 2, fill)
        *grad1, back = backward(offsets, tables, phase, back, wave1, win1)
        grad0 = backward(offsets, tables, phase, back, None, None)
        return [grad0, grad1, grad2]

    grads = gradients(fields, fill_first)
    renewed = [None] * SLICES
    for layer in (2, 0, 1):
        grad, from_right = grads[layer], None
        from_left = shifted(grad[3], "col", 1)
        if layer == 1:
            from_right = shifted(grad[0], "col", -1)
        for_even, for_odd = sums(grad, from_left, from_right)
        even = swapped(for_even, 0)
        odd = swapped(for_odd, 1)
        new = update(layer, fields[layer], grad, from_left, from_right, even, odd)
        if layer != 1:
            new = [*new, shifted(new[0], "col", -1)]
        renewed[layer] = list(new)
    grads = gradients(renewed, fill_next)
    result = None
    for layer in (2, 1, 0):
        grad = grads[layer]
        from_left = shifted(grad[3], "col", 1)
        above_m = shifted(grad[2], "row", 1)
        down = plain(spill_kernel, [shape(2, h, h)], [grad[0], from_left])[0]
        above_l = shifted(down, "row", 1)
        result = last(result, layer, renewed[layer], grad, from_left, above_l, above_m)
    return result


def solution(mesh):
    placed = (
        P(None, None, "row", "col"),
        P(),
        P(),
        P("row", "col", None, None, None),
        P("row", "col", None, None),
    )
    return jax.shard_map(
        on_device,
        mesh=mesh,
        in_specs=placed,
        out_specs=P(None, None, "row", "col"),
        check_vma=False,
    )
```

```python
import functools
import math

import jax
import jax.numpy as jnp
import numpy as np
from jax import lax
from jax.experimental import pallas as pl
from jax.experimental.pallas import tpu as pltpu
from jax.sharding import PartitionSpec as P


PROBE = 128
SLICES = 3
POS = 6
TILE = 256
EXT = TILE + PROBE
SUB = 8
STEP = 0.05
F32 = jnp.float32
BF16 = jnp.bfloat16


def dft_tables():
    index = np.arange(PROBE)
    angle = (index[:, None] * index[None, :] % PROBE) * (-2.0 * math.pi / PROBE)
    cosines, sines = np.cos(angle) / math.sqrt(PROBE), np.sin(angle) / math.sqrt(PROBE)
    right = np.block([[cosines, sines], [-sines, cosines]]).astype(np.float32)
    high = right.astype(BF16)
    return np.stack([high, (right - high.astype(np.float32)).astype(BF16)])


def split(value):
    high = value.astype(BF16)
    return high, (value - high.astype(F32)).astype(BF16)


def dot(a, b):
    return jnp.dot(a, b, preferred_element_type=F32)


def times_right(block, table):
    high, low = block
    wide, fine = table
    return dot(jnp.concatenate([high, low, high], axis=1), jnp.concatenate([wide, wide, fine], axis=0))


def times_left(block, table):
    high, low = block
    wide, fine = table
    return dot(jnp.concatenate([wide, wide, fine], axis=1), jnp.concatenate([high, low, high], axis=0))


def side_to_stack(block):
    h = PROBE
    top = jnp.concatenate([block[:h, :h], block[h:, :h]], axis=1)
    low = jnp.concatenate([block[:h, h:], block[h:, h:]], axis=1)
    return jnp.concatenate([top, low], axis=0)


def times_phase(block, phase_real, phase_imag):
    h = PROBE
    re, im = block[:h], block[h:]
    pr = jnp.concatenate([phase_real, phase_real], axis=1)
    pi = jnp.concatenate([phase_imag, phase_imag], axis=1)
    return jnp.concatenate([re * pr - im * pi, re * pi + im * pr], axis=0)


def keep(work, n, slot, block):
    work[slot, n, 0], work[slot, n, 1] = split(block)


def kept(work, n, slot):
    return work[slot, n, 0], work[slot, n, 1]


PAIRS = POS // 2


def propagate(work, right, left, phase_real, phase_imag, finish):
    for n in range(PAIRS):
        keep(work, n, 1, side_to_stack(times_right(kept(work, n, 0), right)))
    for n in range(PAIRS):
        keep(work, n, 0, times_phase(times_left(kept(work, n, 1), left), phase_real, phase_imag))
    for n in range(PAIRS):
        keep(work, n, 1, side_to_stack(times_left(kept(work, n, 0), right)))
    for n in range(PAIRS):
        finish(n, times_right(kept(work, n, 1), left))


def tables_of(table_ref):
    right = (table_ref[0], table_ref[1])
    left = (table_ref[2], table_ref[3])
    return right, left


def pair_of(ref, p):
    top = jnp.concatenate([ref[0, p], ref[1, p]], axis=1)
    low = jnp.concatenate([ref[0, p + 1], ref[1, p + 1]], axis=1)
    return jnp.concatenate([top, low], axis=0)


def put_pair(ref, p, block):
    h = PROBE
    ref[0, p] = block[:h, :h]
    ref[1, p] = block[:h, h:]
    ref[0, p + 1] = block[h:, :h]
    ref[1, p + 1] = block[h:, h:]


def place(offset_ref, p):
    row, col = offset_ref[0, p], offset_ref[1, p]
    over = lax.rem(row, SUB)
    base = jnp.where(col >= PROBE, PROBE, 0)
    return pl.multiple_of(row - over, SUB), over, pl.multiple_of(base, PROBE), col - base


TALL = PROBE + SUB


def lanes(rows):
    return lax.broadcasted_iota(jnp.int32, (rows, PROBE), 1)


def take_window(ext, offset_ref, p, part):
    row, over, base, shift = place(offset_ref, p)
    after = pl.multiple_of(base + PROBE, PROBE)
    first = ext[part, pl.ds(row, TALL), pl.ds(base, PROBE)]
    second = ext[part, pl.ds(row, TALL), pl.ds(after, PROBE)]
    block = jnp.where(lanes(TALL) >= shift, first, second)
    block = pltpu.roll(block, jnp.where(shift == 0, 0, PROBE - shift), 1)
    return pltpu.roll(block, jnp.where(over == 0, 0, TALL - over), 0)[:PROBE]


def turn_window(offset_ref, p, value):
    _, over, _, shift = place(offset_ref, p)
    block = jnp.concatenate([value, jnp.zeros((SUB, PROBE), F32)], axis=0)
    return pltpu.roll(pltpu.roll(block, over, 0), shift, 1)


def add_windows(grads, offset_ref, turned):
    for p in range(POS):
        row, _, base, shift = place(offset_ref, p)
        after = pl.multiple_of(base + PROBE, PROBE)
        here = lanes(TALL) >= shift
        for part in range(2):
            block = turned[part, p]
            where = (pl.ds(row, TALL), pl.ds(base, PROBE))
            grads[part][where] = grads[part][where] + jnp.where(here, block, 0.0)
            where = (pl.ds(row, TALL), pl.ds(after, PROBE))
            grads[part][where] = grads[part][where] + jnp.where(here, 0.0, block)


def times(ar, ai, br, bi):
    return ar * br - ai * bi, ar * bi + ai * br


def times_conj(ar, ai, br, bi):
    return ar * br + ai * bi, ar * bi - ai * br


def fill_first(ext, refs):
    tile, low, right, corner = refs
    t = TILE
    ext[:, :t, :t] = tile[:, 0]
    ext[:, t:, :t] = low[...]
    ext[:, :t, t:] = right[...]
    ext[:, t:, t:] = corner[...]


def fill_next(ext, refs):
    left, middle, right = refs
    t, h = TILE, PROBE
    ext[:, :, :h] = left[...]
    ext[:, :, h:t] = middle[...]
    ext[:, :, t:] = right[...]


def forward_kernel(fill, n_field, first, *refs):
    offset_ref, table_ref, phase_ref = refs[:3]
    wave = None if first else refs[3]
    field = refs[4 - first : 4 - first + n_field]
    windows, out, ext, work = refs[4 - first + n_field :]
    fill(ext, field)
    right, left = tables_of(table_ref)
    for n in range(PAIRS):
        rows = []
        for q in (2 * n, 2 * n + 1):
            tr = take_window(ext, offset_ref, q, 0)
            ti = take_window(ext, offset_ref, q, 1)
            windows[0, q] = tr
            windows[1, q] = ti
            if first:
                wr, wi = phase_ref[0], phase_ref[1]
            else:
                wr, wi = wave[0, q], wave[1, q]
            rows.append(jnp.concatenate(times(wr, wi, tr, ti), axis=1))
        keep(work, n, 0, jnp.concatenate(rows, axis=0))

    def finish(n, block):
        put_pair(out, 2 * n, block)

    propagate(work, right, left, phase_ref[2], phase_ref[3], finish)


def write_gradient(grads, outs):
    left, middle, low, right = outs
    h, t = PROBE, TILE
    for part in range(2):
        left[part] = grads[part][:, :h]
        middle[part] = grads[part][:t, h:t]
        low[part] = grads[part][t:, h:t]
        right[part] = grads[part][:, t:]


def turn_kernel(fill, n_field, *refs):
    offset_ref, table_ref, intensity, wave = refs[:4]
    field = refs[4 : 4 + n_field]
    outs = refs[4 + n_field : 8 + n_field]
    back, ext, windows, work, turned, *grads = refs[8 + n_field :]
    fill(ext, field)
    for part in grads:
        part[...] = jnp.zeros_like(part)
    right, left = tables_of(table_ref)
    h = PROBE
    for n in range(PAIRS):
        rows = []
        for q in (2 * n, 2 * n + 1):
            tr = take_window(ext, offset_ref, q, 0)
            ti = take_window(ext, offset_ref, q, 1)
            windows[0, q] = tr
            windows[1, q] = ti
            rows.append(jnp.concatenate(times(wave[0, q], wave[1, q], tr, ti), axis=1))
        keep(work, n, 0, jnp.concatenate(rows, axis=0))
    for n in range(PAIRS):
        keep(work, n, 1, side_to_stack(times_right(kept(work, n, 0), right)))
    for n in range(PAIRS):
        block = times_left(kept(work, n, 1), left)
        re, im = block[:h], block[h:]
        target = jnp.concatenate([intensity[2 * n], intensity[2 * n + 1]], axis=1)
        weight = 4.0 * (re * re + im * im - target)
        keep(work, n, 0, jnp.concatenate([re * weight, im * weight], axis=0))
    for n in range(PAIRS):
        keep(work, n, 1, side_to_stack(times_left(kept(work, n, 0), right)))
    for n in range(PAIRS):
        block = times_right(kept(work, n, 1), left)
        for i in range(2):
            q = 2 * n + i
            gr, gi = block[i * h : (i + 1) * h, :h], block[i * h : (i + 1) * h, h:]
            br, bi = times_conj(windows[0, q], windows[1, q], gr, gi)
            back[0, q] = br
            back[1, q] = bi
            dr, di = times_conj(wave[0, q], wave[1, q], gr, gi)
            turned[0, q] = turn_window(offset_ref, q, dr)
            turned[1, q] = turn_window(offset_ref, q, di)
    add_windows(grads, offset_ref, turned)
    write_gradient(grads, outs)


def backward_kernel(first, *refs):
    if first:
        offset_ref, table_ref, phase_ref, back_in = refs[:4]
        outs = refs[4:8]
    else:
        offset_ref, table_ref, phase_ref, back_in, wave, windows = refs[:6]
        outs, back = refs[6:10], refs[10]
    work, turned, *grads = refs[-4:]
    for part in grads:
        part[...] = jnp.zeros_like(part)
    right, left = tables_of(table_ref)
    h = PROBE
    for n in range(PAIRS):
        keep(work, n, 0, pair_of(back_in, 2 * n))

    def finish(n, block):
        for i in range(2):
            q = 2 * n + i
            gr, gi = block[i * h : (i + 1) * h, :h], block[i * h : (i + 1) * h, h:]
            if first:
                dr, di = times_conj(phase_ref[0], phase_ref[1], gr, gi)
            else:
                br, bi = times_conj(windows[0, q], windows[1, q], gr, gi)
                back[0, q] = br
                back[1, q] = bi
                dr, di = times_conj(wave[0, q], wave[1, q], gr, gi)
            turned[0, q] = turn_window(offset_ref, q, dr)
            turned[1, q] = turn_window(offset_ref, q, di)

    propagate(work, right, left, phase_ref[2], -phase_ref[3], finish)
    add_windows(grads, offset_ref, turned)
    write_gradient(grads, outs)


def whole(array):
    rank = len(array.shape)
    return pl.BlockSpec(array.shape, lambda i: (0,) * rank)


def tile_of(layer):
    return pl.BlockSpec((2, 1, TILE, TILE), lambda i: (0, layer, 0, 0))


def shape(*dims):
    return jax.ShapeDtypeStruct(dims, F32)


STACK = (2, POS, PROBE, PROBE)
GRADIENT = [
    shape(2, EXT, PROBE),
    shape(2, TILE, PROBE),
    shape(2, PROBE, PROBE),
    shape(2, EXT, PROBE),
]
WORK = pltpu.VMEM((2, PAIRS, 2, 256, 256), BF16)
SCRATCH = pltpu.VMEM((2, EXT, EXT), F32)
GRADS = [pltpu.VMEM((2, POS, TALL, PROBE), F32)] + [pltpu.VMEM((EXT, EXT), F32)] * 2


def run(body, operands, outs, scratch, stages, specs=None):
    specs = specs or {}
    flops = stages * POS * PROBE * 256 * 256 * 2 * 3
    moved = sum(math.prod(o.shape) * 4 for o in operands) + sum(math.prod(o.shape) * 4 for o in outs)
    in_specs = [pl.BlockSpec(memory_space=pltpu.SMEM)]
    in_specs += [specs.get(n, None) or whole(o) for n, o in enumerate(operands) if n > 0]
    return pl.pallas_call(
        body,
        grid=(1,),
        in_specs=in_specs,
        out_specs=[whole(o) for o in outs],
        out_shape=outs,
        scratch_shapes=scratch,
        cost_estimate=pl.CostEstimate(flops=flops, bytes_accessed=moved, transcendentals=0),
        compiler_params=pltpu.CompilerParams(vmem_limit_bytes=14 * 2**20),
    )(*operands)


def field_specs(start, layer, fill):
    if fill is not fill_first:
        return {}
    specs = {start: tile_of(layer)}
    if layer > 0:
        specs[start + 2] = pl.BlockSpec((2, None, TILE, PROBE), lambda i: (0, layer - 1, 0, 0))
    return specs


def forward(offsets, tables, phase, wave, field, layer, fill):
    first = wave is None
    operands = [offsets, tables, phase] + ([] if first else [wave])
    specs = field_specs(len(operands), layer, fill)
    body = functools.partial(forward_kernel, fill, len(field), first)
    return run(body, operands + field, [shape(*STACK)] * 2, [SCRATCH, WORK], 4, specs)


def turn(offsets, tables, intensity, wave, field, layer, fill):
    operands = [offsets, tables, intensity, wave]
    specs = field_specs(len(operands), layer, fill)
    body = functools.partial(turn_kernel, fill, len(field))
    scratch = [SCRATCH, pltpu.VMEM(STACK, F32), WORK, *GRADS]
    return run(body, operands + field, [*GRADIENT, shape(*STACK)], scratch, 4, specs)


def backward(offsets, tables, phase, back, wave, windows):
    first = wave is None
    operands = [offsets, tables, phase, back] + ([] if first else [wave, windows])
    outs = [*GRADIENT] if first else [*GRADIENT, shape(*STACK)]
    return run(functools.partial(backward_kernel, first), operands, outs, [WORK, *GRADS], 4)


def shifted(block, axis, distance):
    size = lax.axis_size(axis)
    return lax.ppermute(block, axis, [((i - distance) % size, i) for i in range(size)])


def swapped(block, odd):
    size = lax.axis_size("row")
    route = []
    for i in range(odd, size + odd, 2):
        route += [(i % size, (i + 1) % size), ((i + 1) % size, i % size)]
    return lax.ppermute(block, "row", sorted(route))


def plain(body, outs, operands, specs=None, aliases=None, out_specs=None):
    specs = specs or {}
    moved = sum(math.prod(o.shape) * 4 for o in outs)
    return pl.pallas_call(
        body,
        grid=(1,),
        in_specs=[specs.get(n, None) or whole(o) for n, o in enumerate(operands)],
        out_specs=out_specs or [whole(o) for o in outs],
        out_shape=outs,
        input_output_aliases=aliases or {},
        cost_estimate=pl.CostEstimate(flops=0, bytes_accessed=2 * moved, transcendentals=0),
        compiler_params=pltpu.CompilerParams(vmem_limit_bytes=8 * 2**20),
    )(*operands)


SIDE = shape(2, EXT, PROBE)


def pack_kernel(jobs, tile, *refs):
    outs, sems = refs[:-1], refs[-1]
    copies = [
        pltpu.make_async_copy(tile.at[:, layer, rows, cols], out, sems.at[n])
        for n, ((layer, rows, cols), out) in enumerate(zip(jobs, outs))
    ]
    for copy in copies:
        copy.start()
    for copy in copies:
        copy.wait()


def pack(object_field, jobs, outs):
    return pl.pallas_call(
        functools.partial(pack_kernel, jobs),
        in_specs=[pl.BlockSpec(memory_space=pltpu.HBM)],
        out_specs=[pl.BlockSpec(memory_space=pltpu.VMEM)] * len(outs),
        out_shape=outs,
        scratch_shapes=[pltpu.SemaphoreType.DMA((len(outs),))],
        name="pack",
        cost_estimate=pl.CostEstimate(flops=0, bytes_accessed=4 * 2**18, transcendentals=0),
        compiler_params=pltpu.CompilerParams(vmem_limit_bytes=4 * 2**20),
    )(object_field)


def prepare_kernel(probe, propagator, tables, phase, copied):
    phase[:2] = probe[...]
    phase[2] = jnp.cos(propagator[...])
    phase[3] = jnp.sin(propagator[...])
    h = PROBE
    copied[:2] = tables[...]
    copied[2:, :h, :h] = tables[:, :h, :h]
    copied[2:, :h, h:] = tables[:, h:, :h]
    copied[2:, h:, :h] = tables[:, :h, h:]
    copied[2:, h:, h:] = tables[:, h:, h:]


def prepare(probe, propagator):
    tables = jnp.asarray(dft_tables())
    outs = [shape(4, PROBE, PROBE), jax.ShapeDtypeStruct((4, 2 * PROBE, 2 * PROBE), BF16)]
    return plain(prepare_kernel, outs, [probe, propagator, tables])


def sums_kernel(summed, left, middle, low, right, *refs):
    h, t = PROBE, TILE
    even_out, odd_out = refs[-2:]
    from_left, from_right = refs[:2] if summed else (None, None)

    def total(own, other, rows):
        return own[:, rows] + other[:, rows] if summed else own[:, rows]

    def fill(down, up):
        down[:, :, :h] = total(left, from_left, slice(t, t + h))
        up[:, :, :h] = total(left, from_left, slice(0, h))
        down[:, :, h:t] = low[...]
        up[:, :, h:t] = middle[:, :h]
        down[:, :, t:] = total(right, from_right, slice(t, t + h))
        up[:, :, t:] = total(right, from_right, slice(0, h))

    parity = lax.axis_index("row") & 1

    @pl.when(parity == 0)
    def _():
        fill(even_out, odd_out)

    @pl.when(parity == 1)
    def _():
        fill(odd_out, even_out)


def sums(grad, columns):
    body = functools.partial(sums_kernel, bool(columns))
    return plain(body, [shape(2, PROBE, EXT)] * 2, [*grad, *columns])


class Chosen:
    def __init__(self, for_even, for_odd):
        self.pair = for_even, for_odd

    def __getitem__(self, where):
        odd_row = (lax.axis_index("row") & 1) == 1
        return jnp.where(odd_row, self.pair[1][where], self.pair[0][where])


def edges_kernel(left, right, even, odd, west, east):
    h, t = PROBE, TILE
    above, below = Chosen(odd, even), Chosen(even, odd)
    for out, own, cols in ((west, left, slice(0, h)), (east, right, slice(t, t + h))):
        out[:, :h] = own[:, :h] + above[:, :, cols]
        out[:, h:t] = own[:, h:t]
        out[:, t:] = own[:, t:] + below[:, :, cols]


def update_kernel(rows_first, tile, low, side, corner, left, middle, bottom, right, *refs):
    from_left, from_right, even, odd, new_l, new_m, new_r = refs
    h, t = PROBE, TILE
    above, below = Chosen(odd, even), Chosen(even, odd)
    first, second, third = slice(0, h), slice(h, t), slice(t, t + h)
    top, mid, end = first, second, third

    def side_sum(own, other, rows, cols):
        total = own[:, rows] + other[:, rows]
        if rows_first or rows is mid:
            return total
        return total + (above if rows is top else below)[:, :, cols]

    new_l[:, top] = tile[:, 0, top, first] - STEP * side_sum(left, from_left, top, first)
    new_l[:, mid] = tile[:, 0, mid, first] - STEP * side_sum(left, from_left, mid, first)
    new_l[:, end] = low[:, :, first] - STEP * side_sum(left, from_left, end, first)
    new_m[:, top] = tile[:, 0, top, second] - STEP * (middle[:, top] + above[:, :, second])
    new_m[:, mid] = tile[:, 0, mid, second] - STEP * middle[:, mid]
    new_m[:, end] = low[:, :, second] - STEP * (bottom[...] + below[:, :, second])
    new_r[:, top] = side[:, top] - STEP * side_sum(right, from_right, top, third)
    new_r[:, mid] = side[:, mid] - STEP * side_sum(right, from_right, mid, third)
    new_r[:, end] = corner[...] - STEP * side_sum(right, from_right, end, third)


def update(layer, field, grad, columns, even, odd, rows_first):
    operands = [*field, *grad, *columns, even, odd]
    specs = field_specs(0, layer, fill_first)
    body = functools.partial(update_kernel, rows_first)
    return plain(body, [SIDE] * 3, operands, specs)


def spill_kernel(left, from_left, down):
    rows = from_left.shape[1]
    down[...] = left[:, TILE:] + from_left[:, rows - PROBE :]


def last_kernel(n_alias, *refs):
    old_l, old_m, left, middle, from_left, above_l, above_m = refs[:7]
    out = refs[7 + n_alias]
    h, t = PROBE, TILE
    out[:, 0, :h, :h] = old_l[:, :h] - STEP * (left[:, :h] + from_left[:, :h] + above_l[...])
    out[:, 0, h:, :h] = old_l[:, h:t] - STEP * (left[:, h:t] + from_left[:, h:t])
    out[:, 0, :h, h:] = old_m[:, :h] - STEP * (middle[:, :h] + above_m[...])
    out[:, 0, h:, h:] = old_m[:, h:t] - STEP * middle[:, h:t]


def last(result, layer, field, grad, from_left, above_l, above_m):
    operands = [field[0], field[1], grad[0], grad[1], from_left, above_l, above_m]
    specs, aliases = {}, {}
    if result is not None:
        operands.append(result)
        specs, aliases = {7: pl.BlockSpec(memory_space=pl.ANY)}, {7: 0}
    return plain(
        functools.partial(last_kernel, len(operands) - 7),
        [shape(2, SLICES, TILE, TILE)],
        operands,
        specs,
        aliases,
        [tile_of(layer)],
    )[0]


def on_device(object_field, probe, propagator, measured, offsets):
    h, t = PROBE, TILE
    phase, tables = prepare(probe, propagator)
    offsets = jnp.swapaxes(offsets, 2, 3).reshape(2, POS)
    intensity = measured.reshape(POS, h, h)

    top, all_rows, left, all_cols = pl.ds(0, h), pl.ds(0, t), pl.ds(0, h), pl.ds(0, t)
    rows_shape = shape(2, h, t)
    rows0, cols0 = pack(
        object_field, [(0, top, all_cols), (0, all_rows, left)], [rows_shape, shape(2, t, h)]
    )
    rows1, rows2, cols12 = pack(
        object_field,
        [(1, top, all_cols), (2, top, all_cols), (pl.ds(1, 2), all_rows, left)],
        [rows_shape, rows_shape, shape(2, 2, t, h)],
    )
    right0 = shifted(cols0, "col", -1)
    right12 = shifted(cols12, "col", -1)
    fields = []
    for layer, rows in enumerate((rows0, rows1, rows2)):
        low = shifted(rows, "row", -1)
        corner = shifted(low[:, :, :h], "col", -1)
        fields.append([object_field, low, right0 if layer == 0 else right12, corner])

    def gradients(fields, fill):
        _, wave1 = forward(offsets, tables, phase, None, fields[0], 0, fill)
        win1, wave2 = forward(offsets, tables, phase, wave1, fields[1], 1, fill)
        *grad2, back = turn(offsets, tables, intensity, wave2, fields[2], 2, fill)
        *grad1, back = backward(offsets, tables, phase, back, wave1, win1)
        grad0 = backward(offsets, tables, phase, back, None, None)
        return [grad0, grad1, grad2]

    grads = gradients(fields, fill_first)
    renewed = [None] * SLICES

    def columns(west, east):
        from_left = shifted(east, "col", 1)
        from_right = shifted(west, "col", -1)
        return [from_left, from_right]

    for layer in (2, 0, 1):
        grad, rows_first = grads[layer], layer != 1
        moved = [] if rows_first else columns(grad[0], grad[3])
        for_even, for_odd = sums(grad, moved)
        even = swapped(for_even, 0)
        odd = swapped(for_odd, 1)
        if rows_first:
            west, east = plain(edges_kernel, [SIDE] * 2, [grad[0], grad[3], even, odd])
            moved = columns(west, east)
            grad = [west, grad[1], grad[2], east]
        renewed[layer] = list(update(layer, fields[layer], grad, moved, even, odd, rows_first))
    grads = gradients(renewed, fill_next)
    result = None
    for layer in (2, 1, 0):
        grad = grads[layer]
        from_left = from_left_low = shifted(grad[3] if layer else grad[3][:, t:], "col", 1)
        if layer == 0:
            from_left = shifted(grad[3][:, :t], "col", 1)
        above_m = shifted(grad[2], "row", 1)
        down = plain(spill_kernel, [shape(2, h, h)], [grad[0], from_left_low])[0]
        above_l = shifted(down, "row", 1)
        result = last(result, layer, renewed[layer], grad, from_left, above_l, above_m)
    return result


def solution(mesh):
    placed = (
        P(None, None, "row", "col"),
        P(),
        P(),
        P("row", "col", None, None, None),
        P("row", "col", None, None),
    )
    return jax.shard_map(
        on_device,
        mesh=mesh,
        in_specs=placed,
        out_specs=P(None, None, "row", "col"),
        check_vma=False,
    )
```

```python
import functools
import math

import jax
import jax.numpy as jnp
import numpy as np
from jax import lax
from jax.experimental import pallas as pl
from jax.experimental.pallas import tpu as pltpu
from jax.sharding import PartitionSpec as P


PROBE = 128
SLICES = 3
POS = 6
TILE = 256
EXT = TILE + PROBE
SUB = 8
STEP = 0.05
F32 = jnp.float32
BF16 = jnp.bfloat16


def dft_tables():
    index = np.arange(PROBE)
    angle = (index[:, None] * index[None, :] % PROBE) * (-2.0 * math.pi / PROBE)
    cosines, sines = np.cos(angle) / math.sqrt(PROBE), np.sin(angle) / math.sqrt(PROBE)
    right = np.block([[cosines, sines], [-sines, cosines]]).astype(np.float32)
    high = right.astype(BF16)
    return np.stack([high, (right - high.astype(np.float32)).astype(BF16)])


def split(value):
    high = value.astype(BF16)
    return high, (value - high.astype(F32)).astype(BF16)


def dot(a, b):
    return jnp.dot(a, b, preferred_element_type=F32)


def times_right(block, table):
    high, low = block
    wide, fine = table
    return dot(jnp.concatenate([high, low, high], axis=1), jnp.concatenate([wide, wide, fine], axis=0))


def times_left(block, table):
    high, low = block
    wide, fine = table
    return dot(jnp.concatenate([wide, wide, fine], axis=1), jnp.concatenate([high, low, high], axis=0))


def side_to_stack(block):
    h = PROBE
    top = jnp.concatenate([block[:h, :h], block[h:, :h]], axis=1)
    low = jnp.concatenate([block[:h, h:], block[h:, h:]], axis=1)
    return jnp.concatenate([top, low], axis=0)


def times_phase(block, phase_real, phase_imag):
    h = PROBE
    re, im = block[:h], block[h:]
    pr = jnp.concatenate([phase_real, phase_real], axis=1)
    pi = jnp.concatenate([phase_imag, phase_imag], axis=1)
    return jnp.concatenate([re * pr - im * pi, re * pi + im * pr], axis=0)


def keep(work, n, slot, block):
    work[slot, n, 0], work[slot, n, 1] = split(block)


def kept(work, n, slot):
    return work[slot, n, 0], work[slot, n, 1]


PAIRS = POS // 2


def propagate(work, right, left, phase_real, phase_imag, finish):
    for n in range(PAIRS):
        keep(work, n, 1, side_to_stack(times_right(kept(work, n, 0), right)))
    for n in range(PAIRS):
        keep(work, n, 0, times_phase(times_left(kept(work, n, 1), left), phase_real, phase_imag))
    for n in range(PAIRS):
        keep(work, n, 1, side_to_stack(times_left(kept(work, n, 0), right)))
    for n in range(PAIRS):
        finish(n, times_right(kept(work, n, 1), left))


def tables_of(table_ref):
    right = (table_ref[0], table_ref[1])
    left = (table_ref[2], table_ref[3])
    return right, left


def pair_of(ref, p):
    top = jnp.concatenate([ref[0, p], ref[1, p]], axis=1)
    low = jnp.concatenate([ref[0, p + 1], ref[1, p + 1]], axis=1)
    return jnp.concatenate([top, low], axis=0)


def put_pair(ref, p, block):
    h = PROBE
    ref[0, p] = block[:h, :h]
    ref[1, p] = block[:h, h:]
    ref[0, p + 1] = block[h:, :h]
    ref[1, p + 1] = block[h:, h:]


def place(offset_ref, p):
    row, col = offset_ref[0, p], offset_ref[1, p]
    over = lax.rem(row, SUB)
    base = jnp.where(col >= PROBE, PROBE, 0)
    return pl.multiple_of(row - over, SUB), over, pl.multiple_of(base, PROBE), col - base


TALL = PROBE + SUB


def lanes(rows):
    return lax.broadcasted_iota(jnp.int32, (rows, PROBE), 1)


def take_window(ext, offset_ref, p, part):
    row, over, base, shift = place(offset_ref, p)
    after = pl.multiple_of(base + PROBE, PROBE)
    first = ext[part, pl.ds(row, TALL), pl.ds(base, PROBE)]
    second = ext[part, pl.ds(row, TALL), pl.ds(after, PROBE)]
    block = jnp.where(lanes(TALL) >= shift, first, second)
    block = pltpu.roll(block, jnp.where(shift == 0, 0, PROBE - shift), 1)
    return pltpu.roll(block, jnp.where(over == 0, 0, TALL - over), 0)[:PROBE]


def turn_window(offset_ref, p, value):
    _, over, _, shift = place(offset_ref, p)
    block = jnp.concatenate([value, jnp.zeros((SUB, PROBE), F32)], axis=0)
    return pltpu.roll(pltpu.roll(block, over, 0), shift, 1)


def add_windows(grads, offset_ref, turned):
    for p in range(POS):
        row, _, base, shift = place(offset_ref, p)
        after = pl.multiple_of(base + PROBE, PROBE)
        here = lanes(TALL) >= shift
        for part in range(2):
            block = turned[part, p]
            where = (pl.ds(row, TALL), pl.ds(base, PROBE))
            grads[part][where] = grads[part][where] + jnp.where(here, block, 0.0)
            where = (pl.ds(row, TALL), pl.ds(after, PROBE))
            grads[part][where] = grads[part][where] + jnp.where(here, 0.0, block)


def times(ar, ai, br, bi):
    return ar * br - ai * bi, ar * bi + ai * br


def times_conj(ar, ai, br, bi):
    return ar * br + ai * bi, ar * bi - ai * br


def fill_first(ext, refs):
    tile, low, right, corner = refs
    t = TILE
    ext[:, :t, :t] = tile[:, 0]
    ext[:, t:, :t] = low[...]
    ext[:, :t, t:] = right[...]
    ext[:, t:, t:] = corner[...]


def fill_next(ext, refs):
    left, middle, right = refs
    t, h = TILE, PROBE
    ext[:, :, :h] = left[...]
    ext[:, :, h:t] = middle[...]
    ext[:, :, t:] = right[...]


def forward_kernel(fill, n_field, first, *refs):
    offset_ref, table_ref, phase_ref = refs[:3]
    wave = None if first else refs[3]
    field = refs[4 - first : 4 - first + n_field]
    windows, out, ext, work = refs[4 - first + n_field :]
    fill(ext, field)
    right, left = tables_of(table_ref)
    for n in range(PAIRS):
        rows = []
        for q in (2 * n, 2 * n + 1):
            tr = take_window(ext, offset_ref, q, 0)
            ti = take_window(ext, offset_ref, q, 1)
            windows[0, q] = tr
            windows[1, q] = ti
            if first:
                wr, wi = phase_ref[0], phase_ref[1]
            else:
                wr, wi = wave[0, q], wave[1, q]
            rows.append(jnp.concatenate(times(wr, wi, tr, ti), axis=1))
        keep(work, n, 0, jnp.concatenate(rows, axis=0))

    def finish(n, block):
        put_pair(out, 2 * n, block)

    propagate(work, right, left, phase_ref[2], phase_ref[3], finish)


def write_gradient(grads, outs):
    left, middle, low, right = outs
    h, t = PROBE, TILE
    for part in range(2):
        left[part] = grads[part][:, :h]
        middle[part] = grads[part][:t, h:t]
        low[part] = grads[part][t:, h:t]
        right[part] = grads[part][:, t:]


def turn_kernel(fill, n_field, *refs):
    offset_ref, table_ref, intensity, wave = refs[:4]
    field = refs[4 : 4 + n_field]
    outs = refs[4 + n_field : 8 + n_field]
    back, ext, windows, work, turned, *grads = refs[8 + n_field :]
    fill(ext, field)
    for part in grads:
        part[...] = jnp.zeros_like(part)
    right, left = tables_of(table_ref)
    h = PROBE
    for n in range(PAIRS):
        rows = []
        for q in (2 * n, 2 * n + 1):
            tr = take_window(ext, offset_ref, q, 0)
            ti = take_window(ext, offset_ref, q, 1)
            windows[0, q] = tr
            windows[1, q] = ti
            rows.append(jnp.concatenate(times(wave[0, q], wave[1, q], tr, ti), axis=1))
        keep(work, n, 0, jnp.concatenate(rows, axis=0))
    for n in range(PAIRS):
        keep(work, n, 1, side_to_stack(times_right(kept(work, n, 0), right)))
    for n in range(PAIRS):
        block = times_left(kept(work, n, 1), left)
        re, im = block[:h], block[h:]
        target = jnp.concatenate([intensity[2 * n], intensity[2 * n + 1]], axis=1)
        weight = 4.0 * (re * re + im * im - target)
        keep(work, n, 0, jnp.concatenate([re * weight, im * weight], axis=0))
    for n in range(PAIRS):
        keep(work, n, 1, side_to_stack(times_left(kept(work, n, 0), right)))
    for n in range(PAIRS):
        block = times_right(kept(work, n, 1), left)
        for i in range(2):
            q = 2 * n + i
            gr, gi = block[i * h : (i + 1) * h, :h], block[i * h : (i + 1) * h, h:]
            br, bi = times_conj(windows[0, q], windows[1, q], gr, gi)
            back[0, q] = br
            back[1, q] = bi
            dr, di = times_conj(wave[0, q], wave[1, q], gr, gi)
            turned[0, q] = turn_window(offset_ref, q, dr)
            turned[1, q] = turn_window(offset_ref, q, di)
    add_windows(grads, offset_ref, turned)
    write_gradient(grads, outs)


def backward_kernel(first, *refs):
    if first:
        offset_ref, table_ref, phase_ref, back_in = refs[:4]
        outs = refs[4:8]
    else:
        offset_ref, table_ref, phase_ref, back_in, wave, windows = refs[:6]
        outs, back = refs[6:10], refs[10]
    work, turned, *grads = refs[-4:]
    for part in grads:
        part[...] = jnp.zeros_like(part)
    right, left = tables_of(table_ref)
    h = PROBE
    for n in range(PAIRS):
        keep(work, n, 0, pair_of(back_in, 2 * n))

    def finish(n, block):
        for i in range(2):
            q = 2 * n + i
            gr, gi = block[i * h : (i + 1) * h, :h], block[i * h : (i + 1) * h, h:]
            if first:
                dr, di = times_conj(phase_ref[0], phase_ref[1], gr, gi)
            else:
                br, bi = times_conj(windows[0, q], windows[1, q], gr, gi)
                back[0, q] = br
                back[1, q] = bi
                dr, di = times_conj(wave[0, q], wave[1, q], gr, gi)
            turned[0, q] = turn_window(offset_ref, q, dr)
            turned[1, q] = turn_window(offset_ref, q, di)

    propagate(work, right, left, phase_ref[2], -phase_ref[3], finish)
    add_windows(grads, offset_ref, turned)
    write_gradient(grads, outs)


def whole(array):
    rank = len(array.shape)
    return pl.BlockSpec(array.shape, lambda i: (0,) * rank)


def tile_of(layer):
    return pl.BlockSpec((2, 1, TILE, TILE), lambda i: (0, layer, 0, 0))


def shape(*dims):
    return jax.ShapeDtypeStruct(dims, F32)


STACK = (2, POS, PROBE, PROBE)
GRADIENT = [
    shape(2, EXT, PROBE),
    shape(2, TILE, PROBE),
    shape(2, PROBE, PROBE),
    shape(2, EXT, PROBE),
]
WORK = pltpu.VMEM((2, PAIRS, 2, 256, 256), BF16)
SCRATCH = pltpu.VMEM((2, EXT, EXT), F32)
GRADS = [pltpu.VMEM((2, POS, TALL, PROBE), F32)] + [pltpu.VMEM((EXT, EXT), F32)] * 2


def run(body, operands, outs, scratch, stages, specs=None):
    specs = specs or {}
    flops = stages * POS * PROBE * 256 * 256 * 2 * 3
    moved = sum(math.prod(o.shape) * 4 for o in operands) + sum(math.prod(o.shape) * 4 for o in outs)
    in_specs = [pl.BlockSpec(memory_space=pltpu.SMEM)]
    in_specs += [specs.get(n, None) or whole(o) for n, o in enumerate(operands) if n > 0]
    return pl.pallas_call(
        body,
        grid=(1,),
        in_specs=in_specs,
        out_specs=[whole(o) for o in outs],
        out_shape=outs,
        scratch_shapes=scratch,
        cost_estimate=pl.CostEstimate(flops=flops, bytes_accessed=moved, transcendentals=0),
        compiler_params=pltpu.CompilerParams(vmem_limit_bytes=14 * 2**20),
    )(*operands)


def field_specs(start, layer, fill):
    if fill is not fill_first:
        return {}
    specs = {start: tile_of(layer)}
    if layer > 0:
        specs[start + 2] = pl.BlockSpec((2, None, TILE, PROBE), lambda i: (0, layer - 1, 0, 0))
    return specs


def forward(offsets, tables, phase, wave, field, layer, fill):
    first = wave is None
    operands = [offsets, tables, phase] + ([] if first else [wave])
    specs = field_specs(len(operands), layer, fill)
    body = functools.partial(forward_kernel, fill, len(field), first)
    return run(body, operands + field, [shape(*STACK)] * 2, [SCRATCH, WORK], 4, specs)


def turn(offsets, tables, intensity, wave, field, layer, fill):
    operands = [offsets, tables, intensity, wave]
    specs = field_specs(len(operands), layer, fill)
    body = functools.partial(turn_kernel, fill, len(field))
    scratch = [SCRATCH, pltpu.VMEM(STACK, F32), WORK, *GRADS]
    return run(body, operands + field, [*GRADIENT, shape(*STACK)], scratch, 4, specs)


def backward(offsets, tables, phase, back, wave, windows):
    first = wave is None
    operands = [offsets, tables, phase, back] + ([] if first else [wave, windows])
    outs = [*GRADIENT] if first else [*GRADIENT, shape(*STACK)]
    return run(functools.partial(backward_kernel, first), operands, outs, [WORK, *GRADS], 4)


def shifted(block, axis, distance):
    size = lax.axis_size(axis)
    return lax.ppermute(block, axis, [((i - distance) % size, i) for i in range(size)])


def swapped(block, odd):
    size = lax.axis_size("row")
    route = []
    for i in range(odd, size + odd, 2):
        route += [(i % size, (i + 1) % size), ((i + 1) % size, i % size)]
    return lax.ppermute(block, "row", sorted(route))


def plain(body, outs, operands, specs=None, aliases=None, out_specs=None):
    specs = specs or {}
    moved = sum(math.prod(o.shape) * 4 for o in outs)
    return pl.pallas_call(
        body,
        grid=(1,),
        in_specs=[specs.get(n, None) or whole(o) for n, o in enumerate(operands)],
        out_specs=out_specs or [whole(o) for o in outs],
        out_shape=outs,
        input_output_aliases=aliases or {},
        cost_estimate=pl.CostEstimate(flops=0, bytes_accessed=2 * moved, transcendentals=0),
        compiler_params=pltpu.CompilerParams(vmem_limit_bytes=8 * 2**20),
    )(*operands)


SIDE = shape(2, EXT, PROBE)


def pack_kernel(jobs, tile, *refs):
    outs, sems = refs[:-1], refs[-1]
    copies = [
        pltpu.make_async_copy(tile.at[:, layer, rows, cols], out, sems.at[n])
        for n, ((layer, rows, cols), out) in enumerate(zip(jobs, outs))
    ]
    for copy in copies:
        copy.start()
    for copy in copies:
        copy.wait()


def pack(object_field, jobs, outs):
    return pl.pallas_call(
        functools.partial(pack_kernel, jobs),
        in_specs=[pl.BlockSpec(memory_space=pltpu.HBM)],
        out_specs=[pl.BlockSpec(memory_space=pltpu.VMEM)] * len(outs),
        out_shape=outs,
        scratch_shapes=[pltpu.SemaphoreType.DMA((len(outs),))],
        name="pack",
        cost_estimate=pl.CostEstimate(flops=0, bytes_accessed=4 * 2**18, transcendentals=0),
        compiler_params=pltpu.CompilerParams(vmem_limit_bytes=4 * 2**20),
    )(object_field)


def prepare_kernel(probe, propagator, tables, phase, copied):
    phase[:2] = probe[...]
    phase[2] = jnp.cos(propagator[...])
    phase[3] = jnp.sin(propagator[...])
    h = PROBE
    copied[:2] = tables[...]
    copied[2:, :h, :h] = tables[:, :h, :h]
    copied[2:, :h, h:] = tables[:, h:, :h]
    copied[2:, h:, :h] = tables[:, :h, h:]
    copied[2:, h:, h:] = tables[:, h:, h:]


def prepare(probe, propagator):
    tables = jnp.asarray(dft_tables())
    outs = [shape(4, PROBE, PROBE), jax.ShapeDtypeStruct((4, 2 * PROBE, 2 * PROBE), BF16)]
    return plain(prepare_kernel, outs, [probe, propagator, tables])


def sums_kernel(summed, left, middle, low, right, *refs):
    h, t = PROBE, TILE
    even_out, odd_out = refs[-2:]
    from_left, from_right = refs[:2] if summed else (None, None)

    def total(own, other, rows):
        return own[:, rows] + other[:, rows] if summed else own[:, rows]

    def fill(down, up):
        down[:, :, :h] = total(left, from_left, slice(t, t + h))
        up[:, :, :h] = total(left, from_left, slice(0, h))
        down[:, :, h:t] = low[...]
        up[:, :, h:t] = middle[:, :h]
        down[:, :, t:] = total(right, from_right, slice(t, t + h))
        up[:, :, t:] = total(right, from_right, slice(0, h))

    parity = lax.axis_index("row") & 1

    @pl.when(parity == 0)
    def _():
        fill(even_out, odd_out)

    @pl.when(parity == 1)
    def _():
        fill(odd_out, even_out)


def sums(grad, columns):
    body = functools.partial(sums_kernel, bool(columns))
    return plain(body, [shape(2, PROBE, EXT)] * 2, [*grad, *columns])


class Chosen:
    def __init__(self, for_even, for_odd):
        self.pair = for_even, for_odd

    def __getitem__(self, where):
        odd_row = (lax.axis_index("row") & 1) == 1
        return jnp.where(odd_row, self.pair[1][where], self.pair[0][where])


def edges_kernel(left, right, even, odd, west, east):
    h, t = PROBE, TILE
    above, below = Chosen(odd, even), Chosen(even, odd)
    for out, own, cols in ((west, left, slice(0, h)), (east, right, slice(t, t + h))):
        out[:, :h] = own[:, :h] + above[:, :, cols]
        out[:, h:t] = own[:, h:t]
        out[:, t:] = own[:, t:] + below[:, :, cols]


def update_kernel(rows_first, tile, low, side, corner, left, middle, bottom, right, *refs):
    from_left, from_right, even, odd, new_l, new_m, new_r = refs
    h, t = PROBE, TILE
    above, below = Chosen(odd, even), Chosen(even, odd)
    first, second, third = slice(0, h), slice(h, t), slice(t, t + h)
    top, mid, end = first, second, third

    def side_sum(own, other, rows, cols):
        total = own[:, rows] + other[:, rows]
        if rows_first or rows is mid:
            return total
        return total + (above if rows is top else below)[:, :, cols]

    new_l[:, top] = tile[:, 0, top, first] - STEP * side_sum(left, from_left, top, first)
    new_l[:, mid] = tile[:, 0, mid, first] - STEP * side_sum(left, from_left, mid, first)
    new_l[:, end] = low[:, :, first] - STEP * side_sum(left, from_left, end, first)
    new_m[:, top] = tile[:, 0, top, second] - STEP * (middle[:, top] + above[:, :, second])
    new_m[:, mid] = tile[:, 0, mid, second] - STEP * middle[:, mid]
    new_m[:, end] = low[:, :, second] - STEP * (bottom[...] + below[:, :, second])
    new_r[:, top] = side[:, top] - STEP * side_sum(right, from_right, top, third)
    new_r[:, mid] = side[:, mid] - STEP * side_sum(right, from_right, mid, third)
    new_r[:, end] = corner[...] - STEP * side_sum(right, from_right, end, third)


def update(layer, field, grad, columns, even, odd, rows_first):
    operands = [*field, *grad, *columns, even, odd]
    specs = field_specs(0, layer, fill_first)
    body = functools.partial(update_kernel, rows_first)
    return plain(body, [SIDE] * 3, operands, specs)


def spill_kernel(*refs):
    down = refs[-1]
    for n in range(down.shape[0]):
        left, from_left = refs[2 * n : 2 * n + 2]
        rows = from_left.shape[1]
        down[n] = left[:, TILE:] + from_left[:, rows - PROBE :]


def spill(*pairs):
    operands = [array for pair in pairs for array in pair]
    return plain(spill_kernel, [shape(len(pairs), 2, PROBE, PROBE)], operands)[0]


def last_kernel(layers, place, *refs):
    out, h, t = refs[-1], PROBE, TILE
    above_l = refs[6 * layers]
    for n in range(layers):
        old_l, old_m, left, middle, from_left, above_m = refs[6 * n : 6 * n + 6]
        top_l = left[:, :h] + from_left[:, :h] + above_l[n]
        out[:, place + n, :h, :h] = old_l[:, :h] - STEP * top_l
        out[:, place + n, h:, :h] = old_l[:, h:t] - STEP * (left[:, h:t] + from_left[:, h:t])
        out[:, place + n, :h, h:] = old_m[:, :h] - STEP * (middle[:, :h] + above_m[...])
        out[:, place + n, h:, h:] = old_m[:, h:t] - STEP * middle[:, h:t]


def last(pieces, above_l, spec, result):
    operands = [array for piece in pieces for array in piece] + [above_l]
    specs, aliases = {}, {}
    if result is not None:
        specs, aliases = {len(operands): pl.BlockSpec(memory_space=pl.ANY)}, {len(operands): 0}
        operands.append(result)
    return plain(
        functools.partial(last_kernel, len(pieces), 0 if result is not None else 1),
        [shape(2, SLICES, TILE, TILE)],
        operands,
        specs,
        aliases,
        [spec],
    )[0]


def on_device(object_field, probe, propagator, measured, offsets):
    h, t = PROBE, TILE
    phase, tables = prepare(probe, propagator)
    offsets = jnp.swapaxes(offsets, 2, 3).reshape(2, POS)
    intensity = measured.reshape(POS, h, h)

    top, all_rows, left, all_cols = pl.ds(0, h), pl.ds(0, t), pl.ds(0, h), pl.ds(0, t)
    rows_shape = shape(2, h, t)
    rows0, cols0 = pack(
        object_field, [(0, top, all_cols), (0, all_rows, left)], [rows_shape, shape(2, t, h)]
    )
    rows1, rows2, cols12 = pack(
        object_field,
        [(1, top, all_cols), (2, top, all_cols), (pl.ds(1, 2), all_rows, left)],
        [rows_shape, rows_shape, shape(2, 2, t, h)],
    )
    right0 = shifted(cols0, "col", -1)
    right12 = shifted(cols12, "col", -1)
    fields = []
    for layer, rows in enumerate((rows0, rows1, rows2)):
        low = shifted(rows, "row", -1)
        corner = shifted(low[:, :, :h], "col", -1)
        fields.append([object_field, low, right0 if layer == 0 else right12, corner])

    def gradients(fields, fill):
        _, wave1 = forward(offsets, tables, phase, None, fields[0], 0, fill)
        win1, wave2 = forward(offsets, tables, phase, wave1, fields[1], 1, fill)
        *grad2, back = turn(offsets, tables, intensity, wave2, fields[2], 2, fill)
        *grad1, back = backward(offsets, tables, phase, back, wave1, win1)
        grad0 = backward(offsets, tables, phase, back, None, None)
        return [grad0, grad1, grad2]

    grads = gradients(fields, fill_first)
    renewed = [None] * SLICES

    def columns(west, east):
        from_left = shifted(east, "col", 1)
        from_right = shifted(west, "col", -1)
        return [from_left, from_right]

    for layer in (2, 1, 0):
        grad, rows_first = grads[layer], layer != 0
        moved = [] if rows_first else columns(grad[0], grad[3])
        for_even, for_odd = sums(grad, moved)
        even = swapped(for_even, 0)
        odd = swapped(for_odd, 1)
        if rows_first:
            west, east = plain(edges_kernel, [SIDE] * 2, [grad[0], grad[3], even, odd])
            moved = columns(west, east)
            grad = [west, grad[1], grad[2], east]
        renewed[layer] = list(update(layer, fields[layer], grad, moved, even, odd, rows_first))
    grads = gradients(renewed, fill_next)
    from_left, above_m = {}, {}
    for layer in (2, 1, 0):
        right = grads[layer][3]
        from_left[layer] = shifted(right if layer else right[:, t:], "col", 1)
        above_m[layer] = shifted(grads[layer][2], "row", 1)
    down = spill((grads[1][0], from_left[1]), (grads[2][0], from_left[2]))
    above_l12 = shifted(down, "row", 1)
    down = spill((grads[0][0], from_left[0]))
    above_l0 = shifted(down, "row", 1)
    from_left[0] = shifted(grads[0][3][:, :t], "col", 1)
    pieces = [
        (renewed[n][0], renewed[n][1], grads[n][0], grads[n][1], from_left[n], above_m[n])
        for n in range(SLICES)
    ]
    result = last(pieces[1:], above_l12, whole(shape(2, SLICES, TILE, TILE)), None)
    return last(pieces[:1], above_l0, tile_of(0), result)


def solution(mesh):
    placed = (
        P(None, None, "row", "col"),
        P(),
        P(),
        P("row", "col", None, None, None),
        P("row", "col", None, None),
    )
    return jax.shard_map(
        on_device,
        mesh=mesh,
        in_specs=placed,
        out_specs=P(None, None, "row", "col"),
        check_vma=False,
    )
```

```python
import functools
import math

import jax
import jax.numpy as jnp
import numpy as np
from jax import lax
from jax.experimental import pallas as pl
from jax.experimental.pallas import tpu as pltpu
from jax.sharding import PartitionSpec as P


PROBE = 128
SLICES = 3
POS = 6
TILE = 256
EXT = TILE + PROBE
SUB = 8
STEP = 0.05
F32 = jnp.float32
BF16 = jnp.bfloat16


def dft_tables():
    index = np.arange(PROBE)
    angle = (index[:, None] * index[None, :] % PROBE) * (-2.0 * math.pi / PROBE)
    cosines, sines = np.cos(angle) / math.sqrt(PROBE), np.sin(angle) / math.sqrt(PROBE)
    right = np.block([[cosines, sines], [-sines, cosines]]).astype(np.float32)
    high = right.astype(BF16)
    return np.stack([high, (right - high.astype(np.float32)).astype(BF16)])


def split(value):
    high = value.astype(BF16)
    return high, (value - high.astype(F32)).astype(BF16)


def dot(a, b):
    return jnp.dot(a, b, preferred_element_type=F32)


def times_right(block, table):
    high, low = block
    wide, fine = table
    return dot(jnp.concatenate([high, low, high], axis=1), jnp.concatenate([wide, wide, fine], axis=0))


def times_left(block, table):
    high, low = block
    wide, fine = table
    return dot(jnp.concatenate([wide, wide, fine], axis=1), jnp.concatenate([high, low, high], axis=0))


def side_to_stack(block):
    h = PROBE
    top = jnp.concatenate([block[:h, :h], block[h:, :h]], axis=1)
    low = jnp.concatenate([block[:h, h:], block[h:, h:]], axis=1)
    return jnp.concatenate([top, low], axis=0)


def times_phase(block, phase_real, phase_imag):
    h = PROBE
    re, im = block[:h], block[h:]
    pr = jnp.concatenate([phase_real, phase_real], axis=1)
    pi = jnp.concatenate([phase_imag, phase_imag], axis=1)
    return jnp.concatenate([re * pr - im * pi, re * pi + im * pr], axis=0)


def keep(work, n, slot, block):
    work[slot, n, 0], work[slot, n, 1] = split(block)


def kept(work, n, slot):
    return work[slot, n, 0], work[slot, n, 1]


PAIRS = POS // 2


def propagate(work, right, left, phase_real, phase_imag, finish):
    for n in range(PAIRS):
        keep(work, n, 1, side_to_stack(times_right(kept(work, n, 0), right)))
    for n in range(PAIRS):
        keep(work, n, 0, times_phase(times_left(kept(work, n, 1), left), phase_real, phase_imag))
    for n in range(PAIRS):
        keep(work, n, 1, side_to_stack(times_left(kept(work, n, 0), right)))
    for n in range(PAIRS):
        finish(n, times_right(kept(work, n, 1), left))


def tables_of(table_ref):
    right = (table_ref[0], table_ref[1])
    left = (table_ref[2], table_ref[3])
    return right, left


def pair_of(ref, p):
    top = jnp.concatenate([ref[0, p], ref[1, p]], axis=1)
    low = jnp.concatenate([ref[0, p + 1], ref[1, p + 1]], axis=1)
    return jnp.concatenate([top, low], axis=0)


def put_pair(ref, p, block):
    h = PROBE
    ref[0, p] = block[:h, :h]
    ref[1, p] = block[:h, h:]
    ref[0, p + 1] = block[h:, :h]
    ref[1, p + 1] = block[h:, h:]


def place(offset_ref, p):
    row, col = offset_ref[0, p], offset_ref[1, p]
    over = lax.rem(row, SUB)
    base = jnp.where(col >= PROBE, PROBE, 0)
    return pl.multiple_of(row - over, SUB), over, pl.multiple_of(base, PROBE), col - base


TALL = PROBE + SUB


def lanes(rows):
    return lax.broadcasted_iota(jnp.int32, (rows, PROBE), 1)


def take_window(ext, offset_ref, p, part):
    row, over, base, shift = place(offset_ref, p)
    after = pl.multiple_of(base + PROBE, PROBE)
    first = ext[part, pl.ds(row, TALL), pl.ds(base, PROBE)]
    second = ext[part, pl.ds(row, TALL), pl.ds(after, PROBE)]
    block = jnp.where(lanes(TALL) >= shift, first, second)
    block = pltpu.roll(block, jnp.where(shift == 0, 0, PROBE - shift), 1)
    return pltpu.roll(block, jnp.where(over == 0, 0, TALL - over), 0)[:PROBE]


def turn_window(offset_ref, p, value):
    _, over, _, shift = place(offset_ref, p)
    block = jnp.concatenate([value, jnp.zeros((SUB, PROBE), F32)], axis=0)
    return pltpu.roll(pltpu.roll(block, over, 0), shift, 1)


def add_windows(grads, offset_ref, turned):
    for p in range(POS):
        row, _, base, shift = place(offset_ref, p)
        after = pl.multiple_of(base + PROBE, PROBE)
        here = lanes(TALL) >= shift
        for part in range(2):
            block = turned[part, p]
            where = (pl.ds(row, TALL), pl.ds(base, PROBE))
            grads[part][where] = grads[part][where] + jnp.where(here, block, 0.0)
            where = (pl.ds(row, TALL), pl.ds(after, PROBE))
            grads[part][where] = grads[part][where] + jnp.where(here, 0.0, block)


def times(ar, ai, br, bi):
    return ar * br - ai * bi, ar * bi + ai * br


def times_conj(ar, ai, br, bi):
    return ar * br + ai * bi, ar * bi - ai * br


def fill_first(ext, refs):
    tile, low_left, low_right, right, corner = refs
    t, h = TILE, PROBE
    ext[:, :t, :t] = tile[:, 0]
    ext[:, t:, :h] = low_left[...]
    ext[:, t:, h:t] = low_right[...]
    ext[:, :t, t:] = right[...]
    ext[:, t:, t:] = corner[...]


def fill_next(ext, refs):
    left, middle, right = refs
    t, h = TILE, PROBE
    ext[:, :, :h] = left[...]
    ext[:, :, h:t] = middle[...]
    ext[:, :, t:] = right[...]


def forward_kernel(fill, n_field, first, *refs):
    offset_ref, table_ref, phase_ref = refs[:3]
    wave = None if first else refs[3]
    field = refs[4 - first : 4 - first + n_field]
    windows, out, ext, work = refs[4 - first + n_field :]
    fill(ext, field)
    right, left = tables_of(table_ref)
    for n in range(PAIRS):
        rows = []
        for q in (2 * n, 2 * n + 1):
            tr = take_window(ext, offset_ref, q, 0)
            ti = take_window(ext, offset_ref, q, 1)
            windows[0, q] = tr
            windows[1, q] = ti
            if first:
                wr, wi = phase_ref[0], phase_ref[1]
            else:
                wr, wi = wave[0, q], wave[1, q]
            rows.append(jnp.concatenate(times(wr, wi, tr, ti), axis=1))
        keep(work, n, 0, jnp.concatenate(rows, axis=0))

    def finish(n, block):
        put_pair(out, 2 * n, block)

    propagate(work, right, left, phase_ref[2], phase_ref[3], finish)


def write_gradient(grads, outs):
    left, middle, low, right = outs
    h, t = PROBE, TILE
    for part in range(2):
        left[part] = grads[part][:, :h]
        middle[part] = grads[part][:t, h:t]
        low[part] = grads[part][t:, h:t]
        right[part] = grads[part][:, t:]


def turn_kernel(fill, n_field, *refs):
    offset_ref, table_ref, intensity, wave = refs[:4]
    field = refs[4 : 4 + n_field]
    outs = refs[4 + n_field : 8 + n_field]
    back, ext, windows, work, turned, *grads = refs[8 + n_field :]
    fill(ext, field)
    for part in grads:
        part[...] = jnp.zeros_like(part)
    right, left = tables_of(table_ref)
    h = PROBE
    for n in range(PAIRS):
        rows = []
        for q in (2 * n, 2 * n + 1):
            tr = take_window(ext, offset_ref, q, 0)
            ti = take_window(ext, offset_ref, q, 1)
            windows[0, q] = tr
            windows[1, q] = ti
            rows.append(jnp.concatenate(times(wave[0, q], wave[1, q], tr, ti), axis=1))
        keep(work, n, 0, jnp.concatenate(rows, axis=0))
    for n in range(PAIRS):
        keep(work, n, 1, side_to_stack(times_right(kept(work, n, 0), right)))
    for n in range(PAIRS):
        block = times_left(kept(work, n, 1), left)
        re, im = block[:h], block[h:]
        target = jnp.concatenate([intensity[2 * n], intensity[2 * n + 1]], axis=1)
        weight = 4.0 * (re * re + im * im - target)
        keep(work, n, 0, jnp.concatenate([re * weight, im * weight], axis=0))
    for n in range(PAIRS):
        keep(work, n, 1, side_to_stack(times_left(kept(work, n, 0), right)))
    for n in range(PAIRS):
        block = times_right(kept(work, n, 1), left)
        for i in range(2):
            q = 2 * n + i
            gr, gi = block[i * h : (i + 1) * h, :h], block[i * h : (i + 1) * h, h:]
            br, bi = times_conj(windows[0, q], windows[1, q], gr, gi)
            back[0, q] = br
            back[1, q] = bi
            dr, di = times_conj(wave[0, q], wave[1, q], gr, gi)
            turned[0, q] = turn_window(offset_ref, q, dr)
            turned[1, q] = turn_window(offset_ref, q, di)
    add_windows(grads, offset_ref, turned)
    write_gradient(grads, outs)


def backward_kernel(first, *refs):
    if first:
        offset_ref, table_ref, phase_ref, back_in = refs[:4]
        outs = refs[4:8]
    else:
        offset_ref, table_ref, phase_ref, back_in, wave, windows = refs[:6]
        outs, back = refs[6:10], refs[10]
    work, turned, *grads = refs[-4:]
    for part in grads:
        part[...] = jnp.zeros_like(part)
    right, left = tables_of(table_ref)
    h = PROBE
    for n in range(PAIRS):
        keep(work, n, 0, pair_of(back_in, 2 * n))

    def finish(n, block):
        for i in range(2):
            q = 2 * n + i
            gr, gi = block[i * h : (i + 1) * h, :h], block[i * h : (i + 1) * h, h:]
            if first:
                dr, di = times_conj(phase_ref[0], phase_ref[1], gr, gi)
            else:
                br, bi = times_conj(windows[0, q], windows[1, q], gr, gi)
                back[0, q] = br
                back[1, q] = bi
                dr, di = times_conj(wave[0, q], wave[1, q], gr, gi)
            turned[0, q] = turn_window(offset_ref, q, dr)
            turned[1, q] = turn_window(offset_ref, q, di)

    propagate(work, right, left, phase_ref[2], -phase_ref[3], finish)
    add_windows(grads, offset_ref, turned)
    write_gradient(grads, outs)


def whole(array):
    rank = len(array.shape)
    return pl.BlockSpec(array.shape, lambda i: (0,) * rank)


def tile_of(layer):
    return pl.BlockSpec((2, 1, TILE, TILE), lambda i: (0, layer, 0, 0))


def shape(*dims):
    return jax.ShapeDtypeStruct(dims, F32)


STACK = (2, POS, PROBE, PROBE)
GRADIENT = [
    shape(2, EXT, PROBE),
    shape(2, TILE, PROBE),
    shape(2, PROBE, PROBE),
    shape(2, EXT, PROBE),
]
WORK = pltpu.VMEM((2, PAIRS, 2, 256, 256), BF16)
SCRATCH = pltpu.VMEM((2, EXT, EXT), F32)
GRADS = [pltpu.VMEM((2, POS, TALL, PROBE), F32)] + [pltpu.VMEM((EXT, EXT), F32)] * 2


def run(body, operands, outs, scratch, stages, specs=None):
    specs = specs or {}
    flops = stages * POS * PROBE * 256 * 256 * 2 * 3
    moved = sum(math.prod(o.shape) * 4 for o in operands) + sum(math.prod(o.shape) * 4 for o in outs)
    in_specs = [pl.BlockSpec(memory_space=pltpu.SMEM)]
    in_specs += [specs.get(n, None) or whole(o) for n, o in enumerate(operands) if n > 0]
    return pl.pallas_call(
        body,
        grid=(1,),
        in_specs=in_specs,
        out_specs=[whole(o) for o in outs],
        out_shape=outs,
        scratch_shapes=scratch,
        cost_estimate=pl.CostEstimate(flops=flops, bytes_accessed=moved, transcendentals=0),
        compiler_params=pltpu.CompilerParams(vmem_limit_bytes=14 * 2**20),
    )(*operands)


def field_specs(start, layer, fill):
    if fill is not fill_first:
        return {}
    h, t = PROBE, TILE
    if layer == 0:
        lows = [pl.BlockSpec((2, h, h), lambda i: (0, 0, 0)), pl.BlockSpec((2, h, h), lambda i: (0, 0, 1))]
        sides = [None, None]
    else:
        low = pl.BlockSpec((2, None, h, h), lambda i: (0, layer - 1, 0, 0))
        lows, sides = [low, low], [pl.BlockSpec((2, None, t, h), lambda i: (0, layer - 1, 0, 0)), low]
    return {start + n: spec for n, spec in enumerate([tile_of(layer), *lows, *sides])}


def forward(offsets, tables, phase, wave, field, layer, fill):
    first = wave is None
    operands = [offsets, tables, phase] + ([] if first else [wave])
    specs = field_specs(len(operands), layer, fill)
    body = functools.partial(forward_kernel, fill, len(field), first)
    return run(body, operands + field, [shape(*STACK)] * 2, [SCRATCH, WORK], 4, specs)


def turn(offsets, tables, intensity, wave, field, layer, fill):
    operands = [offsets, tables, intensity, wave]
    specs = field_specs(len(operands), layer, fill)
    body = functools.partial(turn_kernel, fill, len(field))
    scratch = [SCRATCH, pltpu.VMEM(STACK, F32), WORK, *GRADS]
    return run(body, operands + field, [*GRADIENT, shape(*STACK)], scratch, 4, specs)


def backward(offsets, tables, phase, back, wave, windows):
    first = wave is None
    operands = [offsets, tables, phase, back] + ([] if first else [wave, windows])
    outs = [*GRADIENT] if first else [*GRADIENT, shape(*STACK)]
    return run(functools.partial(backward_kernel, first), operands, outs, [WORK, *GRADS], 4)


def shifted(block, axis, distance):
    size = lax.axis_size(axis)
    return lax.ppermute(block, axis, [((i - distance) % size, i) for i in range(size)])


def swapped(block, odd):
    size = lax.axis_size("row")
    route = []
    for i in range(odd, size + odd, 2):
        route += [(i % size, (i + 1) % size), ((i + 1) % size, i % size)]
    return lax.ppermute(block, "row", sorted(route))


def plain(body, outs, operands, specs=None, aliases=None, out_specs=None):
    specs = specs or {}
    moved = sum(math.prod(o.shape) * 4 for o in outs)
    return pl.pallas_call(
        body,
        grid=(1,),
        in_specs=[specs.get(n, None) or whole(o) for n, o in enumerate(operands)],
        out_specs=out_specs or [whole(o) for o in outs],
        out_shape=outs,
        input_output_aliases=aliases or {},
        cost_estimate=pl.CostEstimate(flops=0, bytes_accessed=2 * moved, transcendentals=0),
        compiler_params=pltpu.CompilerParams(vmem_limit_bytes=8 * 2**20),
    )(*operands)


SIDE = shape(2, EXT, PROBE)


def pack_kernel(jobs, tile, *refs):
    outs, sems = refs[:-1], refs[-1]
    copies = [
        pltpu.make_async_copy(tile.at[:, layer, rows, cols], out, sems.at[n])
        for n, ((layer, rows, cols), out) in enumerate(zip(jobs, outs))
    ]
    for copy in copies:
        copy.start()
    for copy in copies:
        copy.wait()


def pack(object_field, jobs, outs):
    return pl.pallas_call(
        functools.partial(pack_kernel, jobs),
        in_specs=[pl.BlockSpec(memory_space=pltpu.HBM)],
        out_specs=[pl.BlockSpec(memory_space=pltpu.VMEM)] * len(outs),
        out_shape=outs,
        scratch_shapes=[pltpu.SemaphoreType.DMA((len(outs),))],
        name="pack",
        cost_estimate=pl.CostEstimate(flops=0, bytes_accessed=4 * 2**18, transcendentals=0),
        compiler_params=pltpu.CompilerParams(vmem_limit_bytes=4 * 2**20),
    )(object_field)


def prepare_kernel(probe, propagator, tables, phase, copied):
    phase[:2] = probe[...]
    phase[2] = jnp.cos(propagator[...])
    phase[3] = jnp.sin(propagator[...])
    h = PROBE
    copied[:2] = tables[...]
    copied[2:, :h, :h] = tables[:, :h, :h]
    copied[2:, :h, h:] = tables[:, h:, :h]
    copied[2:, h:, :h] = tables[:, :h, h:]
    copied[2:, h:, h:] = tables[:, h:, h:]


def prepare(probe, propagator):
    tables = jnp.asarray(dft_tables())
    outs = [shape(4, PROBE, PROBE), jax.ShapeDtypeStruct((4, 2 * PROBE, 2 * PROBE), BF16)]
    return plain(prepare_kernel, outs, [probe, propagator, tables])


def sums_kernel(summed, left, middle, low, right, *refs):
    h, t = PROBE, TILE
    even_out, odd_out = refs[-2:]
    from_left, from_right = refs[:2] if summed else (None, None)

    def total(own, other, rows):
        return own[:, rows] + other[:, rows] if summed else own[:, rows]

    def fill(down, up):
        down[:, :, :h] = total(left, from_left, slice(t, t + h))
        up[:, :, :h] = total(left, from_left, slice(0, h))
        down[:, :, h:t] = low[...]
        up[:, :, h:t] = middle[:, :h]
        down[:, :, t:] = total(right, from_right, slice(t, t + h))
        up[:, :, t:] = total(right, from_right, slice(0, h))

    parity = lax.axis_index("row") & 1

    @pl.when(parity == 0)
    def _():
        fill(even_out, odd_out)

    @pl.when(parity == 1)
    def _():
        fill(odd_out, even_out)


def sums(grad, columns):
    body = functools.partial(sums_kernel, bool(columns))
    return plain(body, [shape(2, PROBE, EXT)] * 2, [*grad, *columns])


class Chosen:
    def __init__(self, for_even, for_odd):
        self.pair = for_even, for_odd

    def __getitem__(self, where):
        odd_row = (lax.axis_index("row") & 1) == 1
        return jnp.where(odd_row, self.pair[1][where], self.pair[0][where])


def edges_kernel(left, right, even, odd, west, east):
    h, t = PROBE, TILE
    above, below = Chosen(odd, even), Chosen(even, odd)
    for out, own, cols in ((west, left, slice(0, h)), (east, right, slice(t, t + h))):
        out[:, :h] = own[:, :h] + above[:, :, cols]
        out[:, h:t] = own[:, h:t]
        out[:, t:] = own[:, t:] + below[:, :, cols]


def update_kernel(rows_first, tile, low_left, low_right, side, corner, left, middle, bottom, right, *refs):
    from_left, from_right, even, odd, new_l, new_m, new_r = refs
    h, t = PROBE, TILE
    above, below = Chosen(odd, even), Chosen(even, odd)
    first, second, third = slice(0, h), slice(h, t), slice(t, t + h)
    top, mid, end = first, second, third

    def side_sum(own, other, rows, cols):
        total = own[:, rows] + other[:, rows]
        if rows_first or rows is mid:
            return total
        return total + (above if rows is top else below)[:, :, cols]

    new_l[:, top] = tile[:, 0, top, first] - STEP * side_sum(left, from_left, top, first)
    new_l[:, mid] = tile[:, 0, mid, first] - STEP * side_sum(left, from_left, mid, first)
    new_l[:, end] = low_left[...] - STEP * side_sum(left, from_left, end, first)
    new_m[:, top] = tile[:, 0, top, second] - STEP * (middle[:, top] + above[:, :, second])
    new_m[:, mid] = tile[:, 0, mid, second] - STEP * middle[:, mid]
    new_m[:, end] = low_right[...] - STEP * (bottom[...] + below[:, :, second])
    new_r[:, top] = side[:, top] - STEP * side_sum(right, from_right, top, third)
    new_r[:, mid] = side[:, mid] - STEP * side_sum(right, from_right, mid, third)
    new_r[:, end] = corner[...] - STEP * side_sum(right, from_right, end, third)


def update(layer, field, grad, columns, even, odd, rows_first):
    operands = [*field, *grad, *columns, even, odd]
    specs = field_specs(0, layer, fill_first)
    body = functools.partial(update_kernel, rows_first)
    return plain(body, [SIDE] * 3, operands, specs)


def spill_kernel(*refs):
    down = refs[-1]
    for n in range(down.shape[0]):
        left, from_left = refs[2 * n : 2 * n + 2]
        rows = from_left.shape[1]
        down[n] = left[:, TILE:] + from_left[:, rows - PROBE :]


def spill(*pairs):
    operands = [array for pair in pairs for array in pair]
    return plain(spill_kernel, [shape(len(pairs), 2, PROBE, PROBE)], operands)[0]


def last_kernel(layers, place, *refs):
    out, h, t = refs[-1], PROBE, TILE
    above_l = refs[6 * layers]
    for n in range(layers):
        old_l, old_m, left, middle, from_left, above_m = refs[6 * n : 6 * n + 6]
        top_l = left[:, :h] + from_left[:, :h] + above_l[n]
        out[:, place + n, :h, :h] = old_l[:, :h] - STEP * top_l
        out[:, place + n, h:, :h] = old_l[:, h:t] - STEP * (left[:, h:t] + from_left[:, h:t])
        out[:, place + n, :h, h:] = old_m[:, :h] - STEP * (middle[:, :h] + above_m[...])
        out[:, place + n, h:, h:] = old_m[:, h:t] - STEP * middle[:, h:t]


def last(pieces, above_l, spec, result):
    operands = [array for piece in pieces for array in piece] + [above_l]
    specs, aliases = {}, {}
    if result is not None:
        specs, aliases = {len(operands): pl.BlockSpec(memory_space=pl.ANY)}, {len(operands): 0}
        operands.append(result)
    return plain(
        functools.partial(last_kernel, len(pieces), 0 if result is not None else 1),
        [shape(2, SLICES, TILE, TILE)],
        operands,
        specs,
        aliases,
        [spec],
    )[0]


def on_device(object_field, probe, propagator, measured, offsets):
    h, t = PROBE, TILE
    phase, tables = prepare(probe, propagator)
    offsets = jnp.swapaxes(offsets, 2, 3).reshape(2, POS)
    intensity = measured.reshape(POS, h, h)

    top, all_rows, west_half, east_half, rest = pl.ds(0, h), pl.ds(0, t), pl.ds(0, h), pl.ds(h, h), pl.ds(1, 2)
    rows0 = object_field[:, 0, :h]
    cols0, west_rows, east_rows, cols12 = pack(
        object_field,
        [(0, all_rows, west_half), (rest, top, west_half), (rest, top, east_half), (rest, all_rows, west_half)],
        [shape(2, t, h), shape(2, 2, h, h), shape(2, 2, h, h), shape(2, 2, t, h)],
    )
    low0 = shifted(rows0, "row", -1)
    low_west = shifted(west_rows, "row", -1)
    low_east = shifted(east_rows, "row", -1)
    right0 = shifted(cols0, "col", -1)
    right12 = shifted(cols12, "col", -1)
    corner0 = shifted(low0[:, :, :h], "col", -1)
    corner12 = shifted(low_west, "col", -1)
    fields = [
        [object_field, low0, low0, right0, corner0],
        [object_field, low_west, low_east, right12, corner12],
        [object_field, low_west, low_east, right12, corner12],
    ]

    def gradients(fields, fill):
        _, wave1 = forward(offsets, tables, phase, None, fields[0], 0, fill)
        win1, wave2 = forward(offsets, tables, phase, wave1, fields[1], 1, fill)
        *grad2, back = turn(offsets, tables, intensity, wave2, fields[2], 2, fill)
        *grad1, back = backward(offsets, tables, phase, back, wave1, win1)
        grad0 = backward(offsets, tables, phase, back, None, None)
        return [grad0, grad1, grad2]

    grads = gradients(fields, fill_first)
    renewed = [None] * SLICES

    def columns(west, east):
        from_left = shifted(east, "col", 1)
        from_right = shifted(west, "col", -1)
        return [from_left, from_right]

    for layer in (2, 1, 0):
        grad, rows_first = grads[layer], layer != 0
        moved = [] if rows_first else columns(grad[0], grad[3])
        for_even, for_odd = sums(grad, moved)
        even = swapped(for_even, 0)
        odd = swapped(for_odd, 1)
        if rows_first:
            west, east = plain(edges_kernel, [SIDE] * 2, [grad[0], grad[3], even, odd])
            moved = columns(west, east)
            grad = [west, grad[1], grad[2], east]
        renewed[layer] = list(update(layer, fields[layer], grad, moved, even, odd, rows_first))
    grads = gradients(renewed, fill_next)
    from_left, above_m = {}, {}
    for layer in (2, 1, 0):
        right = grads[layer][3]
        from_left[layer] = shifted(right if layer else right[:, t:], "col", 1)
        above_m[layer] = shifted(grads[layer][2], "row", 1)
    down = spill((grads[1][0], from_left[1]), (grads[2][0], from_left[2]))
    above_l12 = shifted(down, "row", 1)
    down = spill((grads[0][0], from_left[0]))
    above_l0 = shifted(down, "row", 1)
    from_left[0] = shifted(grads[0][3][:, :t], "col", 1)
    pieces = [
        (renewed[n][0], renewed[n][1], grads[n][0], grads[n][1], from_left[n], above_m[n])
        for n in range(SLICES)
    ]
    result = last(pieces[1:], above_l12, whole(shape(2, SLICES, TILE, TILE)), None)
    return last(pieces[:1], above_l0, tile_of(0), result)


def solution(mesh):
    placed = (
        P(None, None, "row", "col"),
        P(),
        P(),
        P("row", "col", None, None, None),
        P("row", "col", None, None),
    )
    return jax.shard_map(
        on_device,
        mesh=mesh,
        in_specs=placed,
        out_specs=P(None, None, "row", "col"),
        check_vma=False,
    )
```

```python
import functools
import math

import jax
import jax.numpy as jnp
import numpy as np
from jax import lax
from jax.experimental import pallas as pl
from jax.experimental.pallas import tpu as pltpu
from jax.sharding import PartitionSpec as P


PROBE = 128
SLICES = 3
POS = 6
TILE = 256
EXT = TILE + PROBE
SUB = 8
STEP = 0.05
F32 = jnp.float32
BF16 = jnp.bfloat16


def dft_tables():
    index = np.arange(PROBE)
    angle = (index[:, None] * index[None, :] % PROBE) * (-2.0 * math.pi / PROBE)
    cosines, sines = np.cos(angle) / math.sqrt(PROBE), np.sin(angle) / math.sqrt(PROBE)
    right = np.block([[cosines, sines], [-sines, cosines]]).astype(np.float32)
    high = right.astype(BF16)
    return np.stack([high, (right - high.astype(np.float32)).astype(BF16)])


def split(value):
    high = value.astype(BF16)
    return high, (value - high.astype(F32)).astype(BF16)


def dot(a, b):
    return jnp.dot(a, b, preferred_element_type=F32)


def times_right(block, table):
    high, low = block
    wide, fine = table
    return dot(jnp.concatenate([high, low, high], axis=1), jnp.concatenate([wide, wide, fine], axis=0))


def times_left(block, table):
    high, low = block
    wide, fine = table
    return dot(jnp.concatenate([wide, wide, fine], axis=1), jnp.concatenate([high, low, high], axis=0))


def side_to_stack(block):
    h = PROBE
    top = jnp.concatenate([block[:h, :h], block[h:, :h]], axis=1)
    low = jnp.concatenate([block[:h, h:], block[h:, h:]], axis=1)
    return jnp.concatenate([top, low], axis=0)


def times_phase(block, phase_real, phase_imag):
    h = PROBE
    re, im = block[:h], block[h:]
    pr = jnp.concatenate([phase_real, phase_real], axis=1)
    pi = jnp.concatenate([phase_imag, phase_imag], axis=1)
    return jnp.concatenate([re * pr - im * pi, re * pi + im * pr], axis=0)


def keep(work, n, slot, block):
    work[slot, n, 0], work[slot, n, 1] = split(block)


def kept(work, n, slot):
    return work[slot, n, 0], work[slot, n, 1]


PAIRS = POS // 2


def propagate(work, right, left, phase_real, phase_imag, finish):
    for n in range(PAIRS):
        keep(work, n, 1, side_to_stack(times_right(kept(work, n, 0), right)))
    for n in range(PAIRS):
        keep(work, n, 0, times_phase(times_left(kept(work, n, 1), left), phase_real, phase_imag))
    for n in range(PAIRS):
        keep(work, n, 1, side_to_stack(times_left(kept(work, n, 0), right)))
    for n in range(PAIRS):
        finish(n, times_right(kept(work, n, 1), left))


def tables_of(table_ref):
    right = (table_ref[0], table_ref[1])
    left = (table_ref[2], table_ref[3])
    return right, left


def pair_of(ref, p):
    top = jnp.concatenate([ref[0, p], ref[1, p]], axis=1)
    low = jnp.concatenate([ref[0, p + 1], ref[1, p + 1]], axis=1)
    return jnp.concatenate([top, low], axis=0)


def put_pair(ref, p, block):
    h = PROBE
    ref[0, p] = block[:h, :h]
    ref[1, p] = block[:h, h:]
    ref[0, p + 1] = block[h:, :h]
    ref[1, p + 1] = block[h:, h:]


def place(offset_ref, p):
    row, col = offset_ref[0, p], offset_ref[1, p]
    over = lax.rem(row, SUB)
    base = jnp.where(col >= PROBE, PROBE, 0)
    return pl.multiple_of(row - over, SUB), over, pl.multiple_of(base, PROBE), col - base


TALL = PROBE + SUB


def lanes(rows):
    return lax.broadcasted_iota(jnp.int32, (rows, PROBE), 1)


def take_window(ext, offset_ref, p, part):
    row, over, base, shift = place(offset_ref, p)
    after = pl.multiple_of(base + PROBE, PROBE)
    first = ext[part, pl.ds(row, TALL), pl.ds(base, PROBE)]
    second = ext[part, pl.ds(row, TALL), pl.ds(after, PROBE)]
    block = jnp.where(lanes(TALL) >= shift, first, second)
    block = pltpu.roll(block, jnp.where(shift == 0, 0, PROBE - shift), 1)
    return pltpu.roll(block, jnp.where(over == 0, 0, TALL - over), 0)[:PROBE]


def turn_window(offset_ref, p, value):
    _, over, _, shift = place(offset_ref, p)
    block = jnp.concatenate([value, jnp.zeros((SUB, PROBE), F32)], axis=0)
    return pltpu.roll(pltpu.roll(block, over, 0), shift, 1)


def add_windows(grads, offset_ref, turned):
    for p in range(POS):
        row, _, base, shift = place(offset_ref, p)
        after = pl.multiple_of(base + PROBE, PROBE)
        here = lanes(TALL) >= shift
        for part in range(2):
            block = turned[part, p]
            where = (pl.ds(row, TALL), pl.ds(base, PROBE))
            grads[part][where] = grads[part][where] + jnp.where(here, block, 0.0)
            where = (pl.ds(row, TALL), pl.ds(after, PROBE))
            grads[part][where] = grads[part][where] + jnp.where(here, 0.0, block)


def times(ar, ai, br, bi):
    return ar * br - ai * bi, ar * bi + ai * br


def times_conj(ar, ai, br, bi):
    return ar * br + ai * bi, ar * bi - ai * br


def fill_first(ext, refs):
    tile, low_left, low_right, right, corner = refs
    t, h = TILE, PROBE
    ext[:, :t, :t] = tile[:, 0]
    ext[:, t:, :h] = low_left[...]
    ext[:, t:, h:t] = low_right[...]
    ext[:, :t, t:] = right[...]
    ext[:, t:, t:] = corner[...]


def fill_next(ext, refs):
    left, middle, right = refs
    t, h = TILE, PROBE
    ext[:, :, :h] = left[...]
    ext[:, :, h:t] = middle[...]
    ext[:, :, t:] = right[...]


def forward_kernel(fill, n_field, first, *refs):
    offset_ref, table_ref, phase_ref = refs[:3]
    wave = None if first else refs[3]
    field = refs[4 - first : 4 - first + n_field]
    windows, out, ext, work = refs[4 - first + n_field :]
    fill(ext, field)
    right, left = tables_of(table_ref)
    for n in range(PAIRS):
        rows = []
        for q in (2 * n, 2 * n + 1):
            tr = take_window(ext, offset_ref, q, 0)
            ti = take_window(ext, offset_ref, q, 1)
            windows[0, q] = tr
            windows[1, q] = ti
            if first:
                wr, wi = phase_ref[0], phase_ref[1]
            else:
                wr, wi = wave[0, q], wave[1, q]
            rows.append(jnp.concatenate(times(wr, wi, tr, ti), axis=1))
        keep(work, n, 0, jnp.concatenate(rows, axis=0))

    def finish(n, block):
        put_pair(out, 2 * n, block)

    propagate(work, right, left, phase_ref[2], phase_ref[3], finish)


def write_gradient(grads, outs):
    left, middle, low, right = outs
    h, t = PROBE, TILE
    for part in range(2):
        left[part] = grads[part][:, :h]
        middle[part] = grads[part][:t, h:t]
        low[part] = grads[part][t:, h:t]
        right[part] = grads[part][:, t:]


def turn_kernel(fill, n_field, *refs):
    offset_ref, table_ref, intensity, wave = refs[:4]
    field = refs[4 : 4 + n_field]
    outs = refs[4 + n_field : 8 + n_field]
    back, ext, windows, work, turned, *grads = refs[8 + n_field :]
    fill(ext, field)
    for part in grads:
        part[...] = jnp.zeros_like(part)
    right, left = tables_of(table_ref)
    h = PROBE
    for n in range(PAIRS):
        rows = []
        for q in (2 * n, 2 * n + 1):
            tr = take_window(ext, offset_ref, q, 0)
            ti = take_window(ext, offset_ref, q, 1)
            windows[0, q] = tr
            windows[1, q] = ti
            rows.append(jnp.concatenate(times(wave[0, q], wave[1, q], tr, ti), axis=1))
        keep(work, n, 0, jnp.concatenate(rows, axis=0))
    for n in range(PAIRS):
        keep(work, n, 1, side_to_stack(times_right(kept(work, n, 0), right)))
    for n in range(PAIRS):
        block = times_left(kept(work, n, 1), left)
        re, im = block[:h], block[h:]
        target = jnp.concatenate([intensity[2 * n], intensity[2 * n + 1]], axis=1)
        weight = 4.0 * (re * re + im * im - target)
        keep(work, n, 0, jnp.concatenate([re * weight, im * weight], axis=0))
    for n in range(PAIRS):
        keep(work, n, 1, side_to_stack(times_left(kept(work, n, 0), right)))
    for n in range(PAIRS):
        block = times_right(kept(work, n, 1), left)
        for i in range(2):
            q = 2 * n + i
            gr, gi = block[i * h : (i + 1) * h, :h], block[i * h : (i + 1) * h, h:]
            br, bi = times_conj(windows[0, q], windows[1, q], gr, gi)
            back[0, q] = br
            back[1, q] = bi
            dr, di = times_conj(wave[0, q], wave[1, q], gr, gi)
            turned[0, q] = turn_window(offset_ref, q, dr)
            turned[1, q] = turn_window(offset_ref, q, di)
    add_windows(grads, offset_ref, turned)
    write_gradient(grads, outs)


def backward_kernel(first, *refs):
    if first:
        offset_ref, table_ref, phase_ref, back_in = refs[:4]
        outs = refs[4:8]
    else:
        offset_ref, table_ref, phase_ref, back_in, wave, windows = refs[:6]
        outs, back = refs[6:10], refs[10]
    work, turned, *grads = refs[-4:]
    for part in grads:
        part[...] = jnp.zeros_like(part)
    right, left = tables_of(table_ref)
    h = PROBE
    for n in range(PAIRS):
        keep(work, n, 0, pair_of(back_in, 2 * n))

    def finish(n, block):
        for i in range(2):
            q = 2 * n + i
            gr, gi = block[i * h : (i + 1) * h, :h], block[i * h : (i + 1) * h, h:]
            if first:
                dr, di = times_conj(phase_ref[0], phase_ref[1], gr, gi)
            else:
                br, bi = times_conj(windows[0, q], windows[1, q], gr, gi)
                back[0, q] = br
                back[1, q] = bi
                dr, di = times_conj(wave[0, q], wave[1, q], gr, gi)
            turned[0, q] = turn_window(offset_ref, q, dr)
            turned[1, q] = turn_window(offset_ref, q, di)

    propagate(work, right, left, phase_ref[2], -phase_ref[3], finish)
    add_windows(grads, offset_ref, turned)
    write_gradient(grads, outs)


def whole(array):
    rank = len(array.shape)
    return pl.BlockSpec(array.shape, lambda i: (0,) * rank)


def tile_of(layer):
    return pl.BlockSpec((2, 1, TILE, TILE), lambda i: (0, layer, 0, 0))


def shape(*dims):
    return jax.ShapeDtypeStruct(dims, F32)


STACK = (2, POS, PROBE, PROBE)
GRADIENT = [
    shape(2, EXT, PROBE),
    shape(2, TILE, PROBE),
    shape(2, PROBE, PROBE),
    shape(2, EXT, PROBE),
]
WORK = pltpu.VMEM((2, PAIRS, 2, 256, 256), BF16)
SCRATCH = pltpu.VMEM((2, EXT, EXT), F32)
GRADS = [pltpu.VMEM((2, POS, TALL, PROBE), F32)] + [pltpu.VMEM((EXT, EXT), F32)] * 2


def run(body, operands, outs, scratch, stages, specs=None):
    specs = specs or {}
    flops = stages * POS * PROBE * 256 * 256 * 2 * 3
    moved = sum(math.prod(o.shape) * 4 for o in operands) + sum(math.prod(o.shape) * 4 for o in outs)
    in_specs = [pl.BlockSpec(memory_space=pltpu.SMEM)]
    in_specs += [specs.get(n, None) or whole(o) for n, o in enumerate(operands) if n > 0]
    return pl.pallas_call(
        body,
        grid=(1,),
        in_specs=in_specs,
        out_specs=[whole(o) for o in outs],
        out_shape=outs,
        scratch_shapes=scratch,
        cost_estimate=pl.CostEstimate(flops=flops, bytes_accessed=moved, transcendentals=0),
        compiler_params=pltpu.CompilerParams(vmem_limit_bytes=14 * 2**20),
    )(*operands)


def field_specs(start, layer, fill):
    if fill is not fill_first:
        return {}
    h, t = PROBE, TILE
    if layer == 0:
        lows = [pl.BlockSpec((2, h, h), lambda i: (0, 0, 0)), pl.BlockSpec((2, h, h), lambda i: (0, 0, 1))]
        sides = [None, None]
    else:
        low = pl.BlockSpec((2, None, h, h), lambda i: (0, layer - 1, 0, 0))
        lows, sides = [low, low], [pl.BlockSpec((2, None, t, h), lambda i: (0, layer - 1, 0, 0)), low]
    return {start + n: spec for n, spec in enumerate([tile_of(layer), *lows, *sides])}


def forward(offsets, tables, phase, wave, field, layer, fill):
    first = wave is None
    operands = [offsets, tables, phase] + ([] if first else [wave])
    specs = field_specs(len(operands), layer, fill)
    body = functools.partial(forward_kernel, fill, len(field), first)
    return run(body, operands + field, [shape(*STACK)] * 2, [SCRATCH, WORK], 4, specs)


def turn(offsets, tables, intensity, wave, field, layer, fill):
    operands = [offsets, tables, intensity, wave]
    specs = field_specs(len(operands), layer, fill)
    body = functools.partial(turn_kernel, fill, len(field))
    scratch = [SCRATCH, pltpu.VMEM(STACK, F32), WORK, *GRADS]
    return run(body, operands + field, [*GRADIENT, shape(*STACK)], scratch, 4, specs)


def backward(offsets, tables, phase, back, wave, windows):
    first = wave is None
    operands = [offsets, tables, phase, back] + ([] if first else [wave, windows])
    outs = [*GRADIENT] if first else [*GRADIENT, shape(*STACK)]
    return run(functools.partial(backward_kernel, first), operands, outs, [WORK, *GRADS], 4)


def shifted(block, axis, distance):
    size = lax.axis_size(axis)
    return lax.ppermute(block, axis, [((i - distance) % size, i) for i in range(size)])


def swapped(block, odd):
    size = lax.axis_size("row")
    route = []
    for i in range(odd, size + odd, 2):
        route += [(i % size, (i + 1) % size), ((i + 1) % size, i % size)]
    return lax.ppermute(block, "row", sorted(route))


def plain(body, outs, operands, specs=None, aliases=None, out_specs=None):
    specs = specs or {}
    moved = sum(math.prod(o.shape) * 4 for o in outs)
    return pl.pallas_call(
        body,
        grid=(1,),
        in_specs=[specs.get(n, None) or whole(o) for n, o in enumerate(operands)],
        out_specs=out_specs or [whole(o) for o in outs],
        out_shape=outs,
        input_output_aliases=aliases or {},
        cost_estimate=pl.CostEstimate(flops=0, bytes_accessed=2 * moved, transcendentals=0),
        compiler_params=pltpu.CompilerParams(vmem_limit_bytes=8 * 2**20),
    )(*operands)


SIDE = shape(2, EXT, PROBE)


def pack_kernel(jobs, tile, *refs):
    outs, sems = refs[:-1], refs[-1]
    copies = [
        pltpu.make_async_copy(tile.at[:, layer, rows, cols], out, sems.at[n])
        for n, ((layer, rows, cols), out) in enumerate(zip(jobs, outs))
    ]
    for copy in copies:
        copy.start()
    for copy in copies:
        copy.wait()


def pack(object_field, jobs, outs):
    return pl.pallas_call(
        functools.partial(pack_kernel, jobs),
        in_specs=[pl.BlockSpec(memory_space=pltpu.HBM)],
        out_specs=[pl.BlockSpec(memory_space=pltpu.VMEM)] * len(outs),
        out_shape=outs,
        scratch_shapes=[pltpu.SemaphoreType.DMA((len(outs),))],
        name="pack",
        cost_estimate=pl.CostEstimate(flops=0, bytes_accessed=4 * 2**18, transcendentals=0),
        compiler_params=pltpu.CompilerParams(vmem_limit_bytes=4 * 2**20),
    )(object_field)


def prepare_kernel(probe, propagator, tables, phase, copied):
    phase[:2] = probe[...]
    phase[2] = jnp.cos(propagator[...])
    phase[3] = jnp.sin(propagator[...])
    h = PROBE
    copied[:2] = tables[...]
    copied[2:, :h, :h] = tables[:, :h, :h]
    copied[2:, :h, h:] = tables[:, h:, :h]
    copied[2:, h:, :h] = tables[:, :h, h:]
    copied[2:, h:, h:] = tables[:, h:, h:]


def prepare(probe, propagator):
    tables = jnp.asarray(dft_tables())
    outs = [shape(4, PROBE, PROBE), jax.ShapeDtypeStruct((4, 2 * PROBE, 2 * PROBE), BF16)]
    return plain(prepare_kernel, outs, [probe, propagator, tables])


def sums_kernel(count, left, middle, low, right, *refs):
    h, t = PROBE, TILE
    even_out, odd_out = refs[-2:]
    from_left, from_right = refs[:count] if count else (None, None)

    def total(own, other, rows):
        return own[:, rows] if other is None else own[:, rows] + other[:, rows]

    def fill(down, up):
        down[:, :, :h] = total(left, from_left, slice(t, t + h))
        up[:, :, :h] = total(left, from_left, slice(0, h))
        down[:, :, h:t] = low[...]
        up[:, :, h:t] = middle[:, :h]
        down[:, :, t:] = total(right, from_right, slice(t, t + h))
        up[:, :, t:] = total(right, from_right, slice(0, h))

    parity = lax.axis_index("row") & 1

    @pl.when(parity == 0)
    def _():
        fill(even_out, odd_out)

    @pl.when(parity == 1)
    def _():
        fill(odd_out, even_out)


def sums(grad, columns):
    body = functools.partial(sums_kernel, len(columns))
    return plain(body, [shape(2, PROBE, EXT)] * 2, [*grad, *columns])


class Chosen:
    def __init__(self, for_even, for_odd):
        self.pair = for_even, for_odd

    def __getitem__(self, where):
        odd_row = (lax.axis_index("row") & 1) == 1
        return jnp.where(odd_row, self.pair[1][where], self.pair[0][where])


def edges_kernel(left, right, even, odd, west, east):
    h, t = PROBE, TILE
    above, below = Chosen(odd, even), Chosen(even, odd)
    for out, own, cols in ((west, left, slice(0, h)), (east, right, slice(t, t + h))):
        out[:, :h] = own[:, :h] + above[:, :, cols]
        out[:, h:t] = own[:, h:t]
        out[:, t:] = own[:, t:] + below[:, :, cols]


def update_kernel(rows_first, tile, low_left, low_right, side, corner, left, middle, bottom, right, *refs):
    from_left, from_right, even, odd, new_l, new_m, new_r = refs
    h, t = PROBE, TILE
    above, below = Chosen(odd, even), Chosen(even, odd)
    first, second, third = slice(0, h), slice(h, t), slice(t, t + h)
    top, mid, end = first, second, third

    def side_sum(own, other, rows, cols):
        total = own[:, rows] + other[:, rows]
        if rows_first or rows is mid:
            return total
        return total + (above if rows is top else below)[:, :, cols]

    new_l[:, top] = tile[:, 0, top, first] - STEP * side_sum(left, from_left, top, first)
    new_l[:, mid] = tile[:, 0, mid, first] - STEP * side_sum(left, from_left, mid, first)
    new_l[:, end] = low_left[...] - STEP * side_sum(left, from_left, end, first)
    new_m[:, top] = tile[:, 0, top, second] - STEP * (middle[:, top] + above[:, :, second])
    new_m[:, mid] = tile[:, 0, mid, second] - STEP * middle[:, mid]
    new_m[:, end] = low_right[...] - STEP * (bottom[...] + below[:, :, second])
    new_r[:, top] = side[:, top] - STEP * side_sum(right, from_right, top, third)
    new_r[:, mid] = side[:, mid] - STEP * side_sum(right, from_right, mid, third)
    new_r[:, end] = corner[...] - STEP * side_sum(right, from_right, end, third)


def update(layer, field, grad, columns, even, odd, rows_first):
    operands = [*field, *grad, *columns, even, odd]
    specs = field_specs(0, layer, fill_first)
    body = functools.partial(update_kernel, rows_first)
    return plain(body, [SIDE] * 3, operands, specs)


def spill_kernel(left, from_left, down):
    rows = from_left.shape[1]
    down[...] = left[:, TILE:] + from_left[:, rows - PROBE :]


def join_kernel(left, low, right, down):
    h, t = PROBE, TILE
    down[:, :, :h] = left[:, t:]
    down[:, :, h:t] = low[...]
    down[:, :, t:] = right[:, t:]


def east_kernel(right, above, east):
    h, t = PROBE, TILE
    east[:, :h] = right[:, :h] + above[:, :, t:]
    east[:, h:] = right[:, h:t]


def last_kernel(whole_rows, *refs):
    old_l, old_m, left, middle, from_left = refs[:5]
    out, h, t = refs[-1], PROBE, TILE
    if whole_rows:
        above_l, above_m = refs[5][:, :, :h], refs[5][:, :, h:t]
    else:
        above_l, above_m = refs[5][...], refs[6][...]
    out[:, 0, :h, :h] = old_l[:, :h] - STEP * (left[:, :h] + from_left[:, :h] + above_l)
    out[:, 0, h:, :h] = old_l[:, h:t] - STEP * (left[:, h:t] + from_left[:, h:t])
    out[:, 0, :h, h:] = old_m[:, :h] - STEP * (middle[:, :h] + above_m)
    out[:, 0, h:, h:] = old_m[:, h:t] - STEP * middle[:, h:t]


def last(layer, piece, above, result):
    operands = [*piece, *above]
    specs, aliases = {}, {}
    if result is not None:
        specs, aliases = {len(operands): pl.BlockSpec(memory_space=pl.ANY)}, {len(operands): 0}
        operands.append(result)
    return plain(
        functools.partial(last_kernel, len(above) == 1),
        [shape(2, SLICES, TILE, TILE)],
        operands,
        specs,
        aliases,
        [tile_of(layer)],
    )[0]


def on_device(object_field, probe, propagator, measured, offsets):
    h, t = PROBE, TILE
    phase, tables = prepare(probe, propagator)
    offsets = jnp.swapaxes(offsets, 2, 3).reshape(2, POS)
    intensity = measured.reshape(POS, h, h)

    top, all_rows, west_half, east_half, rest = pl.ds(0, h), pl.ds(0, t), pl.ds(0, h), pl.ds(h, h), pl.ds(1, 2)
    rows0 = object_field[:, 0, :h]
    cols0, west_rows, east_rows, cols12 = pack(
        object_field,
        [(0, all_rows, west_half), (rest, top, west_half), (rest, top, east_half), (rest, all_rows, west_half)],
        [shape(2, t, h), shape(2, 2, h, h), shape(2, 2, h, h), shape(2, 2, t, h)],
    )
    low0 = shifted(rows0, "row", -1)
    low_west = shifted(west_rows, "row", -1)
    low_east = shifted(east_rows, "row", -1)
    right0 = shifted(cols0, "col", -1)
    right12 = shifted(cols12, "col", -1)
    corner0 = shifted(low0[:, :, :h], "col", -1)
    corner12 = shifted(low_west, "col", -1)
    fields = [
        [object_field, low0, low0, right0, corner0],
        [object_field, low_west, low_east, right12, corner12],
        [object_field, low_west, low_east, right12, corner12],
    ]

    def gradients(fields, fill):
        _, wave1 = forward(offsets, tables, phase, None, fields[0], 0, fill)
        win1, wave2 = forward(offsets, tables, phase, wave1, fields[1], 1, fill)
        *grad2, back = turn(offsets, tables, intensity, wave2, fields[2], 2, fill)
        *grad1, back = backward(offsets, tables, phase, back, wave1, win1)
        grad0 = backward(offsets, tables, phase, back, None, None)
        return [grad0, grad1, grad2]

    grads = gradients(fields, fill_first)
    renewed = [None] * SLICES

    def columns(west, east):
        from_left = shifted(east, "col", 1)
        from_right = shifted(west, "col", -1)
        return [from_left, from_right]

    for layer in (1, 0, 2):
        grad, rows_first = grads[layer], layer == 1
        moved = [] if rows_first else columns(grad[0], grad[3])
        for_even, for_odd = sums(grad, moved)
        even = swapped(for_even, 0)
        odd = swapped(for_odd, 1)
        if rows_first:
            west, east = plain(edges_kernel, [SIDE] * 2, [grad[0], grad[3], even, odd])
            moved = columns(west, east)
            grad = [west, grad[1], grad[2], east]
        renewed[layer] = list(update(layer, fields[layer], grad, moved, even, odd, rows_first))
    grads = gradients(renewed, fill_next)
    from_left, above_m, above_l = {}, {}, {}
    down = plain(join_kernel, [shape(2, h, EXT)], [grads[2][0], grads[2][2], grads[2][3]])[0]
    above2 = shifted(down, "row", 1)
    east = plain(east_kernel, [shape(2, t, h)], [grads[2][3], above2])[0]
    from_left[2] = shifted(east, "col", 1)
    for layer in (1, 0):
        right = grads[layer][3]
        from_left[layer] = shifted(right if layer else right[:, t:], "col", 1)
        above_m[layer] = shifted(grads[layer][2], "row", 1)
        down = plain(spill_kernel, [shape(2, h, h)], [grads[layer][0], from_left[layer]])[0]
        above_l[layer] = shifted(down, "row", 1)
    from_left[0] = shifted(grads[0][3][:, :t], "col", 1)
    pieces = [(renewed[n][0], renewed[n][1], grads[n][0], grads[n][1], from_left[n]) for n in range(SLICES)]
    result = last(2, pieces[2], [above2], None)
    result = last(1, pieces[1], [above_l[1], above_m[1]], result)
    return last(0, pieces[0], [above_l[0], above_m[0]], result)


def solution(mesh):
    placed = (
        P(None, None, "row", "col"),
        P(),
        P(),
        P("row", "col", None, None, None),
        P("row", "col", None, None),
    )
    return jax.shard_map(
        on_device,
        mesh=mesh,
        in_specs=placed,
        out_specs=P(None, None, "row", "col"),
        check_vma=False,
    )
```

```python
import functools
import math

import jax
import jax.numpy as jnp
import numpy as np
from jax import lax
from jax.experimental import pallas as pl
from jax.experimental.pallas import tpu as pltpu
from jax.sharding import PartitionSpec as P


PROBE = 128
SLICES = 3
POS = 6
TILE = 256
EXT = TILE + PROBE
SUB = 8
STEP = 0.05
F32 = jnp.float32
BF16 = jnp.bfloat16


def dft_tables():
    index = np.arange(PROBE)
    angle = (index[:, None] * index[None, :] % PROBE) * (-2.0 * math.pi / PROBE)
    cosines, sines = np.cos(angle) / math.sqrt(PROBE), np.sin(angle) / math.sqrt(PROBE)
    right = np.block([[cosines, sines], [-sines, cosines]]).astype(np.float32)
    high = right.astype(BF16)
    return np.stack([high, (right - high.astype(np.float32)).astype(BF16)])


def split(value):
    high = value.astype(BF16)
    return high, (value - high.astype(F32)).astype(BF16)


def dot(a, b):
    return jnp.dot(a, b, preferred_element_type=F32)


def times_right(block, table):
    high, low = block
    wide, fine = table
    return dot(jnp.concatenate([high, low, high], axis=1), jnp.concatenate([wide, wide, fine], axis=0))


def times_left(block, table):
    high, low = block
    wide, fine = table
    return dot(jnp.concatenate([wide, wide, fine], axis=1), jnp.concatenate([high, low, high], axis=0))


def side_to_stack(block):
    h = PROBE
    top = jnp.concatenate([block[:h, :h], block[h:, :h]], axis=1)
    low = jnp.concatenate([block[:h, h:], block[h:, h:]], axis=1)
    return jnp.concatenate([top, low], axis=0)


def times_phase(block, phase_real, phase_imag):
    h = PROBE
    re, im = block[:h], block[h:]
    pr = jnp.concatenate([phase_real, phase_real], axis=1)
    pi = jnp.concatenate([phase_imag, phase_imag], axis=1)
    return jnp.concatenate([re * pr - im * pi, re * pi + im * pr], axis=0)


def keep(work, n, slot, block):
    work[slot, n, 0], work[slot, n, 1] = split(block)


def kept(work, n, slot):
    return work[slot, n, 0], work[slot, n, 1]


PAIRS = POS // 2


def propagate(work, right, left, phase_real, phase_imag, finish):
    for n in range(PAIRS):
        keep(work, n, 1, side_to_stack(times_right(kept(work, n, 0), right)))
    for n in range(PAIRS):
        keep(work, n, 0, times_phase(times_left(kept(work, n, 1), left), phase_real, phase_imag))
    for n in range(PAIRS):
        keep(work, n, 1, side_to_stack(times_left(kept(work, n, 0), right)))
    for n in range(PAIRS):
        finish(n, times_right(kept(work, n, 1), left))


def tables_of(table_ref):
    right = (table_ref[0], table_ref[1])
    left = (table_ref[2], table_ref[3])
    return right, left


def pair_of(ref, p):
    top = jnp.concatenate([ref[0, p], ref[1, p]], axis=1)
    low = jnp.concatenate([ref[0, p + 1], ref[1, p + 1]], axis=1)
    return jnp.concatenate([top, low], axis=0)


def put_pair(ref, p, block):
    h = PROBE
    ref[0, p] = block[:h, :h]
    ref[1, p] = block[:h, h:]
    ref[0, p + 1] = block[h:, :h]
    ref[1, p + 1] = block[h:, h:]


def place(offset_ref, p):
    row, col = offset_ref[0, p], offset_ref[1, p]
    over = lax.rem(row, SUB)
    base = jnp.where(col >= PROBE, PROBE, 0)
    return pl.multiple_of(row - over, SUB), over, pl.multiple_of(base, PROBE), col - base


TALL = PROBE + SUB


def lanes(rows):
    return lax.broadcasted_iota(jnp.int32, (rows, PROBE), 1)


def take_window(ext, offset_ref, p, part):
    row, over, base, shift = place(offset_ref, p)
    after = pl.multiple_of(base + PROBE, PROBE)
    first = ext[part, pl.ds(row, TALL), pl.ds(base, PROBE)]
    second = ext[part, pl.ds(row, TALL), pl.ds(after, PROBE)]
    block = jnp.where(lanes(TALL) >= shift, first, second)
    block = pltpu.roll(block, jnp.where(shift == 0, 0, PROBE - shift), 1)
    return pltpu.roll(block, jnp.where(over == 0, 0, TALL - over), 0)[:PROBE]


def turn_window(offset_ref, p, value):
    _, over, _, shift = place(offset_ref, p)
    block = jnp.concatenate([value, jnp.zeros((SUB, PROBE), F32)], axis=0)
    return pltpu.roll(pltpu.roll(block, over, 0), shift, 1)


def add_windows(grads, offset_ref, turned):
    for p in range(POS):
        row, _, base, shift = place(offset_ref, p)
        after = pl.multiple_of(base + PROBE, PROBE)
        here = lanes(TALL) >= shift
        for part in range(2):
            block = turned[part, p]
            where = (pl.ds(row, TALL), pl.ds(base, PROBE))
            grads[part][where] = grads[part][where] + jnp.where(here, block, 0.0)
            where = (pl.ds(row, TALL), pl.ds(after, PROBE))
            grads[part][where] = grads[part][where] + jnp.where(here, 0.0, block)


def times(ar, ai, br, bi):
    return ar * br - ai * bi, ar * bi + ai * br


def times_conj(ar, ai, br, bi):
    return ar * br + ai * bi, ar * bi - ai * br


def fill_first(ext, refs):
    tile, low_left, low_right, right, corner = refs
    t, h = TILE, PROBE
    ext[:, :t, :t] = tile[:, 0]
    ext[:, t:, :h] = low_left[...]
    ext[:, t:, h:t] = low_right[...]
    ext[:, :t, t:] = right[...]
    ext[:, t:, t:] = corner[...]


def fill_next(ext, refs):
    left, middle, right = refs
    t, h = TILE, PROBE
    ext[:, :, :h] = left[...]
    ext[:, :, h:t] = middle[...]
    ext[:, :, t:] = right[...]


def forward_kernel(fill, n_field, first, *refs):
    offset_ref, table_ref, phase_ref = refs[:3]
    wave = None if first else refs[3]
    field = refs[4 - first : 4 - first + n_field]
    windows, out, ext, work = refs[4 - first + n_field :]
    fill(ext, field)
    right, left = tables_of(table_ref)
    for n in range(PAIRS):
        rows = []
        for q in (2 * n, 2 * n + 1):
            tr = take_window(ext, offset_ref, q, 0)
            ti = take_window(ext, offset_ref, q, 1)
            windows[0, q] = tr
            windows[1, q] = ti
            if first:
                wr, wi = phase_ref[0], phase_ref[1]
            else:
                wr, wi = wave[0, q], wave[1, q]
            rows.append(jnp.concatenate(times(wr, wi, tr, ti), axis=1))
        keep(work, n, 0, jnp.concatenate(rows, axis=0))

    def finish(n, block):
        put_pair(out, 2 * n, block)

    propagate(work, right, left, phase_ref[2], phase_ref[3], finish)


def write_gradient(grads, outs):
    left, middle, low, right = outs
    h, t = PROBE, TILE
    for part in range(2):
        left[part] = grads[part][:, :h]
        middle[part] = grads[part][:t, h:t]
        low[part] = grads[part][t:, h:t]
        right[part] = grads[part][:, t:]


def turn_kernel(fill, n_field, *refs):
    offset_ref, table_ref, intensity, wave = refs[:4]
    field = refs[4 : 4 + n_field]
    outs = refs[4 + n_field : 8 + n_field]
    back, ext, windows, work, turned, *grads = refs[8 + n_field :]
    fill(ext, field)
    for part in grads:
        part[...] = jnp.zeros_like(part)
    right, left = tables_of(table_ref)
    h = PROBE
    for n in range(PAIRS):
        rows = []
        for q in (2 * n, 2 * n + 1):
            tr = take_window(ext, offset_ref, q, 0)
            ti = take_window(ext, offset_ref, q, 1)
            windows[0, q] = tr
            windows[1, q] = ti
            rows.append(jnp.concatenate(times(wave[0, q], wave[1, q], tr, ti), axis=1))
        keep(work, n, 0, jnp.concatenate(rows, axis=0))
    for n in range(PAIRS):
        keep(work, n, 1, side_to_stack(times_right(kept(work, n, 0), right)))
    for n in range(PAIRS):
        block = times_left(kept(work, n, 1), left)
        re, im = block[:h], block[h:]
        target = jnp.concatenate([intensity[2 * n], intensity[2 * n + 1]], axis=1)
        weight = 4.0 * (re * re + im * im - target)
        keep(work, n, 0, jnp.concatenate([re * weight, im * weight], axis=0))
    for n in range(PAIRS):
        keep(work, n, 1, side_to_stack(times_left(kept(work, n, 0), right)))
    for n in range(PAIRS):
        block = times_right(kept(work, n, 1), left)
        for i in range(2):
            q = 2 * n + i
            gr, gi = block[i * h : (i + 1) * h, :h], block[i * h : (i + 1) * h, h:]
            br, bi = times_conj(windows[0, q], windows[1, q], gr, gi)
            back[0, q] = br
            back[1, q] = bi
            dr, di = times_conj(wave[0, q], wave[1, q], gr, gi)
            turned[0, q] = turn_window(offset_ref, q, dr)
            turned[1, q] = turn_window(offset_ref, q, di)
    add_windows(grads, offset_ref, turned)
    write_gradient(grads, outs)


def backward_kernel(first, *refs):
    if first:
        offset_ref, table_ref, phase_ref, back_in = refs[:4]
        outs = refs[4:8]
    else:
        offset_ref, table_ref, phase_ref, back_in, wave, windows = refs[:6]
        outs, back = refs[6:10], refs[10]
    work, turned, *grads = refs[-4:]
    for part in grads:
        part[...] = jnp.zeros_like(part)
    right, left = tables_of(table_ref)
    h = PROBE
    for n in range(PAIRS):
        keep(work, n, 0, pair_of(back_in, 2 * n))

    def finish(n, block):
        for i in range(2):
            q = 2 * n + i
            gr, gi = block[i * h : (i + 1) * h, :h], block[i * h : (i + 1) * h, h:]
            if first:
                dr, di = times_conj(phase_ref[0], phase_ref[1], gr, gi)
            else:
                br, bi = times_conj(windows[0, q], windows[1, q], gr, gi)
                back[0, q] = br
                back[1, q] = bi
                dr, di = times_conj(wave[0, q], wave[1, q], gr, gi)
            turned[0, q] = turn_window(offset_ref, q, dr)
            turned[1, q] = turn_window(offset_ref, q, di)

    propagate(work, right, left, phase_ref[2], -phase_ref[3], finish)
    add_windows(grads, offset_ref, turned)
    write_gradient(grads, outs)


def whole(array):
    rank = len(array.shape)
    return pl.BlockSpec(array.shape, lambda i: (0,) * rank)


def tile_of(layer):
    return pl.BlockSpec((2, 1, TILE, TILE), lambda i: (0, layer, 0, 0))


def shape(*dims):
    return jax.ShapeDtypeStruct(dims, F32)


STACK = (2, POS, PROBE, PROBE)
GRADIENT = [
    shape(2, EXT, PROBE),
    shape(2, TILE, PROBE),
    shape(2, PROBE, PROBE),
    shape(2, EXT, PROBE),
]
WORK = pltpu.VMEM((2, PAIRS, 2, 256, 256), BF16)
SCRATCH = pltpu.VMEM((2, EXT, EXT), F32)
GRADS = [pltpu.VMEM((2, POS, TALL, PROBE), F32)] + [pltpu.VMEM((EXT, EXT), F32)] * 2


def run(body, operands, outs, scratch, stages, specs=None):
    specs = specs or {}
    flops = stages * POS * PROBE * 256 * 256 * 2 * 3
    moved = sum(math.prod(o.shape) * 4 for o in operands) + sum(math.prod(o.shape) * 4 for o in outs)
    in_specs = [pl.BlockSpec(memory_space=pltpu.SMEM)]
    in_specs += [specs.get(n, None) or whole(o) for n, o in enumerate(operands) if n > 0]
    return pl.pallas_call(
        body,
        grid=(1,),
        in_specs=in_specs,
        out_specs=[whole(o) for o in outs],
        out_shape=outs,
        scratch_shapes=scratch,
        cost_estimate=pl.CostEstimate(flops=flops, bytes_accessed=moved, transcendentals=0),
        compiler_params=pltpu.CompilerParams(vmem_limit_bytes=14 * 2**20),
    )(*operands)


def field_specs(start, layer, fill):
    if fill is not fill_first:
        return {}
    h, t = PROBE, TILE
    if layer == 0:
        lows = [pl.BlockSpec((2, h, h), lambda i: (0, 0, 0)), pl.BlockSpec((2, h, h), lambda i: (0, 0, 1))]
        sides = [None, None]
    else:
        low = pl.BlockSpec((2, None, h, h), lambda i: (0, layer - 1, 0, 0))
        lows, sides = [low, low], [pl.BlockSpec((2, None, t, h), lambda i: (0, layer - 1, 0, 0)), low]
    return {start + n: spec for n, spec in enumerate([tile_of(layer), *lows, *sides])}


def forward(offsets, tables, phase, wave, field, layer, fill):
    first = wave is None
    operands = [offsets, tables, phase] + ([] if first else [wave])
    specs = field_specs(len(operands), layer, fill)
    body = functools.partial(forward_kernel, fill, len(field), first)
    return run(body, operands + field, [shape(*STACK)] * 2, [SCRATCH, WORK], 4, specs)


def turn(offsets, tables, intensity, wave, field, layer, fill):
    operands = [offsets, tables, intensity, wave]
    specs = field_specs(len(operands), layer, fill)
    body = functools.partial(turn_kernel, fill, len(field))
    scratch = [SCRATCH, pltpu.VMEM(STACK, F32), WORK, *GRADS]
    return run(body, operands + field, [*GRADIENT, shape(*STACK)], scratch, 4, specs)


def backward(offsets, tables, phase, back, wave, windows):
    first = wave is None
    operands = [offsets, tables, phase, back] + ([] if first else [wave, windows])
    outs = [*GRADIENT] if first else [*GRADIENT, shape(*STACK)]
    return run(functools.partial(backward_kernel, first), operands, outs, [WORK, *GRADS], 4)


def shifted(block, axis, distance):
    size = lax.axis_size(axis)
    return lax.ppermute(block, axis, [((i - distance) % size, i) for i in range(size)])


def swapped(block, odd):
    size = lax.axis_size("row")
    route = []
    for i in range(odd, size + odd, 2):
        route += [(i % size, (i + 1) % size), ((i + 1) % size, i % size)]
    return lax.ppermute(block, "row", sorted(route))


def plain(body, outs, operands, specs=None, aliases=None, out_specs=None):
    specs = specs or {}
    moved = sum(math.prod(o.shape) * 4 for o in outs)
    return pl.pallas_call(
        body,
        grid=(1,),
        in_specs=[specs.get(n, None) or whole(o) for n, o in enumerate(operands)],
        out_specs=out_specs or [whole(o) for o in outs],
        out_shape=outs,
        input_output_aliases=aliases or {},
        cost_estimate=pl.CostEstimate(flops=0, bytes_accessed=2 * moved, transcendentals=0),
        compiler_params=pltpu.CompilerParams(vmem_limit_bytes=8 * 2**20),
    )(*operands)


SIDE = shape(2, EXT, PROBE)


def pack_kernel(jobs, tile, *refs):
    outs, sems = refs[:-1], refs[-1]
    copies = [
        pltpu.make_async_copy(tile.at[:, layer, rows, cols], out, sems.at[n])
        for n, ((layer, rows, cols), out) in enumerate(zip(jobs, outs))
    ]
    for copy in copies:
        copy.start()
    for copy in copies:
        copy.wait()


def pack(object_field, jobs, outs):
    return pl.pallas_call(
        functools.partial(pack_kernel, jobs),
        in_specs=[pl.BlockSpec(memory_space=pltpu.HBM)],
        out_specs=[pl.BlockSpec(memory_space=pltpu.VMEM)] * len(outs),
        out_shape=outs,
        scratch_shapes=[pltpu.SemaphoreType.DMA((len(outs),))],
        name="pack",
        cost_estimate=pl.CostEstimate(flops=0, bytes_accessed=4 * 2**18, transcendentals=0),
        compiler_params=pltpu.CompilerParams(vmem_limit_bytes=4 * 2**20),
    )(object_field)


def prepare_kernel(probe, propagator, tables, phase, copied):
    phase[:2] = probe[...]
    phase[2] = jnp.cos(propagator[...])
    phase[3] = jnp.sin(propagator[...])
    h = PROBE
    copied[:2] = tables[...]
    copied[2:, :h, :h] = tables[:, :h, :h]
    copied[2:, :h, h:] = tables[:, h:, :h]
    copied[2:, h:, :h] = tables[:, :h, h:]
    copied[2:, h:, h:] = tables[:, h:, h:]


def prepare(probe, propagator):
    tables = jnp.asarray(dft_tables())
    outs = [shape(4, PROBE, PROBE), jax.ShapeDtypeStruct((4, 2 * PROBE, 2 * PROBE), BF16)]
    return plain(prepare_kernel, outs, [probe, propagator, tables])


def sums_kernel(count, left, middle, low, right, *refs):
    h, t = PROBE, TILE
    even_out, odd_out = refs[-2:]
    from_left, from_right = (*refs[:count], None, None)[:2]

    def total(own, other, rows):
        return own[:, rows] if other is None else own[:, rows] + other[:, rows]

    def fill(down, up):
        down[:, :, :h] = total(left, from_left, slice(t, t + h))
        up[:, :, :h] = total(left, from_left, slice(0, h))
        down[:, :, h:t] = low[...]
        up[:, :, h:t] = middle[:, :h]
        if count != 1:
            down[:, :, t:] = total(right, from_right, slice(t, t + h))
            up[:, :, t:] = total(right, from_right, slice(0, h))

    parity = lax.axis_index("row") & 1

    @pl.when(parity == 0)
    def _():
        fill(even_out, odd_out)

    @pl.when(parity == 1)
    def _():
        fill(odd_out, even_out)


def sums(grad, columns):
    width = TILE if len(columns) == 1 else EXT
    body = functools.partial(sums_kernel, len(columns))
    return plain(body, [shape(2, PROBE, width)] * 2, [*grad, *columns])


class Chosen:
    def __init__(self, for_even, for_odd):
        self.pair = for_even, for_odd

    def __getitem__(self, where):
        odd_row = (lax.axis_index("row") & 1) == 1
        return jnp.where(odd_row, self.pair[1][where], self.pair[0][where])


def edges_kernel(left, right, even, odd, west, east):
    h, t = PROBE, TILE
    above, below = Chosen(odd, even), Chosen(even, odd)
    for out, own, cols in ((west, left, slice(0, h)), (east, right, slice(t, t + h))):
        out[:, :h] = own[:, :h] + above[:, :, cols]
        out[:, h:t] = own[:, h:t]
        out[:, t:] = own[:, t:] + below[:, :, cols]


def update_kernel(rows_first, narrow, tile, low_left, low_right, side, corner, left, middle, bottom, right, *refs):
    if narrow:
        from_left, even, odd, new_l, new_m = refs
    else:
        from_left, from_right, even, odd, new_l, new_m, new_r = refs
    h, t = PROBE, TILE
    above, below = Chosen(odd, even), Chosen(even, odd)
    first, second, third = slice(0, h), slice(h, t), slice(t, t + h)
    top, mid, end = first, second, third

    def side_sum(own, other, rows, cols):
        total = own[:, rows] + other[:, rows]
        if rows_first or rows is mid:
            return total
        return total + (above if rows is top else below)[:, :, cols]

    new_l[:, top] = tile[:, 0, top, first] - STEP * side_sum(left, from_left, top, first)
    new_l[:, mid] = tile[:, 0, mid, first] - STEP * side_sum(left, from_left, mid, first)
    new_l[:, end] = low_left[...] - STEP * side_sum(left, from_left, end, first)
    new_m[:, top] = tile[:, 0, top, second] - STEP * (middle[:, top] + above[:, :, second])
    new_m[:, mid] = tile[:, 0, mid, second] - STEP * middle[:, mid]
    new_m[:, end] = low_right[...] - STEP * (bottom[...] + below[:, :, second])
    if narrow:
        return
    new_r[:, top] = side[:, top] - STEP * side_sum(right, from_right, top, third)
    new_r[:, mid] = side[:, mid] - STEP * side_sum(right, from_right, mid, third)
    new_r[:, end] = corner[...] - STEP * side_sum(right, from_right, end, third)


def update(layer, field, grad, columns, even, odd, rows_first):
    operands = [*field, *grad, *columns, even, odd]
    specs = field_specs(0, layer, fill_first)
    narrow = len(columns) == 1
    body = functools.partial(update_kernel, rows_first, narrow)
    return plain(body, [SIDE] * (2 if narrow else 3), operands, specs)


def spill_kernel(left, from_left, down):
    rows = from_left.shape[1]
    down[...] = left[:, TILE:] + from_left[:, rows - PROBE :]


def join_kernel(left, low, right, down):
    h, t = PROBE, TILE
    down[:, :, :h] = left[:, t:]
    down[:, :, h:t] = low[...]
    down[:, :, t:] = right[:, t:]


def both_kernel(first, second, down):
    down[0] = first[...]
    down[1] = second[...]


def east_kernel(right, above, east):
    h, t = PROBE, TILE
    east[:, :h] = right[:, :h] + above[:, :, t:]
    east[:, h:] = right[:, h:t]


def last_kernel(whole_rows, *refs):
    old_l, old_m, left, middle, from_left = refs[:5]
    out, h, t = refs[-1], PROBE, TILE
    if whole_rows:
        above_l, above_m = refs[5][:, :, :h], refs[5][:, :, h:t]
    else:
        above_l, above_m = refs[5][...], refs[6][...]
    out[:, 0, :h, :h] = old_l[:, :h] - STEP * (left[:, :h] + from_left[:, :h] + above_l)
    out[:, 0, h:, :h] = old_l[:, h:t] - STEP * (left[:, h:t] + from_left[:, h:t])
    out[:, 0, :h, h:] = old_m[:, :h] - STEP * (middle[:, :h] + above_m)
    out[:, 0, h:, h:] = old_m[:, h:t] - STEP * middle[:, h:t]


def last(layer, piece, above, result):
    operands = [*piece, *above]
    specs, aliases = {}, {}
    if len(above) == 2:
        specs[6] = pl.BlockSpec((None, 2, PROBE, PROBE), lambda i: (layer, 0, 0, 0))
    if result is not None:
        specs[len(operands)], aliases = pl.BlockSpec(memory_space=pl.ANY), {len(operands): 0}
        operands.append(result)
    return plain(
        functools.partial(last_kernel, len(above) == 1),
        [shape(2, SLICES, TILE, TILE)],
        operands,
        specs,
        aliases,
        [tile_of(layer)],
    )[0]


def on_device(object_field, probe, propagator, measured, offsets):
    h, t = PROBE, TILE
    phase, tables = prepare(probe, propagator)
    offsets = jnp.swapaxes(offsets, 2, 3).reshape(2, POS)
    intensity = measured.reshape(POS, h, h)

    top, all_rows, west_half, east_half, rest = pl.ds(0, h), pl.ds(0, t), pl.ds(0, h), pl.ds(h, h), pl.ds(1, 2)
    rows0 = object_field[:, 0, :h]
    cols0, west_rows, east_rows, cols12 = pack(
        object_field,
        [(0, all_rows, west_half), (rest, top, west_half), (rest, top, east_half), (rest, all_rows, west_half)],
        [shape(2, t, h), shape(2, 2, h, h), shape(2, 2, h, h), shape(2, 2, t, h)],
    )
    low0 = shifted(rows0, "row", -1)
    low_west = shifted(west_rows, "row", -1)
    low_east = shifted(east_rows, "row", -1)
    right0 = shifted(cols0, "col", -1)
    right12 = shifted(cols12, "col", -1)
    corner0 = shifted(low0[:, :, :h], "col", -1)
    corner12 = shifted(low_west, "col", -1)
    fields = [
        [object_field, low0, low0, right0, corner0],
        [object_field, low_west, low_east, right12, corner12],
        [object_field, low_west, low_east, right12, corner12],
    ]

    def gradients(fields, fill):
        _, wave1 = forward(offsets, tables, phase, None, fields[0], 0, fill)
        win1, wave2 = forward(offsets, tables, phase, wave1, fields[1], 1, fill)
        *grad2, back = turn(offsets, tables, intensity, wave2, fields[2], 2, fill)
        *grad1, back = backward(offsets, tables, phase, back, wave1, win1)
        grad0 = backward(offsets, tables, phase, back, None, None)
        return [grad0, grad1, grad2]

    grads = gradients(fields, fill_first)
    renewed = [None] * SLICES

    def columns(west, east, layer):
        from_left = shifted(east, "col", 1)
        if layer == 1:
            return [from_left]
        from_right = shifted(west, "col", -1)
        return [from_left, from_right]

    for layer in (2, 1, 0):
        grad, rows_first = grads[layer], layer == 2
        moved = [] if rows_first else columns(grad[0], grad[3], layer)
        for_even, for_odd = sums(grad, moved)
        even = swapped(for_even, 0)
        odd = swapped(for_odd, 1)
        if rows_first:
            west, east = plain(edges_kernel, [SIDE] * 2, [grad[0], grad[3], even, odd])
            moved = columns(west, east, layer)
            grad = [west, grad[1], grad[2], east]
        new = list(update(layer, fields[layer], grad, moved, even, odd, rows_first))
        if layer == 1:
            new.append(shifted(new[0], "col", -1))
        renewed[layer] = new
    grads = gradients(renewed, fill_next)
    from_left, above_l = {}, {}
    down = plain(join_kernel, [shape(2, h, EXT)], [grads[2][0], grads[2][2], grads[2][3]])[0]
    above2 = shifted(down, "row", 1)
    east = plain(east_kernel, [shape(2, t, h)], [grads[2][3], above2])[0]
    from_left[2] = shifted(east, "col", 1)
    for layer in (1, 0):
        right = grads[layer][3]
        from_left[layer] = shifted(right if layer else right[:, t:], "col", 1)
        down = plain(spill_kernel, [shape(2, h, h)], [grads[layer][0], from_left[layer]])[0]
        above_l[layer] = shifted(down, "row", 1)
    down = plain(both_kernel, [shape(2, 2, h, h)], [grads[0][2], grads[1][2]])[0]
    above_m = shifted(down, "row", 1)
    from_left[0] = shifted(grads[0][3][:, :t], "col", 1)
    pieces = [(renewed[n][0], renewed[n][1], grads[n][0], grads[n][1], from_left[n]) for n in range(SLICES)]
    result = last(2, pieces[2], [above2], None)
    result = last(1, pieces[1], [above_l[1], above_m], result)
    return last(0, pieces[0], [above_l[0], above_m], result)


def solution(mesh):
    placed = (
        P(None, None, "row", "col"),
        P(),
        P(),
        P("row", "col", None, None, None),
        P("row", "col", None, None),
    )
    return jax.shard_map(
        on_device,
        mesh=mesh,
        in_specs=placed,
        out_specs=P(None, None, "row", "col"),
        check_vma=False,
    )
```

```python
import functools
import math

import jax
import jax.numpy as jnp
import numpy as np
from jax import lax
from jax.experimental import pallas as pl
from jax.experimental.pallas import tpu as pltpu
from jax.sharding import PartitionSpec as P


PROBE = 128
SLICES = 3
POS = 6
TILE = 256
EXT = TILE + PROBE
SUB = 8
STEP = 0.05
F32 = jnp.float32
BF16 = jnp.bfloat16


def dft_tables():
    index = np.arange(PROBE)
    angle = (index[:, None] * index[None, :] % PROBE) * (-2.0 * math.pi / PROBE)
    cosines, sines = np.cos(angle) / math.sqrt(PROBE), np.sin(angle) / math.sqrt(PROBE)
    right = np.block([[cosines, sines], [-sines, cosines]]).astype(np.float32)
    high = right.astype(BF16)
    return np.stack([high, (right - high.astype(np.float32)).astype(BF16)])


def split(value):
    high = value.astype(BF16)
    return high, (value - high.astype(F32)).astype(BF16)


def dot(a, b):
    return jnp.dot(a, b, preferred_element_type=F32)


def times_right(block, table):
    high, low = block
    wide, fine = table
    return dot(jnp.concatenate([high, low, high], axis=1), jnp.concatenate([wide, wide, fine], axis=0))


def times_left(block, table):
    high, low = block
    wide, fine = table
    return dot(jnp.concatenate([wide, wide, fine], axis=1), jnp.concatenate([high, low, high], axis=0))


def side_to_stack(block):
    h = PROBE
    top = jnp.concatenate([block[:h, :h], block[h:, :h]], axis=1)
    low = jnp.concatenate([block[:h, h:], block[h:, h:]], axis=1)
    return jnp.concatenate([top, low], axis=0)


def times_phase(block, phase_real, phase_imag):
    h = PROBE
    re, im = block[:h], block[h:]
    pr = jnp.concatenate([phase_real, phase_real], axis=1)
    pi = jnp.concatenate([phase_imag, phase_imag], axis=1)
    return jnp.concatenate([re * pr - im * pi, re * pi + im * pr], axis=0)


def keep(work, n, slot, block):
    work[slot, n, 0], work[slot, n, 1] = split(block)


def kept(work, n, slot):
    return work[slot, n, 0], work[slot, n, 1]


PAIRS = POS // 2


def propagate(work, right, left, phase_real, phase_imag, finish):
    for n in range(PAIRS):
        keep(work, n, 1, side_to_stack(times_right(kept(work, n, 0), right)))
    for n in range(PAIRS):
        keep(work, n, 0, times_phase(times_left(kept(work, n, 1), left), phase_real, phase_imag))
    for n in range(PAIRS):
        keep(work, n, 1, side_to_stack(times_left(kept(work, n, 0), right)))
    for n in range(PAIRS):
        finish(n, times_right(kept(work, n, 1), left))


def tables_of(table_ref):
    right = (table_ref[0], table_ref[1])
    left = (table_ref[2], table_ref[3])
    return right, left


def pair_of(ref, p):
    top = jnp.concatenate([ref[0, p], ref[1, p]], axis=1)
    low = jnp.concatenate([ref[0, p + 1], ref[1, p + 1]], axis=1)
    return jnp.concatenate([top, low], axis=0)


def put_pair(ref, p, block):
    h = PROBE
    ref[0, p] = block[:h, :h]
    ref[1, p] = block[:h, h:]
    ref[0, p + 1] = block[h:, :h]
    ref[1, p + 1] = block[h:, h:]


def place(offset_ref, p):
    row, col = offset_ref[0, p], offset_ref[1, p]
    over = lax.rem(row, SUB)
    base = jnp.where(col >= PROBE, PROBE, 0)
    return pl.multiple_of(row - over, SUB), over, pl.multiple_of(base, PROBE), col - base


TALL = PROBE + SUB


def lanes(rows):
    return lax.broadcasted_iota(jnp.int32, (rows, PROBE), 1)


def take_window(ext, offset_ref, p, part):
    row, over, base, shift = place(offset_ref, p)
    after = pl.multiple_of(base + PROBE, PROBE)
    first = ext[part, pl.ds(row, TALL), pl.ds(base, PROBE)]
    second = ext[part, pl.ds(row, TALL), pl.ds(after, PROBE)]
    block = jnp.where(lanes(TALL) >= shift, first, second)
    block = pltpu.roll(block, jnp.where(shift == 0, 0, PROBE - shift), 1)
    return pltpu.roll(block, jnp.where(over == 0, 0, TALL - over), 0)[:PROBE]


def turn_window(offset_ref, p, value):
    _, over, _, shift = place(offset_ref, p)
    block = jnp.concatenate([value, jnp.zeros((SUB, PROBE), F32)], axis=0)
    return pltpu.roll(pltpu.roll(block, over, 0), shift, 1)


def add_windows(grads, offset_ref, turned):
    for p in range(POS):
        row, _, base, shift = place(offset_ref, p)
        after = pl.multiple_of(base + PROBE, PROBE)
        here = lanes(TALL) >= shift
        for part in range(2):
            block = turned[part, p]
            where = (pl.ds(row, TALL), pl.ds(base, PROBE))
            grads[part][where] = grads[part][where] + jnp.where(here, block, 0.0)
            where = (pl.ds(row, TALL), pl.ds(after, PROBE))
            grads[part][where] = grads[part][where] + jnp.where(here, 0.0, block)


def times(ar, ai, br, bi):
    return ar * br - ai * bi, ar * bi + ai * br


def times_conj(ar, ai, br, bi):
    return ar * br + ai * bi, ar * bi - ai * br


def fill_first(ext, refs):
    tile, low_left, low_right, right, corner = refs
    t, h = TILE, PROBE
    ext[:, :t, :t] = tile[:, 0]
    ext[:, t:, :h] = low_left[...]
    ext[:, t:, h:t] = low_right[...]
    ext[:, :t, t:] = right[...]
    ext[:, t:, t:] = corner[...]


def fill_next(ext, refs):
    left, middle, right = refs
    t, h = TILE, PROBE
    ext[:, :, :h] = left[...]
    ext[:, :, h:t] = middle[...]
    ext[:, :, t:] = right[...]


def forward_kernel(fill, n_field, first, *refs):
    offset_ref, table_ref, phase_ref = refs[:3]
    wave = None if first else refs[3]
    field = refs[4 - first : 4 - first + n_field]
    windows, out, ext, work = refs[4 - first + n_field :]
    fill(ext, field)
    right, left = tables_of(table_ref)
    for n in range(PAIRS):
        rows = []
        for q in (2 * n, 2 * n + 1):
            tr = take_window(ext, offset_ref, q, 0)
            ti = take_window(ext, offset_ref, q, 1)
            windows[0, q] = tr
            windows[1, q] = ti
            if first:
                wr, wi = phase_ref[0], phase_ref[1]
            else:
                wr, wi = wave[0, q], wave[1, q]
            rows.append(jnp.concatenate(times(wr, wi, tr, ti), axis=1))
        keep(work, n, 0, jnp.concatenate(rows, axis=0))

    def finish(n, block):
        put_pair(out, 2 * n, block)

    propagate(work, right, left, phase_ref[2], phase_ref[3], finish)


def write_gradient(grads, outs):
    left, middle, low, right = outs
    h, t = PROBE, TILE
    for part in range(2):
        left[part] = grads[part][:, :h]
        middle[part] = grads[part][:t, h:t]
        low[part] = grads[part][t:, h:t]
        right[part] = grads[part][:, t:]


def turn_kernel(fill, n_field, *refs):
    offset_ref, table_ref, intensity, wave = refs[:4]
    field = refs[4 : 4 + n_field]
    outs = refs[4 + n_field : 8 + n_field]
    back, ext, windows, work, turned, *grads = refs[8 + n_field :]
    fill(ext, field)
    for part in grads:
        part[...] = jnp.zeros_like(part)
    right, left = tables_of(table_ref)
    h = PROBE
    for n in range(PAIRS):
        rows = []
        for q in (2 * n, 2 * n + 1):
            tr = take_window(ext, offset_ref, q, 0)
            ti = take_window(ext, offset_ref, q, 1)
            windows[0, q] = tr
            windows[1, q] = ti
            rows.append(jnp.concatenate(times(wave[0, q], wave[1, q], tr, ti), axis=1))
        keep(work, n, 0, jnp.concatenate(rows, axis=0))
    for n in range(PAIRS):
        keep(work, n, 1, side_to_stack(times_right(kept(work, n, 0), right)))
    for n in range(PAIRS):
        block = times_left(kept(work, n, 1), left)
        re, im = block[:h], block[h:]
        target = jnp.concatenate([intensity[2 * n], intensity[2 * n + 1]], axis=1)
        weight = 4.0 * (re * re + im * im - target)
        keep(work, n, 0, jnp.concatenate([re * weight, im * weight], axis=0))
    for n in range(PAIRS):
        keep(work, n, 1, side_to_stack(times_left(kept(work, n, 0), right)))
    for n in range(PAIRS):
        block = times_right(kept(work, n, 1), left)
        for i in range(2):
            q = 2 * n + i
            gr, gi = block[i * h : (i + 1) * h, :h], block[i * h : (i + 1) * h, h:]
            br, bi = times_conj(windows[0, q], windows[1, q], gr, gi)
            back[0, q] = br
            back[1, q] = bi
            dr, di = times_conj(wave[0, q], wave[1, q], gr, gi)
            turned[0, q] = turn_window(offset_ref, q, dr)
            turned[1, q] = turn_window(offset_ref, q, di)
    add_windows(grads, offset_ref, turned)
    write_gradient(grads, outs)


def backward_kernel(first, *refs):
    if first:
        offset_ref, table_ref, phase_ref, back_in = refs[:4]
        outs = refs[4:8]
    else:
        offset_ref, table_ref, phase_ref, back_in, wave, windows = refs[:6]
        outs, back = refs[6:10], refs[10]
    work, turned, *grads = refs[-4:]
    for part in grads:
        part[...] = jnp.zeros_like(part)
    right, left = tables_of(table_ref)
    h = PROBE
    for n in range(PAIRS):
        keep(work, n, 0, pair_of(back_in, 2 * n))

    def finish(n, block):
        for i in range(2):
            q = 2 * n + i
            gr, gi = block[i * h : (i + 1) * h, :h], block[i * h : (i + 1) * h, h:]
            if first:
                dr, di = times_conj(phase_ref[0], phase_ref[1], gr, gi)
            else:
                br, bi = times_conj(windows[0, q], windows[1, q], gr, gi)
                back[0, q] = br
                back[1, q] = bi
                dr, di = times_conj(wave[0, q], wave[1, q], gr, gi)
            turned[0, q] = turn_window(offset_ref, q, dr)
            turned[1, q] = turn_window(offset_ref, q, di)

    propagate(work, right, left, phase_ref[2], -phase_ref[3], finish)
    add_windows(grads, offset_ref, turned)
    write_gradient(grads, outs)


def whole(array):
    rank = len(array.shape)
    return pl.BlockSpec(array.shape, lambda i: (0,) * rank)


def tile_of(layer):
    return pl.BlockSpec((2, 1, TILE, TILE), lambda i: (0, layer, 0, 0))


def shape(*dims):
    return jax.ShapeDtypeStruct(dims, F32)


STACK = (2, POS, PROBE, PROBE)
GRADIENT = [
    shape(2, EXT, PROBE),
    shape(2, TILE, PROBE),
    shape(2, PROBE, PROBE),
    shape(2, EXT, PROBE),
]
WORK = pltpu.VMEM((2, PAIRS, 2, 256, 256), BF16)
SCRATCH = pltpu.VMEM((2, EXT, EXT), F32)
GRADS = [pltpu.VMEM((2, POS, TALL, PROBE), F32)] + [pltpu.VMEM((EXT, EXT), F32)] * 2


def run(body, operands, outs, scratch, stages, specs=None):
    specs = specs or {}
    flops = stages * POS * PROBE * 256 * 256 * 2 * 3
    moved = sum(math.prod(o.shape) * 4 for o in operands) + sum(math.prod(o.shape) * 4 for o in outs)
    in_specs = [pl.BlockSpec(memory_space=pltpu.SMEM)]
    in_specs += [specs.get(n, None) or whole(o) for n, o in enumerate(operands) if n > 0]
    return pl.pallas_call(
        body,
        grid=(1,),
        in_specs=in_specs,
        out_specs=[whole(o) for o in outs],
        out_shape=outs,
        scratch_shapes=scratch,
        cost_estimate=pl.CostEstimate(flops=flops, bytes_accessed=moved, transcendentals=0),
        compiler_params=pltpu.CompilerParams(vmem_limit_bytes=14 * 2**20),
    )(*operands)


def field_specs(start, layer, fill):
    if fill is not fill_first:
        return {}
    h, t = PROBE, TILE
    if layer == 0:
        lows = [pl.BlockSpec((2, h, h), lambda i: (0, 0, 0)), pl.BlockSpec((2, h, h), lambda i: (0, 0, 1))]
        sides = [None, None]
    else:
        low = pl.BlockSpec((2, None, h, h), lambda i: (0, layer - 1, 0, 0))
        lows, sides = [low, low], [pl.BlockSpec((2, None, t, h), lambda i: (0, layer - 1, 0, 0)), low]
    return {start + n: spec for n, spec in enumerate([tile_of(layer), *lows, *sides])}


def forward(offsets, tables, phase, wave, field, layer, fill):
    first = wave is None
    operands = [offsets, tables, phase] + ([] if first else [wave])
    specs = field_specs(len(operands), layer, fill)
    body = functools.partial(forward_kernel, fill, len(field), first)
    return run(body, operands + field, [shape(*STACK)] * 2, [SCRATCH, WORK], 4, specs)


def turn(offsets, tables, intensity, wave, field, layer, fill):
    operands = [offsets, tables, intensity, wave]
    specs = field_specs(len(operands), layer, fill)
    body = functools.partial(turn_kernel, fill, len(field))
    scratch = [SCRATCH, pltpu.VMEM(STACK, F32), WORK, *GRADS]
    return run(body, operands + field, [*GRADIENT, shape(*STACK)], scratch, 4, specs)


def backward(offsets, tables, phase, back, wave, windows):
    first = wave is None
    operands = [offsets, tables, phase, back] + ([] if first else [wave, windows])
    outs = [*GRADIENT] if first else [*GRADIENT, shape(*STACK)]
    return run(functools.partial(backward_kernel, first), operands, outs, [WORK, *GRADS], 4)


def shifted(block, axis, distance):
    size = lax.axis_size(axis)
    return lax.ppermute(block, axis, [((i - distance) % size, i) for i in range(size)])


def swapped(block, odd):
    size = lax.axis_size("row")
    route = []
    for i in range(odd, size + odd, 2):
        route += [(i % size, (i + 1) % size), ((i + 1) % size, i % size)]
    return lax.ppermute(block, "row", sorted(route))


def plain(body, outs, operands, specs=None, aliases=None, out_specs=None):
    specs = specs or {}
    moved = sum(math.prod(o.shape) * 4 for o in outs)
    return pl.pallas_call(
        body,
        grid=(1,),
        in_specs=[specs.get(n, None) or whole(o) for n, o in enumerate(operands)],
        out_specs=out_specs or [whole(o) for o in outs],
        out_shape=outs,
        input_output_aliases=aliases or {},
        cost_estimate=pl.CostEstimate(flops=0, bytes_accessed=2 * moved, transcendentals=0),
        compiler_params=pltpu.CompilerParams(vmem_limit_bytes=8 * 2**20),
    )(*operands)


SIDE = shape(2, EXT, PROBE)


def pack_kernel(jobs, tile, *refs):
    outs, sems = refs[:-1], refs[-1]
    copies = [
        pltpu.make_async_copy(tile.at[:, layer, rows, cols], out, sems.at[n])
        for n, ((layer, rows, cols), out) in enumerate(zip(jobs, outs))
    ]
    for copy in copies:
        copy.start()
    for copy in copies:
        copy.wait()


def pack(object_field, jobs, outs):
    return pl.pallas_call(
        functools.partial(pack_kernel, jobs),
        in_specs=[pl.BlockSpec(memory_space=pltpu.HBM)],
        out_specs=[pl.BlockSpec(memory_space=pltpu.VMEM)] * len(outs),
        out_shape=outs,
        scratch_shapes=[pltpu.SemaphoreType.DMA((len(outs),))],
        name="pack",
        cost_estimate=pl.CostEstimate(flops=0, bytes_accessed=4 * 2**18, transcendentals=0),
        compiler_params=pltpu.CompilerParams(vmem_limit_bytes=4 * 2**20),
    )(object_field)


def prepare_kernel(probe, propagator, tables, phase, copied):
    phase[:2] = probe[...]
    phase[2] = jnp.cos(propagator[...])
    phase[3] = jnp.sin(propagator[...])
    h = PROBE
    copied[:2] = tables[...]
    copied[2:, :h, :h] = tables[:, :h, :h]
    copied[2:, :h, h:] = tables[:, h:, :h]
    copied[2:, h:, :h] = tables[:, :h, h:]
    copied[2:, h:, h:] = tables[:, h:, h:]


def prepare(probe, propagator):
    tables = jnp.asarray(dft_tables())
    outs = [shape(4, PROBE, PROBE), jax.ShapeDtypeStruct((4, 2 * PROBE, 2 * PROBE), BF16)]
    return plain(prepare_kernel, outs, [probe, propagator, tables])


def sums_kernel(count, left, middle, low, right, *refs):
    h, t = PROBE, TILE
    even_out, odd_out = refs[-2:]
    from_left, from_right = (*refs[:count], None, None)[:2]

    def total(own, other, rows):
        return own[:, rows] if other is None else own[:, rows] + other[:, rows]

    def fill(down, up):
        down[:, :, :h] = total(left, from_left, slice(t, t + h))
        up[:, :, :h] = total(left, from_left, slice(0, h))
        down[:, :, h:t] = low[...]
        up[:, :, h:t] = middle[:, :h]
        if count != 1:
            down[:, :, t:] = total(right, from_right, slice(t, t + h))
            up[:, :, t:] = total(right, from_right, slice(0, h))

    parity = lax.axis_index("row") & 1

    @pl.when(parity == 0)
    def _():
        fill(even_out, odd_out)

    @pl.when(parity == 1)
    def _():
        fill(odd_out, even_out)


def sums(grad, columns):
    width = TILE if len(columns) == 1 else EXT
    body = functools.partial(sums_kernel, len(columns))
    return plain(body, [shape(2, PROBE, width)] * 2, [*grad, *columns])


class Chosen:
    def __init__(self, for_even, for_odd):
        self.pair = for_even, for_odd

    def __getitem__(self, where):
        odd_row = (lax.axis_index("row") & 1) == 1
        return jnp.where(odd_row, self.pair[1][where], self.pair[0][where])


def edges_kernel(left, right, even, odd, west, east):
    h, t = PROBE, TILE
    above, below = Chosen(odd, even), Chosen(even, odd)
    for out, own, cols in ((west, left, slice(0, h)), (east, right, slice(t, t + h))):
        out[:, :h] = own[:, :h] + above[:, :, cols]
        out[:, h:t] = own[:, h:t]
        out[:, t:] = own[:, t:] + below[:, :, cols]


def update_kernel(rows_first, narrow, tile, low_left, low_right, side, corner, left, middle, bottom, right, *refs):
    if narrow:
        from_left, even, odd, new_l, new_m = refs
    else:
        from_left, from_right, even, odd, new_l, new_m, new_r = refs
    h, t = PROBE, TILE
    above, below = Chosen(odd, even), Chosen(even, odd)
    first, second, third = slice(0, h), slice(h, t), slice(t, t + h)
    top, mid, end = first, second, third

    def side_sum(own, other, rows, cols):
        total = own[:, rows] + other[:, rows]
        if rows_first or rows is mid:
            return total
        return total + (above if rows is top else below)[:, :, cols]

    new_l[:, top] = tile[:, 0, top, first] - STEP * side_sum(left, from_left, top, first)
    new_l[:, mid] = tile[:, 0, mid, first] - STEP * side_sum(left, from_left, mid, first)
    new_l[:, end] = low_left[...] - STEP * side_sum(left, from_left, end, first)
    new_m[:, top] = tile[:, 0, top, second] - STEP * (middle[:, top] + above[:, :, second])
    new_m[:, mid] = tile[:, 0, mid, second] - STEP * middle[:, mid]
    new_m[:, end] = low_right[...] - STEP * (bottom[...] + below[:, :, second])
    if narrow:
        return
    new_r[:, top] = side[:, top] - STEP * side_sum(right, from_right, top, third)
    new_r[:, mid] = side[:, mid] - STEP * side_sum(right, from_right, mid, third)
    new_r[:, end] = corner[...] - STEP * side_sum(right, from_right, end, third)


def update(layer, field, grad, columns, even, odd, rows_first):
    operands = [*field, *grad, *columns, even, odd]
    specs = field_specs(0, layer, fill_first)
    narrow = len(columns) == 1
    body = functools.partial(update_kernel, rows_first, narrow)
    return plain(body, [SIDE] * (2 if narrow else 3), operands, specs)


def spill_kernel(left, from_left, down):
    rows = from_left.shape[1]
    down[...] = left[:, TILE:] + from_left[:, rows - PROBE :]


def join_kernel(left, low, right, down):
    h, t = PROBE, TILE
    down[:, :, :h] = left[:, t:]
    down[:, :, h:t] = low[...]
    down[:, :, t:] = right[:, t:]


def east_kernel(right, above, east):
    h, t = PROBE, TILE
    east[:, :h] = right[:, :h] + above[:, :, t:]
    east[:, h:] = right[:, h:t]


def last_kernel(whole_rows, *refs):
    old_l, old_m, left, middle, from_left = refs[:5]
    out, h, t = refs[-1], PROBE, TILE
    if whole_rows:
        above_l, above_m = refs[5][:, :, :h], refs[5][:, :, h:t]
    else:
        above_l, above_m = refs[5][...], refs[6][...]
    out[:, 0, :h, :h] = old_l[:, :h] - STEP * (left[:, :h] + from_left[:, :h] + above_l)
    out[:, 0, h:, :h] = old_l[:, h:t] - STEP * (left[:, h:t] + from_left[:, h:t])
    out[:, 0, :h, h:] = old_m[:, :h] - STEP * (middle[:, :h] + above_m)
    out[:, 0, h:, h:] = old_m[:, h:t] - STEP * middle[:, h:t]


def last(layer, piece, above, result):
    operands = [*piece, *above]
    specs, aliases = {}, {}
    if result is not None:
        specs, aliases = {len(operands): pl.BlockSpec(memory_space=pl.ANY)}, {len(operands): 0}
        operands.append(result)
    return plain(
        functools.partial(last_kernel, len(above) == 1),
        [shape(2, SLICES, TILE, TILE)],
        operands,
        specs,
        aliases,
        [tile_of(layer)],
    )[0]


def on_device(object_field, probe, propagator, measured, offsets):
    h, t = PROBE, TILE
    phase, tables = prepare(probe, propagator)
    offsets = jnp.swapaxes(offsets, 2, 3).reshape(2, POS)
    intensity = measured.reshape(POS, h, h)

    top, all_rows, west_half, east_half, rest = pl.ds(0, h), pl.ds(0, t), pl.ds(0, h), pl.ds(h, h), pl.ds(1, 2)
    rows0 = object_field[:, 0, :h]
    cols0, west_rows, east_rows, cols12 = pack(
        object_field,
        [(0, all_rows, west_half), (rest, top, west_half), (rest, top, east_half), (rest, all_rows, west_half)],
        [shape(2, t, h), shape(2, 2, h, h), shape(2, 2, h, h), shape(2, 2, t, h)],
    )
    low0 = shifted(rows0, "row", -1)
    low_west = shifted(west_rows, "row", -1)
    low_east = shifted(east_rows, "row", -1)
    right0 = shifted(cols0, "col", -1)
    right12 = shifted(cols12, "col", -1)
    corner0 = shifted(low0[:, :, :h], "col", -1)
    corner12 = shifted(low_west, "col", -1)
    fields = [
        [object_field, low0, low0, right0, corner0],
        [object_field, low_west, low_east, right12, corner12],
        [object_field, low_west, low_east, right12, corner12],
    ]

    def gradients(fields, fill):
        _, wave1 = forward(offsets, tables, phase, None, fields[0], 0, fill)
        win1, wave2 = forward(offsets, tables, phase, wave1, fields[1], 1, fill)
        *grad2, back = turn(offsets, tables, intensity, wave2, fields[2], 2, fill)
        *grad1, back = backward(offsets, tables, phase, back, wave1, win1)
        grad0 = backward(offsets, tables, phase, back, None, None)
        return [grad0, grad1, grad2]

    grads = gradients(fields, fill_first)
    renewed = [None] * SLICES

    def columns(west, east, layer):
        from_left = shifted(east, "col", 1)
        if layer == 1:
            return [from_left]
        from_right = shifted(west, "col", -1)
        return [from_left, from_right]

    for layer in (2, 1, 0):
        grad, rows_first = grads[layer], layer == 2
        moved = [] if rows_first else columns(grad[0], grad[3], layer)
        for_even, for_odd = sums(grad, moved)
        even = swapped(for_even, 0)
        odd = swapped(for_odd, 1)
        if rows_first:
            west, east = plain(edges_kernel, [SIDE] * 2, [grad[0], grad[3], even, odd])
            moved = columns(west, east, layer)
            grad = [west, grad[1], grad[2], east]
        new = list(update(layer, fields[layer], grad, moved, even, odd, rows_first))
        if layer == 1:
            new.append(shifted(new[0], "col", -1))
        renewed[layer] = new
    grads = gradients(renewed, fill_next)
    from_left, above_m, above_l = {}, {}, {}
    down = plain(join_kernel, [shape(2, h, EXT)], [grads[2][0], grads[2][2], grads[2][3]])[0]
    above2 = shifted(down, "row", 1)
    east = plain(east_kernel, [shape(2, t, h)], [grads[2][3], above2])[0]
    from_left[2] = shifted(east, "col", 1)
    for layer in (1, 0):
        right = grads[layer][3]
        from_left[layer] = shifted(right if layer else right[:, t:], "col", 1)
        above_m[layer] = shifted(grads[layer][2], "row", 1)
        down = plain(spill_kernel, [shape(2, h, h)], [grads[layer][0], from_left[layer]])[0]
        above_l[layer] = shifted(down, "row", 1)
    from_left[0] = shifted(grads[0][3][:, :t], "col", 1)
    pieces = [(renewed[n][0], renewed[n][1], grads[n][0], grads[n][1], from_left[n]) for n in range(SLICES)]
    result = last(2, pieces[2], [above2], None)
    result = last(1, pieces[1], [above_l[1], above_m[1]], result)
    return last(0, pieces[0], [above_l[0], above_m[0]], result)


def solution(mesh):
    placed = (
        P(None, None, "row", "col"),
        P(),
        P(),
        P("row", "col", None, None, None),
        P("row", "col", None, None),
    )
    return jax.shard_map(
        on_device,
        mesh=mesh,
        in_specs=placed,
        out_specs=P(None, None, "row", "col"),
        check_vma=False,
    )
```
